32 devices in a mesh: member: 4 (over y, x), slab: 8 (over z, core).
Axes of the slice: x: 2, y: 2, z: 4, core: 2. Of those that a mesh axis runs over, the one named last changes fastest.
Arguments:
- fluid_head_start: float32 [192, 128, 128], P('member', 'slab'), may hold values from -6 to 6
- conductivity_matrix: float32 [192, 128, 128], P('member', 'slab'), may hold values from 0.1 to 1
- well_rates: float32 [128, 128], P('slab'), may hold values from -3 to 3
- cell_layer: int32 [128, 128], P('slab'), may hold values from 0 to 7
- pixel_coords: int32 [2, 4096], replicated, may hold values from 0 to 63
- obs_index: int32 [1024], replicated, may hold values from 0 to 4095
- obs_value: float32 [1024], replicated, may hold values from -0.6 to 0.6
- obs_sigma: float32 [1024], replicated, may hold values from 0.05 to 0.5
Outputs:
- analysed: float32 [192, 128, 128], P('member', 'slab')
- subsidence: float32 [4096, 192], P(('member', 'slab'))
The draws below stay inside these ranges and needn't reach their ends.
All inputs are finite; a program needn't handle non-finite values.
Results may differ from the reference program's by a relative error of at most 0.00028.
Values sent between devices are 32-bit elements; how exact they have to be, the bound alone decides.
No kernel may reach another device: no remote copies, remote signals or barrier semaphores. Data moves between devices by JAX's collectives and lax.ppermute only.
A program may use at most 64 MiB of HBM per device.

```python
import math
import jax
import jax.numpy as jnp
from jax import lax

E = 192
AQUIFER_BREADTH = 128
STEPS = 4
P_SIZE = 4096
M = 1024
AQUIFER_LINES = 128


def set_ends(values, rng, least, largest):
    shape = values.shape
    place = [jax.random.randint(jax.random.fold_in(rng, axis), (), 0, shape[axis]) for axis in range(len(shape))]
    values = values.at[tuple(place)].set(least)
    longest = shape.index(max(shape))
    place[longest] = (place[longest] + 1) % shape[longest]
    return values.at[tuple(place)].set(largest)


def block_scale(own_key, extent, split, smallest, top_value):
    def one(axis_at, blocks):
        heights = jax.random.uniform(jax.random.fold_in(jax.random.fold_in(own_key, 6), axis_at), (blocks,), jnp.float32, smallest / len(split), top_value / len(split))
        return jnp.repeat(jnp.exp(heights), extent[axis_at] // blocks).reshape((-1,) + (1,) * (len(extent) - axis_at - 1))

    loudness = one(*split[0])
    for cut in split[1:]:
        loudness = loudness * one(*cut)
    return loudness


def normal_values(stream_key, shape, deviation, reach, cuts=(), held_as=jnp.bfloat16):
    loudness = block_scale(stream_key, shape, cuts, -0.22, 0.18) if cuts else 1.0
    entries = jax.random.normal(stream_key, shape, jnp.float32) * deviation * loudness
    return jnp.minimum(jnp.maximum(entries, -reach), reach).astype(held_as)


def setup_inputs(seed: int = 0) -> dict:
    streams_of = jax.random.split(jax.random.key(seed), 9)
    return {
        "fluid_head_start": normal_values(streams_of[0], (E, AQUIFER_LINES, AQUIFER_BREADTH), 1.0, 6.0, ((0, 4), (1, 8)), jnp.float32),
        "conductivity_matrix": jnp.clip(jnp.exp(math.log(1.0) - 2.3025851 * jax.random.uniform(streams_of[1], (E, AQUIFER_LINES, AQUIFER_BREADTH), jnp.float32) ** block_scale(streams_of[1], (E, AQUIFER_LINES, AQUIFER_BREADTH), ((0, 4), (1, 8)), -0.2, 0.2)), 0.1, 1.0),
        "well_rates": normal_values(streams_of[2], (AQUIFER_LINES, AQUIFER_BREADTH), 0.5, 3.0, ((0, 8),), jnp.float32),
        "cell_layer": set_ends(jax.random.randint(streams_of[3], (AQUIFER_LINES, AQUIFER_BREADTH), 0, 8), jax.random.fold_in(streams_of[3], 1), 0, 7).astype(jnp.int32),
        "pixel_coords": set_ends(jax.random.randint(streams_of[4], (2, P_SIZE), 0, 64), jax.random.fold_in(streams_of[4], 1), 0, 63).astype(jnp.int32),
        "obs_index": set_ends(jax.random.randint(streams_of[5], (M,), 0, P_SIZE), jax.random.fold_in(streams_of[5], 1), 0, P_SIZE - 1).astype(jnp.int32),
        "obs_value": normal_values(streams_of[6], (M,), 0.1, 0.6, (), jnp.float32),
        "obs_sigma": jnp.clip(jnp.exp(jax.random.uniform(streams_of[7], (M,), jnp.float32, math.log(0.05), math.log(0.5))), 0.05, 0.5),
    }


time_step = 0.15
pixel_span = 64.0
top_depth = 2.0

def advance_in_time(fluid_head_grid, perm_field, source, open_faces):
    mobility = perm_field * (1.0 + 0.5 * jnp.tanh(fluid_head_grid))
    sample_vectors, height, across_cells = fluid_head_grid.shape
    across = 0.5 * (mobility[:, 1:] + mobility[:, :-1]) * open_faces[None, :, None]
    flux_rows = across * (fluid_head_grid[:, 1:] - fluid_head_grid[:, :-1])
    zero_row = jnp.zeros((sample_vectors, 1, across_cells), fluid_head_grid.dtype)
    inflow = jnp.concatenate([flux_rows, zero_row], 1) - jnp.concatenate([zero_row, flux_rows], 1)
    along = 0.5 * (mobility[:, :, 1:] + mobility[:, :, :-1])
    flux_cols = along * (fluid_head_grid[:, :, 1:] - fluid_head_grid[:, :, :-1])
    zero_col = jnp.zeros((sample_vectors, height, 1), fluid_head_grid.dtype)
    inflow = inflow + (jnp.concatenate([flux_cols, zero_col], 2) - jnp.concatenate([zero_col, flux_cols], 2))
    return fluid_head_grid + time_step * (inflow + source[None])

def kernel_rows(pixel_x, pixel_y, cell_x, cell_y, depth, volume):
    delta_x = cell_x[None, :] - pixel_x[:, None]
    delta_y = cell_y[None, :] - pixel_y[:, None]
    radius = delta_x * delta_x + delta_y * delta_y + depth[None, :] * depth[None, :]
    return volume * depth[None, :] / (radius * jnp.sqrt(radius))

def gram_terms(predicted, obs_value, obs_sigma, owned):
    centre = lax.optimization_barrier(jnp.mean(predicted, axis=1))
    anomaly = predicted - centre[:, None]
    inverse_var = 1.0 / (obs_sigma * obs_sigma)
    weighted = anomaly * inverse_var[:, None]
    gram = lax.dot_general(anomaly, weighted, (((0,), (0,)), ((), ())), precision=lax.Precision.HIGHEST)
    rhs = jnp.dot(owned * (obs_value - centre), weighted, precision=lax.Precision.HIGHEST)
    return (gram, rhs)

def finish(gram, rhs, sample_vector_pile):
    sample_vectors = sample_vector_pile.shape[0]
    ident = jnp.eye(sample_vectors, dtype=gram.dtype)
    gram = gram + (sample_vectors - 1.0) * ident
    factor = jnp.linalg.cholesky(gram)
    inverse = jax.scipy.linalg.solve_triangular(factor, ident, lower=True)
    weights = jnp.dot(inverse.T, jnp.dot(inverse, rhs, precision=lax.Precision.HIGHEST), precision=lax.Precision.HIGHEST)
    transform = jnp.sqrt(sample_vectors - 1.0) * inverse.T
    mix = weights[:, None] + transform
    centre = lax.optimization_barrier(jnp.mean(sample_vector_pile, axis=0))
    spread = sample_vector_pile - centre[None]
    return centre[None] + lax.dot_general(mix, spread, (((0,), (0,)), ((), ())), precision=lax.Precision.HIGHEST)

def reference(fluid_head_start, conductivity_matrix, well_rates, cell_layer, pixel_coords, obs_index, obs_value, obs_sigma):
    open_faces = jnp.ones((AQUIFER_LINES - 1,), jnp.float32)

    def evolve_sample(pair):
        fluid_head_grid = pair[0][None]
        perm_field = pair[1][None]
        for repeat in range(STEPS):
            fluid_head_grid = advance_in_time(fluid_head_grid, perm_field, well_rates, open_faces)
        return fluid_head_grid[0]
    predicted_ensemble = lax.map(evolve_sample, (fluid_head_start, conductivity_matrix))
    sample_vectors = predicted_ensemble.shape[0]
    volume = pixel_span * pixel_span / (AQUIFER_LINES * AQUIFER_BREADTH)
    row_pos = (jnp.arange(AQUIFER_LINES).astype(jnp.float32) + 0.5) * (pixel_span / AQUIFER_LINES)
    col_pos = (jnp.arange(AQUIFER_BREADTH).astype(jnp.float32) + 0.5) * (pixel_span / AQUIFER_BREADTH)
    pixel_f = pixel_coords.astype(jnp.float32)
    lines_in_slab_part = math.gcd(AQUIFER_LINES, 16)

    def add_block(index, total):
        topmost_line = (index * lines_in_slab_part).astype(jnp.int32)
        sample_vector_pile = lax.dynamic_slice_in_dim(predicted_ensemble, topmost_line, lines_in_slab_part, 1).reshape(sample_vectors, lines_in_slab_part * AQUIFER_BREADTH)
        layers = lax.dynamic_slice_in_dim(cell_layer, topmost_line, lines_in_slab_part, 0).astype(jnp.float32)
        depth = (top_depth + layers).reshape(-1)
        rows_here = lax.dynamic_slice_in_dim(row_pos, topmost_line, lines_in_slab_part, 0)
        cell_x = jnp.broadcast_to(rows_here[:, None], (lines_in_slab_part, AQUIFER_BREADTH)).reshape(-1)
        cell_y = jnp.broadcast_to(col_pos[None, :], (lines_in_slab_part, AQUIFER_BREADTH)).reshape(-1)
        kern = kernel_rows(pixel_f[0], pixel_f[1], cell_x, cell_y, depth, volume)
        return total + lax.dot_general(kern, sample_vector_pile, (((1,), (1,)), ((), ())), precision=lax.Precision.HIGHEST)
    subsidence = lax.fori_loop(0, AQUIFER_LINES // lines_in_slab_part, add_block, jnp.zeros((P_SIZE, sample_vectors), jnp.float32))
    predicted = jnp.take(subsidence, obs_index, axis=0)
    gram, rhs = gram_terms(predicted, obs_value, obs_sigma, jnp.ones_like(obs_value))
    sample_vector_pile = predicted_ensemble.reshape(sample_vectors, AQUIFER_LINES * AQUIFER_BREADTH)
    analysed = finish(gram, rhs, sample_vector_pile).reshape(sample_vectors, AQUIFER_LINES, AQUIFER_BREADTH)
    return (analysed, subsidence)
```

```python
import functools
import math

import jax
import jax.numpy as jnp
from jax import lax
from jax.experimental import pallas as pl
from jax.experimental.pallas import tpu as pltpu
from jax.sharding import PartitionSpec as P

STEPS = 4

time_step = 0.15
pixel_span = 64.0
top_depth = 2.0

F32 = jnp.float32
BF16 = jnp.bfloat16
VMEM_BYTES = 56 * 1024 * 1024


def params(**more):
    return pltpu.CompilerParams(vmem_limit_bytes=VMEM_BYTES, **more)


def cost(flops, bytes_accessed):
    return pl.CostEstimate(flops=int(flops), bytes_accessed=int(bytes_accessed), transcendentals=0)


def split(value):
    high = value.astype(BF16)
    return high, (value - high.astype(F32)).astype(BF16)


def dot(a, b):
    return lax.dot_general(a, b, (((1,), (0,)), ((), ())), preferred_element_type=F32)


def accumulate(step, total_ref, part):
    @pl.when(step == 0)
    def _():
        total_ref[...] = part

    @pl.when(step > 0)
    def _():
        total_ref[...] = total_ref[...] + part


def pack_kernel(slab_ref, head_ref, perm_ref, wells_ref, near_ref, far_ref):
    members, rows, cells = head_ref.shape
    even = lax.rem(slab_ref[0], 2) == 0
    for k in range(STEPS):
        for source, first in ((head_ref, 0), (perm_ref, members)):
            top = source[:, k, :]
            bottom = source[:, rows - STEPS + k, :]
            near_ref[k, first : first + members, :] = jnp.where(even, bottom, top)
            far_ref[k, first : first + members, :] = jnp.where(even, top, bottom)
        top = jnp.broadcast_to(wells_ref[k : k + 1, :], (8, cells))
        bottom = jnp.broadcast_to(wells_ref[rows - STEPS + k : rows - STEPS + k + 1, :], (8, cells))
        near_ref[k, 2 * members :, :] = jnp.where(even, bottom, top)
        far_ref[k, 2 * members :, :] = jnp.where(even, top, bottom)


def pack(slab, head, perm, wells):
    members, _, cells = head.shape
    out = jax.ShapeDtypeStruct((STEPS, 2 * members + 8, cells), F32)
    return pl.pallas_call(
        pack_kernel,
        out_shape=(out, out),
        in_specs=[pl.BlockSpec(memory_space=pltpu.SMEM)] + [pl.BlockSpec(memory_space=pltpu.VMEM)] * 3,
        out_specs=(pl.BlockSpec(memory_space=pltpu.VMEM),) * 2,
        compiler_params=params(),
        name="pack_rims",
    )(slab, head, perm, wells)


def kernel_body(total_rows, rows_here, slab_ref, px, py, layer_ref, high_ref, low_ref, dy2_ref):
    cells = dy2_ref.shape[0]
    pixels = dy2_ref.shape[1]
    row = pl.program_id(0)

    @pl.when(row == 0)
    def _():
        position = lax.broadcasted_iota(jnp.int32, (cells, 128), 0).astype(F32)
        cell_y = (position + 0.5) * (pixel_span / cells)
        for lane in range(0, pixels, 128):
            delta = cell_y - jnp.broadcast_to(py(lane), (cells, 128))
            dy2_ref[:, lane : lane + 128] = delta * delta

    global_row = slab_ref[0] * rows_here + row
    cell_x = (global_row.astype(F32) + 0.5) * (pixel_span / total_rows)
    layer = layer_ref[pl.ds(row, 1), :].astype(F32) + top_depth
    depth = jnp.swapaxes(jnp.broadcast_to(layer, (cells, cells)), 0, 1)
    depth2 = depth * depth
    scaled = depth * (pixel_span * pixel_span / (total_rows * cells))
    for lane in range(0, pixels, 128):
        delta = cell_x - px(lane)
        dx2 = jnp.broadcast_to(delta * delta, (32, 128))
        for sub in range(0, cells, 32):
            r2 = dy2_ref[sub : sub + 32, lane : lane + 128] + dx2 + depth2[sub : sub + 32, :128]
            inverse = lax.rsqrt(r2)
            value = scaled[sub : sub + 32, :128] * inverse * (inverse * inverse)
            high, low = split(value)
            high_ref[sub : sub + 32, lane : lane + 128] = high
            low_ref[sub : sub + 32, lane : lane + 128] = low


def observed_kernel(total_rows, rows_here, slab_ref, table_ref, index_ref, layer_ref, high_ref, low_ref, dy2_ref, at_ref):
    pixels = dy2_ref.shape[1]
    tall = table_ref.shape[0] // 2

    @pl.when(pl.program_id(0) == 0)
    def _():
        for lane in range(0, pixels, 128):
            index = index_ref[0:1, lane : lane + 128]
            low = index & 127
            high = index >> 7
            pick = (lax.broadcasted_iota(jnp.int32, (128, 128), 0) == low).astype(BF16)
            found = dot(table_ref[...].astype(BF16), pick)
            own = lax.broadcasted_iota(jnp.int32, (tall, 128), 0) == high
            at_ref[0:1, lane : lane + 128] = jnp.sum(jnp.where(own, found[:tall], 0.0), 0, keepdims=True)
            at_ref[1:2, lane : lane + 128] = jnp.sum(jnp.where(own, found[tall:], 0.0), 0, keepdims=True)

    px = lambda lane: at_ref[0:1, lane : lane + 128]
    py = lambda lane: at_ref[1:2, lane : lane + 128]
    kernel_body(total_rows, rows_here, slab_ref, px, py, layer_ref, high_ref, low_ref, dy2_ref)


def pixel_kernel(total_rows, rows_here, slab_ref, at_in_ref, layer_ref, high_ref, low_ref, dy2_ref):
    px = lambda lane: at_in_ref[0:1, lane : lane + 128]
    py = lambda lane: at_in_ref[1:2, lane : lane + 128]
    kernel_body(total_rows, rows_here, slab_ref, px, py, layer_ref, high_ref, low_ref, dy2_ref)


def forward_kernel(total_rows, slab, layer, at=None, table=None, index=None):
    rows, cells = layer.shape
    whole = lambda a: pl.BlockSpec(a.shape, lambda i: (0,) * a.ndim)
    smem = pl.BlockSpec(memory_space=pltpu.SMEM)
    if at is None:
        pixels = index.shape[1]
        body = functools.partial(observed_kernel, total_rows, rows)
        operands = (slab, table, index, layer)
        scratch = [pltpu.VMEM((cells, pixels), F32), pltpu.VMEM((8, pixels), F32)]
    else:
        pixels = at.shape[1]
        body = functools.partial(pixel_kernel, total_rows, rows)
        operands = (slab, at, layer)
        scratch = [pltpu.VMEM((cells, pixels), F32)]
    out = jax.ShapeDtypeStruct((rows * cells, pixels), BF16)
    return pl.pallas_call(
        body,
        grid=(rows,),
        out_shape=(out, out),
        in_specs=[smem] + [whole(a) for a in operands[1:]],
        out_specs=(pl.BlockSpec((cells, pixels), lambda i: (i, 0)),) * 2,
        scratch_shapes=scratch,
        compiler_params=params(dimension_semantics=("arbitrary",)),
        cost_estimate=cost(rows * cells * pixels * 16, rows * cells * pixels * 4),
        name="kernel_of_observed" if at is None else "kernel_of_pixels",
    )(*operands)


def forecast_steps(rows, slab, slabs, head_ref, perm_ref, wells_ref, near_ref, far_ref, p_ref, k_ref):
    members, _, cells = head_ref.shape
    even = lax.rem(slab, 2) == 0
    reach = rows + 2 * STEPS
    for k in range(STEPS):
        near = near_ref[k]
        far = far_ref[k]
        before = jnp.where(even, far, near)
        after = jnp.where(even, near, far)
        p_ref[k] = before[:members]
        k_ref[k] = before[members : 2 * members]
        p_ref[STEPS + rows + k] = after[:members]
        k_ref[STEPS + rows + k] = after[members : 2 * members]
    for k in range(rows):
        p_ref[STEPS + k] = head_ref[:, k, :]
        k_ref[STEPS + k] = perm_ref[:, k, :]
    last_lane = lax.broadcasted_iota(jnp.int32, (members, cells), 1) == cells - 1
    no_before = slab == 0
    no_after = slab == slabs - 1

    def wells_of(i):
        if i < STEPS:
            return jnp.where(even, far_ref[i, 2 * members : 2 * members + 1, :], near_ref[i, 2 * members : 2 * members + 1, :])
        if i >= STEPS + rows:
            j = i - STEPS - rows
            return jnp.where(even, near_ref[j, 2 * members : 2 * members + 1, :], far_ref[j, 2 * members : 2 * members + 1, :])
        return wells_ref[i - STEPS : i - STEPS + 1, :]

    def row_flux(mobility, head, mobility_next, head_next, i):
        flux = 0.5 * (mobility_next + mobility) * (head_next - head)
        if i == STEPS - 1:
            flux = jnp.where(no_before, 0.0, flux)
        if i == STEPS + rows - 1:
            flux = jnp.where(no_after, 0.0, flux)
        return flux

    def mobility_of(i, head):
        return k_ref[i] * (1.0 + 0.5 * jnp.tanh(head))

    for step in range(STEPS):
        first = step + 1
        head_before = p_ref[first - 1]
        head = p_ref[first]
        mobility_before = mobility_of(first - 1, head_before)
        mobility = mobility_of(first, head)
        flux_before = row_flux(mobility_before, head_before, mobility, head, first - 1)
        for i in range(first, reach - first):
            head_next = p_ref[i + 1]
            mobility_next = mobility_of(i + 1, head_next)
            flux_after = row_flux(mobility, head, mobility_next, head_next, i)
            along = 0.5 * (pltpu.roll(mobility, cells - 1, 1) + mobility) * (pltpu.roll(head, cells - 1, 1) - head)
            along = jnp.where(last_lane, 0.0, along)
            inflow = (flux_after - flux_before) + (along - pltpu.roll(along, 1, 1))
            p_ref[i] = head + time_step * (inflow + wells_of(i))
            head, mobility, flux_before = head_next, mobility_next, flux_after


def forecast_kernel(slabs, slab_ref, head_ref, perm_ref, wells_ref, near_ref, far_ref, high_ref, low_ref, cast_ref, own_ref, other_ref, p_ref, k_ref, lhs_ref, wide_ref, thin_ref):
    members, rows, cells = head_ref.shape
    padded = cast_ref.shape[0]
    depth = high_ref.shape[0]
    step = pl.program_id(0)

    @pl.when(step == 0)
    def _():
        forecast_steps(rows, slab_ref[0], slabs, head_ref, perm_ref, wells_ref, near_ref, far_ref, p_ref, k_ref)
        per = depth // cells
        if padded != members:
            cast_ref[...] = jnp.zeros_like(cast_ref)
            lhs_ref[...] = jnp.zeros_like(lhs_ref)
        for i in range(rows):
            value = p_ref[STEPS + i]
            high, low = split(value)
            lane = (i % per) * cells
            cast_ref[0:members, i * cells : (i + 1) * cells] = value
            lhs_ref[i // per, 0:members, lane : lane + cells] = high
            lhs_ref[i // per, padded : padded + members, lane : lane + cells] = low

    both = lhs_ref[step]
    accumulate(step, wide_ref, dot(both, high_ref[...]))
    accumulate(step, thin_ref, dot(both[:padded], low_ref[...]))

    @pl.when(step == pl.num_programs(0) - 1)
    def _():
        half = own_ref.shape[1]
        seen = wide_ref[0:padded, :] + wide_ref[padded:, :] + thin_ref[...]
        own_ref[...] = seen[:, :half]
        other_ref[...] = seen[:, half:]


def forecast(slabs, padded, slab, head, perm, wells, near, far, high, low):
    members, rows, cells = head.shape
    total, observed = high.shape
    depth = min(total, 512)
    whole = lambda a: pl.BlockSpec(a.shape, lambda i: (0,) * a.ndim)
    const = lambda shape: pl.BlockSpec(shape, lambda i: (0,) * len(shape))
    half = (padded, observed // 2)
    return pl.pallas_call(
        functools.partial(forecast_kernel, slabs),
        grid=(total // depth,),
        out_shape=(
            jax.ShapeDtypeStruct((padded, total), F32),
            jax.ShapeDtypeStruct(half, F32),
            jax.ShapeDtypeStruct(half, F32),
        ),
        in_specs=[pl.BlockSpec(memory_space=pltpu.SMEM)]
        + [whole(a) for a in (head, perm, wells, near, far)]
        + [pl.BlockSpec((depth, observed), lambda i: (i, 0))] * 2,
        out_specs=(const((padded, total)), const(half), const(half)),
        scratch_shapes=[
            pltpu.VMEM((rows + 2 * STEPS, members, cells), F32),
            pltpu.VMEM((rows + 2 * STEPS, members, cells), F32),
            pltpu.VMEM((total // depth, 2 * padded, depth), BF16),
            pltpu.VMEM((2 * padded, observed), F32),
            pltpu.VMEM((padded, observed), F32),
        ],
        compiler_params=params(dimension_semantics=("arbitrary",)),
        cost_estimate=cost(6 * padded * total * observed, 4 * total * observed),
        name="forecast",
    )(slab, head, perm, wells, near, far, high, low)


def subsidence_kernel(groups, member_ref, *refs):
    pieces = refs[:groups]
    high_ref, low_ref, own_ref, other_ref, lhs_ref, wide_ref, thin_ref = refs[groups:]
    padded = pieces[0].shape[0]
    every = groups * padded
    depth = high_ref.shape[0]
    step = pl.program_id(0)

    for offset in range(groups):
        at = member_ref[0] ^ offset
        high, low = split(pieces[offset][...])
        lhs_ref[at] = high
        lhs_ref[groups + at] = low
    both = lhs_ref[...].reshape(2 * every, depth)
    accumulate(step, wide_ref, dot(both, high_ref[...]))
    accumulate(step, thin_ref, dot(both[:every], low_ref[...]))

    @pl.when(step == pl.num_programs(0) - 1)
    def _():
        half = own_ref.shape[1]
        seen = wide_ref[0:every, :] + wide_ref[every:, :] + thin_ref[...]
        own_ref[...] = seen[:, :half]
        other_ref[...] = seen[:, half:]


def subsidence_partial(member, pieces, high, low):
    groups = len(pieces)
    padded, total = pieces[0].shape
    pixels = high.shape[1]
    depth = min(total, 512)
    every = groups * padded
    half = (every, pixels // 2)
    out = jax.ShapeDtypeStruct(half, F32)
    return pl.pallas_call(
        functools.partial(subsidence_kernel, groups),
        grid=(total // depth,),
        out_shape=(out, out),
        in_specs=[pl.BlockSpec(memory_space=pltpu.SMEM)]
        + [pl.BlockSpec((padded, depth), lambda i: (0, i))] * groups
        + [pl.BlockSpec((depth, pixels), lambda i: (i, 0))] * 2,
        out_specs=(pl.BlockSpec(half, lambda i: (0, 0)),) * 2,
        scratch_shapes=[
            pltpu.VMEM((2 * groups, padded, depth), BF16),
            pltpu.VMEM((2 * every, pixels), F32),
            pltpu.VMEM((every, pixels), F32),
        ],
        compiler_params=params(dimension_semantics=("arbitrary",)),
        cost_estimate=cost(6 * every * total * pixels, 4 * total * pixels + 4 * every * total),
        name="subsidence",
    )(member, *pieces, high, low)


def gram_kernel(groups, members, member_ref, *refs):
    pieces = refs[:groups]
    value_ref, sigma_ref, out_ref, seen_ref = refs[groups:]
    padded, half = pieces[0].shape
    every = groups * padded
    for offset in range(groups):
        seen_ref[member_ref[0] ^ offset] = pieces[offset][...]
    seen = seen_ref[...].reshape(every, half)
    centre = jnp.sum(seen, 0, keepdims=True) * (1.0 / (groups * members))
    anomaly = seen - centre
    if padded != members:
        here = lax.rem(lax.broadcasted_iota(jnp.int32, (every, half), 0), padded) < members
        anomaly = jnp.where(here, anomaly, 0.0)
    sigma = sigma_ref[...]
    weighted = anomaly * (1.0 / (sigma * sigma))
    innovation = jnp.broadcast_to(value_ref[...] - centre, (8, half))
    extra = jnp.where(lax.broadcasted_iota(jnp.int32, (8, half), 0) == 0, innovation, 0.0)
    contract = (((1,), (1,)), ((), ()))
    out_ref[...] = jnp.zeros_like(out_ref)
    out_ref[:, 0:every] = lax.dot_general(
        weighted, anomaly, contract, precision=lax.Precision.HIGHEST, preferred_element_type=F32
    )
    out_ref[:, every : every + 8] = lax.dot_general(
        weighted, extra, contract, precision=lax.Precision.HIGHEST, preferred_element_type=F32
    )


def gram_partial(members, member, pieces, value, sigma):
    groups = len(pieces)
    padded, half = pieces[0].shape
    every = groups * padded
    width = -(-(every + 8) // 128) * 128
    vmem = pl.BlockSpec(memory_space=pltpu.VMEM)
    return pl.pallas_call(
        functools.partial(gram_kernel, groups, members),
        out_shape=jax.ShapeDtypeStruct((every, width), F32),
        in_specs=[pl.BlockSpec(memory_space=pltpu.SMEM)] + [vmem] * (groups + 2),
        out_specs=vmem,
        scratch_shapes=[pltpu.VMEM((groups, padded, half), F32)],
        compiler_params=params(),
        cost_estimate=cost(12 * every * every * half, 4 * every * half),
        name="gram",
    )(member, *pieces, value, sigma)


def update_kernel(groups, members, member_ref, mix_ref, *refs):
    pieces = refs[:groups]
    out_ref, cast_ref = refs[groups:]
    padded, total = pieces[0].shape
    rows, cells = out_ref.shape[1:]
    every = groups * padded
    for offset in range(groups):
        at = member_ref[0] ^ offset
        high, low = split(pieces[offset][...])
        cast_ref[at] = high
        cast_ref[groups + at] = low
    mix_high, mix_low = split(mix_ref[...])
    mix_both = jnp.concatenate([mix_high, mix_low], 0)
    depth = 4 * cells if rows % 4 == 0 else cells
    for lane in range(0, total, depth):
        high = cast_ref[0:groups, :, lane : lane + depth].reshape(every, depth)
        low = cast_ref[groups:, :, lane : lane + depth].reshape(every, depth)
        both = dot(mix_both, high)
        value = both[:padded] + both[padded:] + dot(mix_high, low)
        for part in range(depth // cells):
            out_ref[:, lane // cells + part, :] = value[:members, part * cells : (part + 1) * cells]


def update(members, rows, cells, member, mix, pieces):
    groups = len(pieces)
    padded, total = pieces[0].shape
    vmem = pl.BlockSpec(memory_space=pltpu.VMEM)
    return pl.pallas_call(
        functools.partial(update_kernel, groups, members),
        out_shape=jax.ShapeDtypeStruct((members, rows, cells), F32),
        in_specs=[pl.BlockSpec(memory_space=pltpu.SMEM)] + [vmem] * (groups + 1),
        out_specs=vmem,
        scratch_shapes=[pltpu.VMEM((2 * groups, padded, total), BF16)],
        compiler_params=params(),
        cost_estimate=cost(6 * padded * groups * padded * total, 4 * groups * padded * total),
        name="update",
    )(member, mix, *pieces)


def weights_of(members, padded, member, gram_sum):
    every = gram_sum.shape[0]
    count = every // padded * members
    ident = jnp.eye(every, dtype=F32)
    gram = gram_sum[:, :every] + (count - 1.0) * ident
    rhs = gram_sum[:, every]
    factor = jnp.linalg.cholesky(gram)
    inverse = jax.scipy.linalg.solve_triangular(factor, ident, lower=True)
    high = lax.Precision.HIGHEST
    weights = jnp.dot(inverse.T, jnp.dot(inverse, rhs, precision=high), precision=high)
    own = lax.dynamic_slice_in_dim(inverse, member * padded, padded, 0)
    mix = weights[None, :] + math.sqrt(count - 1.0) * own
    here = (jnp.arange(every) % padded < members).astype(F32)
    mix = mix * here[None, :]
    return (mix + (1.0 - jnp.sum(mix, 1, keepdims=True)) / count) * here[None, :]


def shards(head, perm, wells, layer, coords, obs_index, obs_value, obs_sigma):
    members, rows, cells = head.shape
    groups = lax.axis_size("member")
    slabs = lax.axis_size("slab")
    slab = lax.axis_index("slab")
    member = lax.axis_index("member")
    core = slab % 2
    total_rows = rows * slabs
    padded = -(-members // 16) * 16
    slab_s = slab.astype(jnp.int32).reshape(1)
    member_s = member.astype(jnp.int32).reshape(1)
    pair = [(i, i ^ 1) for i in range(slabs)]
    across = [(i, i + 1) for i in range(1, slabs - 1, 2)] + [(i + 1, i) for i in range(1, slabs - 1, 2)]

    def swap(value, axis, offset):
        size = lax.axis_size(axis)
        return lax.ppermute(value, axis, [(i, i ^ offset) for i in range(size)])

    near, far = pack(slab_s, head, perm, wells)
    far = lax.ppermute(far, "slab", across)
    near = lax.ppermute(near, "slab", pair)

    observed = obs_index.shape[0]
    half = observed // 2

    def own_first(row):
        return jnp.where(core == 0, row, jnp.roll(row, half)).reshape(1, observed)

    pixel_total = coords.shape[1]
    table = coords.astype(F32).reshape(2 * pixel_total // 128, 128)
    high, low = forward_kernel(total_rows, slab_s, layer, table=table, index=own_first(obs_index))

    cast, own, other = forecast(slabs, padded, slab_s, head, perm, wells, near, far, high, low)
    seen = own + swap(other, "slab", 1)
    pieces = [cast] + [swap(cast, "member", offset) for offset in range(1, groups)]
    offset = 2
    while offset < slabs:
        seen = seen + swap(seen, "slab", offset)
        offset *= 2
    views = [seen] + [swap(seen, "member", offset) for offset in range(1, groups)]
    value = own_first(obs_value)[:, :half]
    sigma = own_first(obs_sigma)[:, :half]
    gram = gram_partial(members, member_s, views, value, sigma)
    gram = gram + swap(gram, "slab", 1)

    chips = slabs // 2
    own_rows = pixel_total // (groups * slabs)
    at = coords.astype(F32).reshape(2, groups, chips, 2, own_rows)
    at = lax.dynamic_index_in_dim(at, member, 1, keepdims=False)
    at = jnp.swapaxes(at, 1, 2)
    at = jnp.where(core == 0, at, at[:, ::-1]).reshape(2, pixel_total // groups)
    pixel_high, pixel_low = forward_kernel(total_rows, slab_s, layer, at=at)
    sunk, sunk_other = subsidence_partial(member_s, pieces, pixel_high, pixel_low)
    sunk_recv = swap(sunk_other, "slab", 1)
    chip = slab // 2

    def block(which):
        first = which * own_rows
        return lax.dynamic_slice_in_dim(sunk, first, own_rows, 1) + lax.dynamic_slice_in_dim(
            sunk_recv, first, own_rows, 1
        )

    sunk_own = block(chip)
    for offset in range(1, chips):
        sunk_own = sunk_own + swap(block(chip ^ offset), "slab", 2 * offset)
    if padded != members:
        sunk_own = sunk_own.reshape(groups, padded, own_rows)[:, :members].reshape(groups * members, own_rows)
    subsidence = sunk_own.T

    mix = weights_of(members, padded, member, gram)
    analysed = update(members, rows, cells, member_s, mix, pieces)
    return (analysed, subsidence)


def solution(mesh):
    return jax.shard_map(
        shards,
        mesh=mesh,
        in_specs=(
            P("member", "slab", None),
            P("member", "slab", None),
            P("slab", None),
            P("slab", None),
            P(),
            P(),
            P(),
            P(),
        ),
        out_specs=(P("member", "slab", None), P(("member", "slab"), None)),
        check_vma=False,
    )
```

```python
import functools
import math

import jax
import jax.numpy as jnp
from jax import lax
from jax.experimental import pallas as pl
from jax.experimental.pallas import tpu as pltpu
from jax.sharding import PartitionSpec as P

STEPS = 4

time_step = 0.15
pixel_span = 64.0
top_depth = 2.0

F32 = jnp.float32
BF16 = jnp.bfloat16
MIB = 1024 * 1024


def params(mib=16, **more):
    return pltpu.CompilerParams(vmem_limit_bytes=mib * MIB, **more)


def cost(flops, bytes_accessed):
    return pl.CostEstimate(flops=int(flops), bytes_accessed=int(bytes_accessed), transcendentals=0)


def split(value):
    high = value.astype(BF16)
    return high, (value - high.astype(F32)).astype(BF16)


def dot(a, b):
    return lax.dot_general(a, b, (((1,), (0,)), ((), ())), preferred_element_type=F32)


def accumulate(step, total_ref, part):
    @pl.when(step == 0)
    def _():
        total_ref[...] = part

    @pl.when(step > 0)
    def _():
        total_ref[...] = total_ref[...] + part


def pack_kernel(slab_ref, head_ref, perm_ref, wells_ref, near_ref, far_ref):
    members, rows, cells = head_ref.shape
    even = lax.rem(slab_ref[0], 2) == 0
    for k in range(STEPS):
        for source, first in ((head_ref, 0), (perm_ref, members)):
            top = source[:, k, :]
            bottom = source[:, rows - STEPS + k, :]
            near_ref[k, first : first + members, :] = jnp.where(even, bottom, top)
            far_ref[k, first : first + members, :] = jnp.where(even, top, bottom)
        top = jnp.broadcast_to(wells_ref[k : k + 1, :], (8, cells))
        bottom = jnp.broadcast_to(wells_ref[rows - STEPS + k : rows - STEPS + k + 1, :], (8, cells))
        near_ref[k, 2 * members :, :] = jnp.where(even, bottom, top)
        far_ref[k, 2 * members :, :] = jnp.where(even, top, bottom)


def pack(slab, head, perm, wells):
    members, _, cells = head.shape
    out = jax.ShapeDtypeStruct((STEPS, 2 * members + 8, cells), F32)
    return pl.pallas_call(
        pack_kernel,
        out_shape=(out, out),
        in_specs=[pl.BlockSpec(memory_space=pltpu.SMEM)] + [pl.BlockSpec(memory_space=pltpu.VMEM)] * 3,
        out_specs=(pl.BlockSpec(memory_space=pltpu.VMEM),) * 2,
        compiler_params=params(),
        name="pack_rims",
    )(slab, head, perm, wells)


def kernel_body(total_rows, rows_here, slab_ref, px, py, layer_ref, high_ref, low_ref, dy2_ref):
    cells = dy2_ref.shape[0]
    pixels = dy2_ref.shape[1]
    row = pl.program_id(0)

    @pl.when(row == 0)
    def _():
        position = lax.broadcasted_iota(jnp.int32, (cells, 128), 0).astype(F32)
        cell_y = (position + 0.5) * (pixel_span / cells)
        for lane in range(0, pixels, 128):
            delta = cell_y - jnp.broadcast_to(py(lane), (cells, 128))
            dy2_ref[:, lane : lane + 128] = delta * delta

    global_row = slab_ref[0] * rows_here + row
    cell_x = (global_row.astype(F32) + 0.5) * (pixel_span / total_rows)
    layer = layer_ref[pl.ds(row, 1), :].astype(F32) + top_depth
    depth = jnp.swapaxes(jnp.broadcast_to(layer, (cells, cells)), 0, 1)
    depth2 = depth * depth
    scaled = depth * (pixel_span * pixel_span / (total_rows * cells))
    for lane in range(0, pixels, 128):
        delta = cell_x - px(lane)
        dx2 = jnp.broadcast_to(delta * delta, (32, 128))
        for sub in range(0, cells, 32):
            r2 = dy2_ref[sub : sub + 32, lane : lane + 128] + dx2 + depth2[sub : sub + 32, :128]
            inverse = lax.rsqrt(r2)
            value = scaled[sub : sub + 32, :128] * inverse * (inverse * inverse)
            high, low = split(value)
            high_ref[sub : sub + 32, lane : lane + 128] = high
            low_ref[sub : sub + 32, lane : lane + 128] = low


def observed_kernel(total_rows, rows_here, slab_ref, table_ref, index_ref, layer_ref, high_ref, low_ref, dy2_ref, at_ref):
    pixels = dy2_ref.shape[1]
    tall = table_ref.shape[0] // 2

    @pl.when(pl.program_id(0) == 0)
    def _():
        for lane in range(0, pixels, 128):
            index = index_ref[0:1, lane : lane + 128]
            low = index & 127
            high = index >> 7
            pick = (lax.broadcasted_iota(jnp.int32, (128, 128), 0) == low).astype(BF16)
            found = dot(table_ref[...].astype(BF16), pick)
            own = lax.broadcasted_iota(jnp.int32, (tall, 128), 0) == high
            at_ref[0:1, lane : lane + 128] = jnp.sum(jnp.where(own, found[:tall], 0.0), 0, keepdims=True)
            at_ref[1:2, lane : lane + 128] = jnp.sum(jnp.where(own, found[tall:], 0.0), 0, keepdims=True)

    px = lambda lane: at_ref[0:1, lane : lane + 128]
    py = lambda lane: at_ref[1:2, lane : lane + 128]
    kernel_body(total_rows, rows_here, slab_ref, px, py, layer_ref, high_ref, low_ref, dy2_ref)


def pixel_kernel(total_rows, rows_here, slab_ref, at_in_ref, layer_ref, high_ref, low_ref, dy2_ref):
    px = lambda lane: at_in_ref[0:1, lane : lane + 128]
    py = lambda lane: at_in_ref[1:2, lane : lane + 128]
    kernel_body(total_rows, rows_here, slab_ref, px, py, layer_ref, high_ref, low_ref, dy2_ref)


def forward_kernel(total_rows, slab, layer, at=None, table=None, index=None):
    rows, cells = layer.shape
    whole = lambda a: pl.BlockSpec(a.shape, lambda i: (0,) * a.ndim)
    smem = pl.BlockSpec(memory_space=pltpu.SMEM)
    if at is None:
        pixels = index.shape[1]
        body = functools.partial(observed_kernel, total_rows, rows)
        operands = (slab, table, index, layer)
        scratch = [pltpu.VMEM((cells, pixels), F32), pltpu.VMEM((8, pixels), F32)]
    else:
        pixels = at.shape[1]
        body = functools.partial(pixel_kernel, total_rows, rows)
        operands = (slab, at, layer)
        scratch = [pltpu.VMEM((cells, pixels), F32)]
    out = jax.ShapeDtypeStruct((rows * cells, pixels), BF16)
    return pl.pallas_call(
        body,
        grid=(rows,),
        out_shape=(out, out),
        in_specs=[smem] + [whole(a) for a in operands[1:]],
        out_specs=(pl.BlockSpec((cells, pixels), lambda i: (i, 0)),) * 2,
        scratch_shapes=scratch,
        compiler_params=params(dimension_semantics=("arbitrary",)),
        cost_estimate=cost(rows * cells * pixels * 16, rows * cells * pixels * 4),
        name="kernel_of_observed" if at is None else "kernel_of_pixels",
    )(*operands)


def forecast_steps(rows, slab, slabs, head_ref, perm_ref, wells_ref, near_ref, far_ref, p_ref, k_ref):
    members, _, cells = head_ref.shape
    even = lax.rem(slab, 2) == 0
    reach = rows + 2 * STEPS
    for k in range(STEPS):
        near = near_ref[k]
        far = far_ref[k]
        before = jnp.where(even, far, near)
        after = jnp.where(even, near, far)
        p_ref[k] = before[:members]
        k_ref[k] = before[members : 2 * members]
        p_ref[STEPS + rows + k] = after[:members]
        k_ref[STEPS + rows + k] = after[members : 2 * members]
    for k in range(rows):
        p_ref[STEPS + k] = head_ref[:, k, :]
        k_ref[STEPS + k] = perm_ref[:, k, :]
    last_lane = lax.broadcasted_iota(jnp.int32, (members, cells), 1) == cells - 1
    no_before = slab == 0
    no_after = slab == slabs - 1

    def wells_of(i):
        if i < STEPS:
            return jnp.where(even, far_ref[i, 2 * members : 2 * members + 1, :], near_ref[i, 2 * members : 2 * members + 1, :])
        if i >= STEPS + rows:
            j = i - STEPS - rows
            return jnp.where(even, near_ref[j, 2 * members : 2 * members + 1, :], far_ref[j, 2 * members : 2 * members + 1, :])
        return wells_ref[i - STEPS : i - STEPS + 1, :]

    def row_flux(mobility, head, mobility_next, head_next, i):
        flux = 0.5 * (mobility_next + mobility) * (head_next - head)
        if i == STEPS - 1:
            flux = jnp.where(no_before, 0.0, flux)
        if i == STEPS + rows - 1:
            flux = jnp.where(no_after, 0.0, flux)
        return flux

    def mobility_of(i, head):
        return k_ref[i] * (1.0 + 0.5 * jnp.tanh(head))

    for step in range(STEPS):
        first = step + 1
        head_before = p_ref[first - 1]
        head = p_ref[first]
        mobility_before = mobility_of(first - 1, head_before)
        mobility = mobility_of(first, head)
        flux_before = row_flux(mobility_before, head_before, mobility, head, first - 1)
        for i in range(first, reach - first):
            head_next = p_ref[i + 1]
            mobility_next = mobility_of(i + 1, head_next)
            flux_after = row_flux(mobility, head, mobility_next, head_next, i)
            along = 0.5 * (pltpu.roll(mobility, cells - 1, 1) + mobility) * (pltpu.roll(head, cells - 1, 1) - head)
            along = jnp.where(last_lane, 0.0, along)
            inflow = (flux_after - flux_before) + (along - pltpu.roll(along, 1, 1))
            p_ref[i] = head + time_step * (inflow + wells_of(i))
            head, mobility, flux_before = head_next, mobility_next, flux_after


def forecast_kernel(slabs, slab_ref, head_ref, perm_ref, wells_ref, near_ref, far_ref, high_ref, low_ref, cast_ref, own_ref, other_ref, p_ref, k_ref, lhs_ref, wide_ref, thin_ref):
    members, rows, cells = head_ref.shape
    padded = cast_ref.shape[0]
    depth = high_ref.shape[0]
    step = pl.program_id(0)

    @pl.when(step == 0)
    def _():
        forecast_steps(rows, slab_ref[0], slabs, head_ref, perm_ref, wells_ref, near_ref, far_ref, p_ref, k_ref)
        per = depth // cells
        if padded != members:
            cast_ref[...] = jnp.zeros_like(cast_ref)
            lhs_ref[...] = jnp.zeros_like(lhs_ref)
        for i in range(rows):
            value = p_ref[STEPS + i]
            high, low = split(value)
            lane = (i % per) * cells
            cast_ref[0:members, i * cells : (i + 1) * cells] = value
            lhs_ref[i // per, 0:members, lane : lane + cells] = high
            lhs_ref[i // per, padded : padded + members, lane : lane + cells] = low

    both = lhs_ref[step]
    accumulate(step, wide_ref, dot(both, high_ref[...]))
    accumulate(step, thin_ref, dot(both[:padded], low_ref[...]))

    @pl.when(step == pl.num_programs(0) - 1)
    def _():
        half = own_ref.shape[1]
        seen = wide_ref[0:padded, :] + wide_ref[padded:, :] + thin_ref[...]
        own_ref[...] = seen[:, :half]
        other_ref[...] = seen[:, half:]


def forecast(slabs, padded, slab, head, perm, wells, near, far, high, low):
    members, rows, cells = head.shape
    total, observed = high.shape
    depth = min(total, 512)
    whole = lambda a: pl.BlockSpec(a.shape, lambda i: (0,) * a.ndim)
    const = lambda shape: pl.BlockSpec(shape, lambda i: (0,) * len(shape))
    half = (padded, observed // 2)
    return pl.pallas_call(
        functools.partial(forecast_kernel, slabs),
        grid=(total // depth,),
        out_shape=(
            jax.ShapeDtypeStruct((padded, total), F32),
            jax.ShapeDtypeStruct(half, F32),
            jax.ShapeDtypeStruct(half, F32),
        ),
        in_specs=[pl.BlockSpec(memory_space=pltpu.SMEM)]
        + [whole(a) for a in (head, perm, wells, near, far)]
        + [pl.BlockSpec((depth, observed), lambda i: (i, 0))] * 2,
        out_specs=(const((padded, total)), const(half), const(half)),
        scratch_shapes=[
            pltpu.VMEM((rows + 2 * STEPS, members, cells), F32),
            pltpu.VMEM((rows + 2 * STEPS, members, cells), F32),
            pltpu.VMEM((total // depth, 2 * padded, depth), BF16),
            pltpu.VMEM((2 * padded, observed), F32),
            pltpu.VMEM((padded, observed), F32),
        ],
        compiler_params=params(dimension_semantics=("arbitrary",)),
        cost_estimate=cost(6 * padded * total * observed, 4 * total * observed),
        name="forecast",
    )(slab, head, perm, wells, near, far, high, low)


def subsidence_kernel(groups, member_ref, *refs):
    pieces = refs[:groups]
    high_ref, low_ref, own_ref, other_ref, lhs_ref, wide_ref, thin_ref = refs[groups:]
    padded = pieces[0].shape[0]
    every = groups * padded
    depth = high_ref.shape[0]
    step = pl.program_id(0)

    for offset in range(groups):
        at = member_ref[0] ^ offset
        high, low = split(pieces[offset][...])
        lhs_ref[at] = high
        lhs_ref[groups + at] = low
    both = lhs_ref[...].reshape(2 * every, depth)
    accumulate(step, wide_ref, dot(both, high_ref[...]))
    accumulate(step, thin_ref, dot(both[:every], low_ref[...]))

    @pl.when(step == pl.num_programs(0) - 1)
    def _():
        half = own_ref.shape[1]
        seen = wide_ref[0:every, :] + wide_ref[every:, :] + thin_ref[...]
        own_ref[...] = seen[:, :half]
        other_ref[...] = seen[:, half:]


def subsidence_partial(member, pieces, high, low):
    groups = len(pieces)
    padded, total = pieces[0].shape
    pixels = high.shape[1]
    depth = min(total, 512)
    every = groups * padded
    half = (every, pixels // 2)
    out = jax.ShapeDtypeStruct(half, F32)
    return pl.pallas_call(
        functools.partial(subsidence_kernel, groups),
        grid=(total // depth,),
        out_shape=(out, out),
        in_specs=[pl.BlockSpec(memory_space=pltpu.SMEM)]
        + [pl.BlockSpec((padded, depth), lambda i: (0, i))] * groups
        + [pl.BlockSpec((depth, pixels), lambda i: (i, 0))] * 2,
        out_specs=(pl.BlockSpec(half, lambda i: (0, 0)),) * 2,
        scratch_shapes=[
            pltpu.VMEM((2 * groups, padded, depth), BF16),
            pltpu.VMEM((2 * every, pixels), F32),
            pltpu.VMEM((every, pixels), F32),
        ],
        compiler_params=params(dimension_semantics=("arbitrary",)),
        cost_estimate=cost(6 * every * total * pixels, 4 * total * pixels + 4 * every * total),
        name="subsidence",
    )(member, *pieces, high, low)


def gram_kernel(groups, members, member_ref, *refs):
    pieces = refs[:groups]
    value_ref, sigma_ref, out_ref, seen_ref = refs[groups:]
    padded, half = pieces[0].shape
    every = groups * padded
    for offset in range(groups):
        seen_ref[member_ref[0] ^ offset] = pieces[offset][...]
    seen = seen_ref[...].reshape(every, half)
    centre = jnp.sum(seen, 0, keepdims=True) * (1.0 / (groups * members))
    anomaly = seen - centre
    if padded != members:
        here = lax.rem(lax.broadcasted_iota(jnp.int32, (every, half), 0), padded) < members
        anomaly = jnp.where(here, anomaly, 0.0)
    sigma = sigma_ref[...]
    weighted = anomaly * (1.0 / (sigma * sigma))
    innovation = jnp.broadcast_to(value_ref[...] - centre, (8, half))
    extra = jnp.where(lax.broadcasted_iota(jnp.int32, (8, half), 0) == 0, innovation, 0.0)
    contract = (((1,), (1,)), ((), ()))
    out_ref[...] = jnp.zeros_like(out_ref)
    out_ref[:, 0:every] = lax.dot_general(
        weighted, anomaly, contract, precision=lax.Precision.HIGHEST, preferred_element_type=F32
    )
    out_ref[:, every : every + 8] = lax.dot_general(
        weighted, extra, contract, precision=lax.Precision.HIGHEST, preferred_element_type=F32
    )


def gram_partial(members, member, pieces, value, sigma):
    groups = len(pieces)
    padded, half = pieces[0].shape
    every = groups * padded
    width = -(-(every + 8) // 128) * 128
    vmem = pl.BlockSpec(memory_space=pltpu.VMEM)
    return pl.pallas_call(
        functools.partial(gram_kernel, groups, members),
        out_shape=jax.ShapeDtypeStruct((every, width), F32),
        in_specs=[pl.BlockSpec(memory_space=pltpu.SMEM)] + [vmem] * (groups + 2),
        out_specs=vmem,
        scratch_shapes=[pltpu.VMEM((groups, padded, half), F32)],
        compiler_params=params(),
        cost_estimate=cost(12 * every * every * half, 4 * every * half),
        name="gram",
    )(member, *pieces, value, sigma)


def eliminate_panel(rows, scaled, first, count):
    groups = count // 8
    tiles = rows.shape[1] // 128
    sub_row = lax.broadcasted_iota(jnp.int32, (8, 128), 0)
    lane = lax.broadcasted_iota(jnp.int32, (8, 128), 1)
    x = [[rows[8 * g : 8 * g + 8, 128 * t : 128 * t + 128] for t in range(tiles)] for g in range(groups)]
    full = lambda v: jnp.broadcast_to(v, (8, 128))
    scale = [None] * groups
    for s in range(groups):
        column = first + 8 * s
        tile, at = column // 128, column % 128
        c = [[full(x[g][tile][:, at + j : at + j + 1]) for g in range(s, groups)] for j in range(8)]
        scale[s] = jnp.zeros((8, 128), F32)
        for j in range(8):
            pivot = full(c[j][0][j : j + 1, :])
            inverse = pltpu.reciprocal(pivot, approx=False)
            below = sub_row > j
            m = [v * inverse for v in c[j]]
            m[0] = jnp.where(below, m[0], 0.0)
            root = lax.rsqrt(pivot)
            root = root * (1.5 - 0.5 * pivot * root * root)
            scale[s] = jnp.where(sub_row == j, root, scale[s])
            for l in range(j + 1, 8):
                entry = full(c[l][0][j : j + 1, :])
                c[l] = [v - k * entry for v, k in zip(c[l], m)]
            here = lane == at + j
            for t in range(tiles):
                row = full(x[s][t][j : j + 1, :])
                if t == tile:
                    row = jnp.where(here, 1.0, row)
                for g in range(s, groups):
                    old = x[g][t]
                    if t == tile:
                        old = jnp.where(here & below if g == s else here, 0.0, old)
                    x[g][t] = old - m[g - s] * row
    for g in range(groups):
        for t in range(tiles):
            value = x[g][t]
            column = lane + 128 * t
            row = first + 8 * g + sub_row
            inside = column < first + count
            value = jnp.where(inside & (column == row), 1.0, jnp.where(inside & (column > row), 0.0, value))
            scaled[first + 8 * g : first + 8 * g + 8, 128 * t : 128 * t + 128] = value * scale[g]


def invert(count, work_ref):
    every, width = work_ref.shape
    panel = 32
    for first in range(0, every, panel):
        eliminate_panel(work_ref[first : first + panel, :], work_ref, first, panel)
        below = first + panel
        if below < every:
            done = work_ref[first:below, :]
            product = lax.dot_general(
                done[:, below:every] if below % 128 == 0 else done[:, below // 128 * 128 : every],
                done,
                (((0,), (0,)), ((), ())),
                precision=lax.Precision.HIGHEST,
                preferred_element_type=F32,
            )
            column = lax.broadcasted_iota(jnp.int32, (every - below, width), 1)
            own = (column >= first) & (column < below)
            old = jnp.where(own, 0.0, work_ref[below:every, :])
            work_ref[below:every, :] = old - product[below - below // 128 * 128 :]


def finish_kernel(groups, members, member_ref, gram_ref, more_ref, *refs):
    pieces = refs[:groups]
    out_ref, cast_ref, work_ref = refs[groups:]
    padded, total = pieces[0].shape
    rows, cells = out_ref.shape[1:]
    every, width = work_ref.shape
    count = groups * members
    member = member_ref[0]
    for offset in range(groups):
        at = member ^ offset
        high, low = split(pieces[offset][...])
        cast_ref[at] = high
        cast_ref[groups + at] = low
    row = lax.broadcasted_iota(jnp.int32, (every, width), 0)
    column = lax.broadcasted_iota(jnp.int32, (every, width), 1)
    work_ref[...] = gram_ref[...] + more_ref[...] + jnp.where(row == column, count - 1.0, 0.0)
    invert(count, work_ref)

    solved = jnp.broadcast_to(work_ref[:, every : every + 1], (every, width))
    inverse = jnp.where(column <= row, work_ref[...], 0.0)
    weights = jnp.sum(inverse * solved, 0, keepdims=True)
    first = pl.multiple_of(member * padded, padded)
    column = lax.broadcasted_iota(jnp.int32, (padded, width), 1)
    row = lax.broadcasted_iota(jnp.int32, (padded, width), 0) + first
    own = jnp.where(column <= row, work_ref[pl.ds(first, padded), :], 0.0)
    here = column < every
    if padded != members:
        here = here & (lax.rem(column, padded) < members)
    mix = jnp.where(here, weights + math.sqrt(count - 1.0) * own, 0.0)
    mix = mix + (1.0 - jnp.sum(mix, 1, keepdims=True)) * (1.0 / count)
    mix = jnp.where(here, mix, 0.0)[:, :every]

    mix_high, mix_low = split(mix)
    mix_both = jnp.concatenate([mix_high, mix_low], 0)
    depth = 4 * cells if rows % 4 == 0 else cells
    for lane in range(0, total, depth):
        high = cast_ref[0:groups, :, lane : lane + depth].reshape(every, depth)
        low = cast_ref[groups:, :, lane : lane + depth].reshape(every, depth)
        both = dot(mix_both, high)
        value = both[:padded] + both[padded:] + dot(mix_high, low)
        for part in range(depth // cells):
            out_ref[:, lane // cells + part, :] = value[:members, part * cells : (part + 1) * cells]


def finish(members, rows, cells, member, gram, more, pieces):
    groups = len(pieces)
    padded, total = pieces[0].shape
    vmem = pl.BlockSpec(memory_space=pltpu.VMEM)
    return pl.pallas_call(
        functools.partial(finish_kernel, groups, members),
        out_shape=jax.ShapeDtypeStruct((members, rows, cells), F32),
        in_specs=[pl.BlockSpec(memory_space=pltpu.SMEM)] + [vmem] * (groups + 2),
        out_specs=vmem,
        scratch_shapes=[pltpu.VMEM((2 * groups, padded, total), BF16), pltpu.VMEM(gram.shape, F32)],
        compiler_params=params(),
        cost_estimate=cost(6 * padded * groups * padded * total, 4 * groups * padded * total),
        name="finish",
    )(member, gram, more, *pieces)


def shards(head, perm, wells, layer, coords, obs_index, obs_value, obs_sigma):
    members, rows, cells = head.shape
    groups = lax.axis_size("member")
    slabs = lax.axis_size("slab")
    slab = lax.axis_index("slab")
    member = lax.axis_index("member")
    core = slab % 2
    total_rows = rows * slabs
    padded = -(-members // 16) * 16
    slab_s = slab.astype(jnp.int32).reshape(1)
    member_s = member.astype(jnp.int32).reshape(1)
    pair = [(i, i ^ 1) for i in range(slabs)]
    across = [(i, i + 1) for i in range(1, slabs - 1, 2)] + [(i + 1, i) for i in range(1, slabs - 1, 2)]

    def swap(value, axis, offset):
        size = lax.axis_size(axis)
        return lax.ppermute(value, axis, [(i, i ^ offset) for i in range(size)])

    near, far = pack(slab_s, head, perm, wells)
    far = lax.ppermute(far, "slab", across)
    near = lax.ppermute(near, "slab", pair)

    observed = obs_index.shape[0]
    half = observed // 2

    def own_first(row):
        return jnp.where(core == 0, row, jnp.roll(row, half)).reshape(1, observed)

    pixel_total = coords.shape[1]
    table = coords.astype(F32).reshape(2 * pixel_total // 128, 128)
    high, low = forward_kernel(total_rows, slab_s, layer, table=table, index=own_first(obs_index))

    cast, own, other = forecast(slabs, padded, slab_s, head, perm, wells, near, far, high, low)
    seen = own + swap(other, "slab", 1)
    pieces = [cast] + [swap(cast, "member", offset) for offset in range(1, groups)]
    offset = 2
    while offset < slabs:
        seen = seen + swap(seen, "slab", offset)
        offset *= 2
    views = [seen] + [swap(seen, "member", offset) for offset in range(1, groups)]
    value = own_first(obs_value)[:, :half]
    sigma = own_first(obs_sigma)[:, :half]
    gram = gram_partial(members, member_s, views, value, sigma)
    gram_more = swap(gram, "slab", 1)

    chips = slabs // 2
    own_rows = pixel_total // (groups * slabs)
    at = coords.astype(F32).reshape(2, groups, chips, 2, own_rows)
    at = lax.dynamic_index_in_dim(at, member, 1, keepdims=False)
    at = jnp.swapaxes(at, 1, 2)
    at = jnp.where(core == 0, at, at[:, ::-1]).reshape(2, pixel_total // groups)
    pixel_high, pixel_low = forward_kernel(total_rows, slab_s, layer, at=at)
    sunk, sunk_other = subsidence_partial(member_s, pieces, pixel_high, pixel_low)
    sunk_recv = swap(sunk_other, "slab", 1)
    chip = slab // 2

    def block(which):
        first = which * own_rows
        return lax.dynamic_slice_in_dim(sunk, first, own_rows, 1) + lax.dynamic_slice_in_dim(
            sunk_recv, first, own_rows, 1
        )

    sunk_own = block(chip)
    for offset in range(1, chips):
        sunk_own = sunk_own + swap(block(chip ^ offset), "slab", 2 * offset)
    if padded != members:
        sunk_own = sunk_own.reshape(groups, padded, own_rows)[:, :members].reshape(groups * members, own_rows)
    subsidence = sunk_own.T

    analysed = finish(members, rows, cells, member_s, gram, gram_more, pieces)
    return (analysed, subsidence)


def solution(mesh):
    return jax.shard_map(
        shards,
        mesh=mesh,
        in_specs=(
            P("member", "slab", None),
            P("member", "slab", None),
            P("slab", None),
            P("slab", None),
            P(),
            P(),
            P(),
            P(),
        ),
        out_specs=(P("member", "slab", None), P(("member", "slab"), None)),
        check_vma=False,
    )
```

```python
import functools
import math

import jax
import jax.numpy as jnp
from jax import lax
from jax.experimental import pallas as pl
from jax.experimental.pallas import tpu as pltpu
from jax.sharding import PartitionSpec as P


STEPS = 4

time_step = 0.15
pixel_span = 64.0
top_depth = 2.0

F32 = jnp.float32
BF16 = jnp.bfloat16
MIB = 1024 * 1024


def params(mib=16, **more):
    return pltpu.CompilerParams(vmem_limit_bytes=mib * MIB, **more)


def cost(flops, bytes_accessed):
    return pl.CostEstimate(flops=int(flops), bytes_accessed=int(bytes_accessed), transcendentals=0)


def split(value):
    high = value.astype(BF16)
    return high, (value - high.astype(F32)).astype(BF16)


def dot(a, b):
    return lax.dot_general(a, b, (((1,), (0,)), ((), ())), preferred_element_type=F32)


VMEM = pl.BlockSpec(memory_space=pltpu.VMEM)
SMEM = pl.BlockSpec(memory_space=pltpu.SMEM)
HBM = pl.BlockSpec(memory_space=pltpu.HBM)


def pack_kernel(slab_ref, head_ref, perm_ref, wells_ref, *refs):
    small = (len(refs) - 3) // 2
    smalls = refs[:small]
    near_ref, far_ref = refs[small : small + 2]
    copies = refs[small + 2 : -1]
    sems = refs[-1]
    members, rows, _ = head_ref.shape
    even = lax.rem(slab_ref[0], 2) == 0
    moves = []

    def move(source, target):
        moves.append(pltpu.make_async_copy(source, target, sems.at[len(moves)]))
        moves[-1].start()

    for k in range(STEPS):
        near = jnp.where(even, rows - STEPS + k, k)
        far = jnp.where(even, k, rows - STEPS + k)
        for target, at in ((near_ref, near), (far_ref, far)):
            move(head_ref.at[:, at, :], target.at[k, 0:members, :])
            move(perm_ref.at[:, at, :], target.at[k, members : 2 * members, :])
            move(wells_ref.at[pl.ds(at, 1), :], target.at[k, 2 * members : 2 * members + 1, :])
    for source, target in zip(smalls, copies):
        move(source, target)
    for one in moves:
        one.wait()


def pack(slab, head, perm, wells, smalls):
    members, _, cells = head.shape
    out = jax.ShapeDtypeStruct((STEPS, 2 * members + 8, cells), F32)
    return pl.pallas_call(
        pack_kernel,
        out_shape=(out, out) + tuple(jax.ShapeDtypeStruct(a.shape, a.dtype) for a in smalls),
        in_specs=[SMEM] + [HBM] * (3 + len(smalls)),
        out_specs=(VMEM,) * (2 + len(smalls)),
        scratch_shapes=[pltpu.SemaphoreType.DMA((6 * STEPS + len(smalls),))],
        compiler_params=params(4),
        name="pack_rims",
    )(slab, head, perm, wells, *smalls)


def kernel_rows(total_rows, slab, at_ref, layer_ref, high_ref, low_ref, dy2_ref):
    cells, pixels = dy2_ref.shape
    rows = layer_ref.shape[0]
    position = lax.broadcasted_iota(jnp.int32, (cells, 128), 0).astype(F32)
    cell_y = (position + 0.5) * (pixel_span / cells)
    for lane in range(0, pixels, 128):
        delta = cell_y - at_ref[1:2, lane : lane + 128]
        dy2_ref[:, lane : lane + 128] = delta * delta

    def one_row(row, carry):
        cell_x = ((slab * rows + row).astype(F32) + 0.5) * (pixel_span / total_rows)
        layer = layer_ref[pl.ds(row, 1), :].astype(F32) + top_depth
        depth = jnp.swapaxes(jnp.broadcast_to(layer, (cells, cells)), 0, 1)
        depth2 = depth * depth
        scaled = depth * (pixel_span * pixel_span / (total_rows * cells))
        for lane in range(0, pixels, 128):
            delta = cell_x - at_ref[0:1, lane : lane + 128]
            dx2 = jnp.broadcast_to(delta * delta, (32, 128))
            for sub in range(0, cells, 32):
                r2 = dy2_ref[sub : sub + 32, lane : lane + 128] + dx2 + depth2[sub : sub + 32, :128]
                inverse = lax.rsqrt(r2)
                value = scaled[sub : sub + 32, :128] * inverse * (inverse * inverse)
                high, low = split(value)
                at = pl.ds(pl.multiple_of(row * cells + sub, 32), 32)
                high_ref[at, lane : lane + 128] = high
                low_ref[at, lane : lane + 128] = low
        return carry

    lax.fori_loop(0, rows, one_row, 0)


def observed_kernel(total_rows, slab_ref, coords_ref, index_ref, layer_ref, head_ref, perm_ref, high_ref, low_ref, p_ref, k_ref, dy2_ref, at_ref, table_ref, sems):
    rows = layer_ref.shape[0]
    pixels = dy2_ref.shape[1]
    tall = table_ref.shape[0] // 2
    moves = []
    for row in range(rows):
        for source, target in ((head_ref, p_ref), (perm_ref, k_ref)):
            moves.append(pltpu.make_async_copy(source.at[:, row, :], target.at[row], sems.at[len(moves)]))
            moves[-1].start()
    for row in range(tall):
        for which in range(2):
            table_ref[which * tall + row : which * tall + row + 1, :] = coords_ref[
                which : which + 1, row * 128 : row * 128 + 128
            ].astype(F32)
    table = table_ref[...].astype(BF16)
    blocks = pixels // 128
    core = lax.rem(slab_ref[0], 2)
    for block in range(blocks):
        lane = block * 128
        index = index_ref[pl.ds(lax.rem(core * (blocks // 2) + block, blocks), 1), :]
        pick = (lax.broadcasted_iota(jnp.int32, (128, 128), 0) == (index & 127)).astype(BF16)
        found = dot(table, pick)
        own = lax.broadcasted_iota(jnp.int32, (tall, 128), 0) == (index >> 7)
        at_ref[0:1, lane : lane + 128] = jnp.sum(jnp.where(own, found[:tall], 0.0), 0, keepdims=True)
        at_ref[1:2, lane : lane + 128] = jnp.sum(jnp.where(own, found[tall:], 0.0), 0, keepdims=True)
    kernel_rows(total_rows, slab_ref[0], at_ref, layer_ref, high_ref, low_ref, dy2_ref)
    for one in moves:
        one.wait()


def kernel_of_observed(total_rows, slab, coords, index, layer, head, perm):
    members = head.shape[0]
    rows, cells = layer.shape
    pixels = index.size
    out = jax.ShapeDtypeStruct((rows * cells, pixels), BF16)
    state = jax.ShapeDtypeStruct((rows, members, cells), F32)
    return pl.pallas_call(
        functools.partial(observed_kernel, total_rows),
        out_shape=(out, out, state, state),
        in_specs=[SMEM, VMEM, VMEM, VMEM, HBM, HBM],
        out_specs=(VMEM,) * 4,
        scratch_shapes=[
            pltpu.VMEM((cells, pixels), F32),
            pltpu.VMEM((8, pixels), F32),
            pltpu.VMEM((coords.size // 128, 128), F32),
            pltpu.SemaphoreType.DMA((2 * rows,)),
        ],
        compiler_params=params(20),
        cost_estimate=cost(rows * cells * pixels * 16, rows * cells * pixels * 4),
        name="kernel_of_observed",
    )(slab, coords, index, layer, head, perm)


def pixel_kernel(total_rows, chips, own_rows, slab_ref, member_ref, coords_ref, layer_ref, high_ref, low_ref, dy2_ref, at_ref):
    if own_rows % 128:
        at_ref[0:2, :] = coords_ref[...]
    else:
        core = lax.rem(slab_ref[0], 2)
        lane = 0
        for own in (core, 1 - core):
            for chip in range(chips):
                first = ((member_ref[0] * chips + chip) * 2 + own) * own_rows
                for part in range(0, own_rows, 128):
                    at = pl.ds(pl.multiple_of(first + part, 128), 128)
                    at_ref[0:2, lane : lane + 128] = coords_ref[:, at].astype(F32)
                    lane += 128
    kernel_rows(total_rows, slab_ref[0], at_ref, layer_ref, high_ref, low_ref, dy2_ref)


def kernel_of_pixels(total_rows, groups, slab, member, coords, layer):
    rows, cells = layer.shape
    slabs = total_rows // rows
    chips = slabs // 2
    own_rows = coords.shape[1] // (groups * slabs)
    pixels = slabs * own_rows
    if own_rows % 128:
        coords = coords.astype(F32).reshape(2, groups, chips, 2, own_rows)
        coords = lax.dynamic_index_in_dim(coords, member[0], 1, keepdims=False)
        coords = jnp.swapaxes(coords, 1, 2)
        coords = jnp.where(slab[0] % 2 == 0, coords, coords[:, ::-1]).reshape(2, pixels)
    out = jax.ShapeDtypeStruct((rows * cells, pixels), BF16)
    return pl.pallas_call(
        functools.partial(pixel_kernel, total_rows, chips, own_rows),
        out_shape=(out, out),
        in_specs=[SMEM, SMEM, VMEM, VMEM],
        out_specs=(VMEM,) * 2,
        scratch_shapes=[pltpu.VMEM((cells, pixels), F32), pltpu.VMEM((8, pixels), F32)],
        compiler_params=params(20),
        cost_estimate=cost(rows * cells * pixels * 16, rows * cells * pixels * 4),
        name="kernel_of_pixels",
    )(slab, member, coords, layer)


def forecast_steps(slab, slabs, start_ref, perm_ref, wells_ref, near_ref, far_ref, p_ref, rim_ref):
    rows, members, cells = start_ref.shape
    even = lax.rem(slab, 2) == 0
    reach = rows + 2 * STEPS
    for k in range(STEPS):
        near = near_ref[k, 0 : 2 * members, :]
        far = far_ref[k, 0 : 2 * members, :]
        before = jnp.where(even, far, near)
        after = jnp.where(even, near, far)
        p_ref[k] = before[:members]
        rim_ref[k] = before[members:]
        p_ref[STEPS + rows + k] = after[:members]
        rim_ref[STEPS + k] = after[members:]
    last_lane = lax.broadcasted_iota(jnp.int32, (members, cells), 1) == cells - 1
    no_before = slab == 0
    no_after = slab == slabs - 1
    well_row = slice(2 * members, 2 * members + 1)

    def wells_of(i):
        if i < STEPS:
            return jnp.where(even, far_ref[i, well_row, :], near_ref[i, well_row, :])
        if i >= STEPS + rows:
            j = i - STEPS - rows
            return jnp.where(even, near_ref[j, well_row, :], far_ref[j, well_row, :])
        return wells_ref[i - STEPS : i - STEPS + 1, :]

    def head_of(step, i):
        if step == 0 and STEPS <= i < STEPS + rows:
            return start_ref[i - STEPS]
        return p_ref[i]

    def mobility_of(i, head):
        if i < STEPS:
            perm = rim_ref[i]
        elif i >= STEPS + rows:
            perm = rim_ref[i - rows]
        else:
            perm = perm_ref[i - STEPS]
        return perm * (1.0 + 0.5 * jnp.tanh(head))

    def row_flux(mobility, head, mobility_next, head_next, i):
        flux = 0.5 * (mobility_next + mobility) * (head_next - head)
        if i == STEPS - 1:
            flux = jnp.where(no_before, 0.0, flux)
        if i == STEPS + rows - 1:
            flux = jnp.where(no_after, 0.0, flux)
        return flux

    for step in range(STEPS):
        first = step + 1
        head_before = head_of(step, first - 1)
        head = head_of(step, first)
        mobility_before = mobility_of(first - 1, head_before)
        mobility = mobility_of(first, head)
        flux_before = row_flux(mobility_before, head_before, mobility, head, first - 1)
        for i in range(first, reach - first):
            head_next = head_of(step, i + 1)
            mobility_next = mobility_of(i + 1, head_next)
            flux_after = row_flux(mobility, head, mobility_next, head_next, i)
            along = 0.5 * (pltpu.roll(mobility, cells - 1, 1) + mobility) * (pltpu.roll(head, cells - 1, 1) - head)
            along = jnp.where(last_lane, 0.0, along)
            inflow = (flux_after - flux_before) + (along - pltpu.roll(along, 1, 1))
            p_ref[i] = head + time_step * (inflow + wells_of(i))
            head, mobility, flux_before = head_next, mobility_next, flux_after


def spread_product(left, padded, high_ref, low_ref, own_ref, other_ref):
    half = own_ref.shape[1]
    wide = 256 if half % 256 == 0 else 128
    for first in range(0, 2 * half, wide):
        both = dot(left, high_ref[:, first : first + wide])
        value = both[:padded] + both[padded:] + dot(left[:padded], low_ref[:, first : first + wide])
        if first < half:
            own_ref[:, first : first + wide] = value
        else:
            other_ref[:, first - half : first - half + wide] = value


def forecast_kernel(slabs, slab_ref, start_ref, perm_ref, wells_ref, near_ref, far_ref, high_ref, low_ref, cast_ref, own_ref, other_ref, p_ref, rim_ref, left_ref):
    rows, members, cells = start_ref.shape
    padded = cast_ref.shape[0]
    forecast_steps(slab_ref[0], slabs, start_ref, perm_ref, wells_ref, near_ref, far_ref, p_ref, rim_ref)
    if padded != members:
        cast_ref[...] = jnp.zeros_like(cast_ref)
        left_ref[...] = jnp.zeros_like(left_ref)
    for i in range(rows):
        value = p_ref[STEPS + i]
        high, low = split(value)
        lane = slice(i * cells, (i + 1) * cells)
        cast_ref[0:members, lane] = value
        left_ref[0:members, lane] = high
        left_ref[padded : padded + members, lane] = low
    spread_product(left_ref[...], padded, high_ref, low_ref, own_ref, other_ref)


def forecast(slabs, padded, slab, start, perm, wells, near, far, high, low):
    rows, members, cells = start.shape
    total, observed = high.shape
    half = jax.ShapeDtypeStruct((padded, observed // 2), F32)
    return pl.pallas_call(
        functools.partial(forecast_kernel, slabs),
        out_shape=(jax.ShapeDtypeStruct((padded, total), F32), half, half),
        in_specs=[SMEM] + [VMEM] * 7,
        out_specs=(VMEM,) * 3,
        scratch_shapes=[
            pltpu.VMEM((rows + 2 * STEPS, members, cells), F32),
            pltpu.VMEM((2 * STEPS, members, cells), F32),
            pltpu.VMEM((2 * padded, total), BF16),
        ],
        compiler_params=params(20),
        cost_estimate=cost(6 * padded * total * observed, 4 * total * observed),
        name="forecast",
    )(slab, start, perm, wells, near, far, high, low)


def subsidence_kernel(groups, member_ref, *refs):
    pieces = refs[:groups]
    high_ref, low_ref, own_ref, other_ref, cast_ref = refs[groups:]
    padded, total = pieces[0].shape
    every = groups * padded
    for offset in range(groups):
        at = member_ref[0] ^ offset
        high, low = split(pieces[offset][...])
        cast_ref[at] = high
        cast_ref[groups + at] = low
    left = cast_ref[...].reshape(2 * every, total)
    spread_product(left, every, high_ref, low_ref, own_ref, other_ref)


def subsidence_partial(member, pieces, high, low):
    groups = len(pieces)
    padded, total = pieces[0].shape
    pixels = high.shape[1]
    every = groups * padded
    out = jax.ShapeDtypeStruct((every, pixels // 2), F32)
    return pl.pallas_call(
        functools.partial(subsidence_kernel, groups),
        out_shape=(out, out),
        in_specs=[SMEM] + [VMEM] * (groups + 2),
        out_specs=(VMEM,) * 2,
        scratch_shapes=[pltpu.VMEM((2 * groups, padded, total), BF16)],
        compiler_params=params(24),
        cost_estimate=cost(6 * every * total * pixels, 4 * total * pixels + 4 * every * total),
        name="subsidence",
    )(member, *pieces, high, low)


def gram_kernel(groups, members, slab_ref, member_ref, *refs):
    pieces = refs[:groups]
    value_ref, sigma_ref, out_ref, seen_ref = refs[groups:]
    padded, half = pieces[0].shape
    every = groups * padded
    for offset in range(groups):
        seen_ref[member_ref[0] ^ offset] = pieces[offset][...]
    seen = seen_ref[...].reshape(every, half)
    centre = jnp.sum(seen, 0, keepdims=True) * (1.0 / (groups * members))
    anomaly = seen - centre
    if padded != members:
        here = lax.rem(lax.broadcasted_iota(jnp.int32, (every, half), 0), padded) < members
        anomaly = jnp.where(here, anomaly, 0.0)
    blocks = half // 128
    first = lax.rem(slab_ref[0], 2) * blocks
    rows_of = lambda ref: jnp.concatenate([ref[pl.ds(first + k, 1), :] for k in range(blocks)], 1)
    sigma = rows_of(sigma_ref)
    weighted = anomaly * (1.0 / (sigma * sigma))
    innovation = jnp.broadcast_to(rows_of(value_ref) - centre, (8, half))
    extra = jnp.where(lax.broadcasted_iota(jnp.int32, (8, half), 0) == 0, innovation, 0.0)
    contract = (((1,), (1,)), ((), ()))
    out_ref[...] = jnp.zeros_like(out_ref)
    out_ref[:, 0:every] = lax.dot_general(
        weighted, anomaly, contract, precision=lax.Precision.HIGHEST, preferred_element_type=F32
    )
    out_ref[:, every : every + 8] = lax.dot_general(
        weighted, extra, contract, precision=lax.Precision.HIGHEST, preferred_element_type=F32
    )


def gram_partial(members, slab, member, pieces, value, sigma):
    groups = len(pieces)
    padded, half = pieces[0].shape
    every = groups * padded
    width = -(-(every + 8) // 128) * 128
    return pl.pallas_call(
        functools.partial(gram_kernel, groups, members),
        out_shape=jax.ShapeDtypeStruct((every, width), F32),
        in_specs=[SMEM, SMEM] + [VMEM] * (groups + 2),
        out_specs=VMEM,
        scratch_shapes=[pltpu.VMEM((groups, padded, half), F32)],
        compiler_params=params(),
        cost_estimate=cost(12 * every * every * half, 4 * every * half),
        name="gram",
    )(slab, member, *pieces, value, sigma)


def eliminate_panel(rows, scaled, first, count):
    groups = count // 8
    tiles = rows.shape[1] // 128
    sub_row = lax.broadcasted_iota(jnp.int32, (8, 128), 0)
    lane = lax.broadcasted_iota(jnp.int32, (8, 128), 1)
    x = [[rows[8 * g : 8 * g + 8, 128 * t : 128 * t + 128] for t in range(tiles)] for g in range(groups)]
    full = lambda v: jnp.broadcast_to(v, (8, 128))
    scale = [None] * groups
    for s in range(groups):
        column = first + 8 * s
        tile, at = column // 128, column % 128
        c = [[full(x[g][tile][:, at + j : at + j + 1]) for g in range(s, groups)] for j in range(8)]
        scale[s] = jnp.zeros((8, 128), F32)
        for j in range(8):
            pivot = full(c[j][0][j : j + 1, :])
            inverse = pltpu.reciprocal(pivot, approx=False)
            below = sub_row > j
            m = [v * inverse for v in c[j]]
            m[0] = jnp.where(below, m[0], 0.0)
            root = lax.rsqrt(pivot)
            root = root * (1.5 - 0.5 * pivot * root * root)
            scale[s] = jnp.where(sub_row == j, root, scale[s])
            for l in range(j + 1, 8):
                entry = full(c[l][0][j : j + 1, :])
                c[l] = [v - k * entry for v, k in zip(c[l], m)]
            here = lane == at + j
            for t in range(tiles):
                row = full(x[s][t][j : j + 1, :])
                if t == tile:
                    row = jnp.where(here, 1.0, row)
                for g in range(s, groups):
                    old = x[g][t]
                    if t == tile:
                        old = jnp.where(here & below if g == s else here, 0.0, old)
                    x[g][t] = old - m[g - s] * row
    for g in range(groups):
        for t in range(tiles):
            value = x[g][t]
            column = lane + 128 * t
            row = first + 8 * g + sub_row
            inside = column < first + count
            value = jnp.where(inside & (column == row), 1.0, jnp.where(inside & (column > row), 0.0, value))
            scaled[first + 8 * g : first + 8 * g + 8, 128 * t : 128 * t + 128] = value * scale[g]


def invert(work_ref):
    every, width = work_ref.shape
    panel = 32
    for first in range(0, every, panel):
        eliminate_panel(work_ref[first : first + panel, :], work_ref, first, panel)
        below = first + panel
        if below < every:
            done = work_ref[first:below, :]
            product = lax.dot_general(
                done[:, below:every] if below % 128 == 0 else done[:, below // 128 * 128 : every],
                done,
                (((0,), (0,)), ((), ())),
                precision=lax.Precision.HIGHEST,
                preferred_element_type=F32,
            )
            column = lax.broadcasted_iota(jnp.int32, (every - below, width), 1)
            own = (column >= first) & (column < below)
            old = jnp.where(own, 0.0, work_ref[below:every, :])
            work_ref[below:every, :] = old - product[below - below // 128 * 128 :]


def finish_kernel(groups, members, member_ref, gram_ref, more_ref, *refs):
    pieces = refs[:groups]
    out_ref, cast_ref, work_ref = refs[groups:]
    padded, total = pieces[0].shape
    rows, cells = out_ref.shape[1:]
    every, width = work_ref.shape
    count = groups * members
    member = member_ref[0]
    for offset in range(groups):
        at = member ^ offset
        high, low = split(pieces[offset][...])
        cast_ref[at] = high
        cast_ref[groups + at] = low
    row = lax.broadcasted_iota(jnp.int32, (every, width), 0)
    column = lax.broadcasted_iota(jnp.int32, (every, width), 1)
    work_ref[...] = gram_ref[...] + more_ref[...] + jnp.where(row == column, count - 1.0, 0.0)
    invert(work_ref)

    solved = jnp.broadcast_to(work_ref[:, every : every + 1], (every, width))
    inverse = jnp.where(column <= row, work_ref[...], 0.0)
    weights = jnp.sum(inverse * solved, 0, keepdims=True)
    first = pl.multiple_of(member * padded, padded)
    column = lax.broadcasted_iota(jnp.int32, (padded, width), 1)
    row = lax.broadcasted_iota(jnp.int32, (padded, width), 0) + first
    own = jnp.where(column <= row, work_ref[pl.ds(first, padded), :], 0.0)
    here = column < every
    if padded != members:
        here = here & (lax.rem(column, padded) < members)
    mix = jnp.where(here, weights + math.sqrt(count - 1.0) * own, 0.0)
    mix = mix + (1.0 - jnp.sum(mix, 1, keepdims=True)) * (1.0 / count)
    mix = jnp.where(here, mix, 0.0)[:, :every]

    mix_high, mix_low = split(mix)
    mix_both = jnp.concatenate([mix_high, mix_low], 0)
    depth = 4 * cells if rows % 4 == 0 else cells
    for lane in range(0, total, depth):
        high = cast_ref[0:groups, :, lane : lane + depth].reshape(every, depth)
        low = cast_ref[groups:, :, lane : lane + depth].reshape(every, depth)
        both = dot(mix_both, high)
        value = both[:padded] + both[padded:] + dot(mix_high, low)
        for part in range(depth // cells):
            out_ref[:, lane // cells + part, :] = value[:members, part * cells : (part + 1) * cells]


def finish(members, rows, cells, member, gram, more, pieces):
    groups = len(pieces)
    padded, total = pieces[0].shape
    return pl.pallas_call(
        functools.partial(finish_kernel, groups, members),
        out_shape=jax.ShapeDtypeStruct((members, rows, cells), F32),
        in_specs=[SMEM] + [VMEM] * (groups + 2),
        out_specs=VMEM,
        scratch_shapes=[pltpu.VMEM((2 * groups, padded, total), BF16), pltpu.VMEM(gram.shape, F32)],
        compiler_params=params(),
        cost_estimate=cost(6 * padded * groups * padded * total, 4 * groups * padded * total),
        name="finish",
    )(member, gram, more, *pieces)


def cycle(head, perm, wells, layer, coords, obs_index, obs_value, obs_sigma):
    members, rows, cells = head.shape
    groups = lax.axis_size("member")
    slabs = lax.axis_size("slab")
    slab = lax.axis_index("slab")
    member = lax.axis_index("member")
    total_rows = rows * slabs
    padded = -(-members // 16) * 16
    slab_s = slab.astype(jnp.int32).reshape(1)
    member_s = member.astype(jnp.int32).reshape(1)
    pair = [(i, i ^ 1) for i in range(slabs)]
    across = [(i, i + 1) for i in range(1, slabs - 1, 2)] + [(i + 1, i) for i in range(1, slabs - 1, 2)]

    def swap(value, axis, offset):
        size = lax.axis_size(axis)
        return lax.ppermute(value, axis, [(i, i ^ offset) for i in range(size)])

    smalls = (wells, layer, coords, *(a.reshape(-1, 128) for a in (obs_index, obs_value, obs_sigma)))
    head, perm, wells, *smalls = (
        pltpu.with_memory_space_constraint(a, pltpu.HBM) for a in (head, perm, wells, *smalls)
    )
    near, far, wells, layer, coords, index, value, sigma = pack(slab_s, head, perm, wells, smalls)
    far = lax.ppermute(far, "slab", across)
    near = lax.ppermute(near, "slab", pair)

    high, low, start, perm_rows = kernel_of_observed(total_rows, slab_s, coords, index, layer, head, perm)
    cast, own, other = forecast(slabs, padded, slab_s, start, perm_rows, wells, near, far, high, low)
    seen = own + swap(other, "slab", 1)
    pieces = [cast] + [swap(cast, "member", offset) for offset in range(1, groups)]
    offset = 2
    while offset < slabs:
        seen = seen + swap(seen, "slab", offset)
        offset *= 2
    views = [seen] + [swap(seen, "member", offset) for offset in range(1, groups)]
    gram = gram_partial(members, slab_s, member_s, views, value, sigma)
    gram_more = swap(gram, "slab", 1)

    chips = slabs // 2
    own_rows = coords.shape[1] // (groups * slabs)
    pixel_high, pixel_low = kernel_of_pixels(total_rows, groups, slab_s, member_s, coords, layer)
    sunk, sunk_other = subsidence_partial(member_s, pieces, pixel_high, pixel_low)
    sunk_recv = swap(sunk_other, "slab", 1)
    chip = slab // 2

    def block(which):
        first = which * own_rows
        return lax.dynamic_slice_in_dim(sunk, first, own_rows, 1) + lax.dynamic_slice_in_dim(
            sunk_recv, first, own_rows, 1
        )

    sunk_own = block(chip)
    for offset in range(1, chips):
        sunk_own = sunk_own + swap(block(chip ^ offset), "slab", 2 * offset)
    if padded != members:
        sunk_own = sunk_own.reshape(groups, padded, own_rows)[:, :members].reshape(groups * members, own_rows)
    subsidence = sunk_own.T

    analysed = finish(members, rows, cells, member_s, gram, gram_more, pieces)
    return (analysed, subsidence)


def solution(mesh):
    return jax.shard_map(
        cycle,
        mesh=mesh,
        in_specs=(
            P("member", "slab", None),
            P("member", "slab", None),
            P("slab", None),
            P("slab", None),
            P(),
            P(),
            P(),
            P(),
        ),
        out_specs=(P("member", "slab", None), P(("member", "slab"), None)),
        check_vma=False,
    )
```

```python
import functools
import math

import jax
import jax.numpy as jnp
from jax import lax
from jax.experimental import pallas as pl
from jax.experimental.pallas import tpu as pltpu
from jax.sharding import PartitionSpec as P


STEPS = 4

time_step = 0.15
pixel_span = 64.0
top_depth = 2.0

F32 = jnp.float32
BF16 = jnp.bfloat16

MIB = 1024 * 1024


def params(mib=16, **more):
    return pltpu.CompilerParams(vmem_limit_bytes=mib * MIB, **more)


def cost(flops, bytes_accessed):
    return pl.CostEstimate(flops=int(flops), bytes_accessed=int(bytes_accessed), transcendentals=0)


def split(value):
    high = value.astype(BF16)
    return high, (value - high.astype(F32)).astype(BF16)


def dot(a, b):
    return lax.dot_general(a, b, (((1,), (0,)), ((), ())), preferred_element_type=F32)


VMEM = pl.BlockSpec(memory_space=pltpu.VMEM)
SMEM = pl.BlockSpec(memory_space=pltpu.SMEM)
HBM = pl.BlockSpec(memory_space=pltpu.HBM)


def pack_kernel(slab_ref, head_ref, perm_ref, wells_ref, *refs):
    small = (len(refs) - 3) // 2
    smalls = refs[:small]
    near_ref, far_ref = refs[small : small + 2]
    copies = refs[small + 2 : -1]
    sems = refs[-1]
    members, rows, _ = head_ref.shape
    even = lax.rem(slab_ref[0], 2) == 0
    moves = []

    def move(source, target):
        moves.append(pltpu.make_async_copy(source, target, sems.at[len(moves)]))
        moves[-1].start()

    for k in range(STEPS):
        near = jnp.where(even, rows - STEPS + k, k)
        far = jnp.where(even, k, rows - STEPS + k)
        for target, at in ((near_ref, near), (far_ref, far)):
            move(head_ref.at[:, at, :], target.at[k, 0:members, :])
            move(perm_ref.at[:, at, :], target.at[k, members : 2 * members, :])
            move(wells_ref.at[pl.ds(at, 1), :], target.at[k, 2 * members : 2 * members + 1, :])
    for source, target in zip(smalls, copies):
        move(source, target)
    for one in moves:
        one.wait()


def pack(slab, head, perm, wells, smalls):
    members, _, cells = head.shape
    out = jax.ShapeDtypeStruct((STEPS, 2 * members + 8, cells), F32)
    return pl.pallas_call(
        pack_kernel,
        out_shape=(out, out) + tuple(jax.ShapeDtypeStruct(a.shape, a.dtype) for a in smalls),
        in_specs=[SMEM] + [HBM] * (3 + len(smalls)),
        out_specs=(VMEM,) * (2 + len(smalls)),
        scratch_shapes=[pltpu.SemaphoreType.DMA((6 * STEPS + len(smalls),))],
        compiler_params=params(4),
        name="pack_rims",
    )(slab, head, perm, wells, *smalls)


def kernel_rows(total_rows, slab, at_ref, layer_ref, out_ref, dy2_ref):
    cells, pixels = dy2_ref.shape
    rows = layer_ref.shape[0]
    position = lax.broadcasted_iota(jnp.int32, (cells, 128), 0).astype(F32)
    cell_y = (position + 0.5) * (pixel_span / cells)
    for lane in range(0, pixels, 128):
        delta = cell_y - at_ref[1:2, lane : lane + 128]
        dy2_ref[:, lane : lane + 128] = delta * delta

    def one_row(row, carry):
        cell_x = ((slab * rows + row).astype(F32) + 0.5) * (pixel_span / total_rows)
        layer = layer_ref[pl.ds(row, 1), :].astype(F32) + top_depth
        depth = jnp.swapaxes(jnp.broadcast_to(layer, (cells, cells)), 0, 1)
        depth2 = depth * depth
        scaled = depth * (pixel_span * pixel_span / (total_rows * cells))
        for lane in range(0, pixels, 128):
            delta = cell_x - at_ref[0:1, lane : lane + 128]
            dx2 = jnp.broadcast_to(delta * delta, (32, 128))
            for sub in range(0, cells, 32):
                r2 = dy2_ref[sub : sub + 32, lane : lane + 128] + dx2 + depth2[sub : sub + 32, :128]
                inverse = lax.rsqrt(r2)
                at = pl.ds(pl.multiple_of(row * cells + sub, 32), 32)
                out_ref[at, lane : lane + 128] = scaled[sub : sub + 32, :128] * inverse * (inverse * inverse)
        return carry

    lax.fori_loop(0, rows, one_row, 0, unroll=4)


def observed_kernel(total_rows, slab_ref, coords_ref, index_ref, layer_ref, head_ref, perm_ref, out_ref, p_ref, k_ref, dy2_ref, at_ref, table_ref, sems):
    rows = layer_ref.shape[0]
    pixels = dy2_ref.shape[1]
    tall = table_ref.shape[0] // 2
    moves = []
    for row in range(rows):
        for source, target in ((head_ref, p_ref), (perm_ref, k_ref)):
            moves.append(pltpu.make_async_copy(source.at[:, row, :], target.at[row], sems.at[len(moves)]))
            moves[-1].start()
    for row in range(tall):
        for which in range(2):
            table_ref[which * tall + row : which * tall + row + 1, :] = coords_ref[
                which : which + 1, row * 128 : row * 128 + 128
            ].astype(F32)
    table = table_ref[...].astype(BF16)
    blocks = pixels // 128
    core = lax.rem(slab_ref[0], 2)
    for block in range(blocks):
        lane = block * 128
        index = index_ref[pl.ds(lax.rem(core * (blocks // 2) + block, blocks), 1), :]
        pick = (lax.broadcasted_iota(jnp.int32, (128, 128), 0) == (index & 127)).astype(BF16)
        found = dot(table, pick)
        own = lax.broadcasted_iota(jnp.int32, (tall, 128), 0) == (index >> 7)
        at_ref[0:1, lane : lane + 128] = jnp.sum(jnp.where(own, found[:tall], 0.0), 0, keepdims=True)
        at_ref[1:2, lane : lane + 128] = jnp.sum(jnp.where(own, found[tall:], 0.0), 0, keepdims=True)
    kernel_rows(total_rows, slab_ref[0], at_ref, layer_ref, out_ref, dy2_ref)
    for one in moves:
        one.wait()


def kernel_of_observed(total_rows, slab, coords, index, layer, head, perm):
    members = head.shape[0]
    rows, cells = layer.shape
    pixels = index.size
    out = jax.ShapeDtypeStruct((rows * cells, pixels), F32)
    state = jax.ShapeDtypeStruct((rows, members, cells), F32)
    return pl.pallas_call(
        functools.partial(observed_kernel, total_rows),
        out_shape=(out, state, state),
        in_specs=[SMEM, VMEM, VMEM, VMEM, HBM, HBM],
        out_specs=(VMEM,) * 3,
        scratch_shapes=[
            pltpu.VMEM((cells, pixels), F32),
            pltpu.VMEM((8, pixels), F32),
            pltpu.VMEM((coords.size // 128, 128), F32),
            pltpu.SemaphoreType.DMA((2 * rows,)),
        ],
        compiler_params=params(20),
        cost_estimate=cost(rows * cells * pixels * 16, rows * cells * pixels * 4),
        name="kernel_of_observed",
    )(slab, coords, index, layer, head, perm)


def pixel_kernel(total_rows, chips, own_rows, slab_ref, member_ref, coords_ref, layer_ref, out_ref, dy2_ref, at_ref):
    if own_rows % 128:
        at_ref[0:2, :] = coords_ref[...]
    else:
        core = lax.rem(slab_ref[0], 2)
        lane = 0
        for own in (core, 1 - core):
            for chip in range(chips):
                first = ((member_ref[0] * chips + chip) * 2 + own) * own_rows
                for part in range(0, own_rows, 128):
                    at = pl.ds(pl.multiple_of(first + part, 128), 128)
                    at_ref[0:2, lane : lane + 128] = coords_ref[:, at].astype(F32)
                    lane += 128
    kernel_rows(total_rows, slab_ref[0], at_ref, layer_ref, out_ref, dy2_ref)


def kernel_of_pixels(total_rows, groups, slab, member, coords, layer):
    rows, cells = layer.shape
    slabs = total_rows // rows
    chips = slabs // 2
    own_rows = coords.shape[1] // (groups * slabs)
    pixels = slabs * own_rows
    if own_rows % 128:
        coords = coords.astype(F32).reshape(2, groups, chips, 2, own_rows)
        coords = lax.dynamic_index_in_dim(coords, member[0], 1, keepdims=False)
        coords = jnp.swapaxes(coords, 1, 2)
        coords = jnp.where(slab[0] % 2 == 0, coords, coords[:, ::-1]).reshape(2, pixels)
    out = jax.ShapeDtypeStruct((rows * cells, pixels), F32)
    return pl.pallas_call(
        functools.partial(pixel_kernel, total_rows, chips, own_rows),
        out_shape=out,
        in_specs=[SMEM, SMEM, VMEM, VMEM],
        out_specs=VMEM,
        scratch_shapes=[pltpu.VMEM((cells, pixels), F32), pltpu.VMEM((8, pixels), F32)],
        compiler_params=params(20),
        cost_estimate=cost(rows * cells * pixels * 16, rows * cells * pixels * 4),
        name="kernel_of_pixels",
    )(slab, member, coords, layer)


def forecast_steps(slab, slabs, start_ref, perm_ref, wells_ref, near_ref, far_ref, p_ref, rim_ref):
    rows, members, cells = start_ref.shape
    even = lax.rem(slab, 2) == 0
    reach = rows + 2 * STEPS
    for k in range(STEPS):
        near = near_ref[k, 0 : 2 * members, :]
        far = far_ref[k, 0 : 2 * members, :]
        before = jnp.where(even, far, near)
        after = jnp.where(even, near, far)
        p_ref[k] = before[:members]
        rim_ref[k] = before[members:]
        p_ref[STEPS + rows + k] = after[:members]
        rim_ref[STEPS + k] = after[members:]
    last_lane = lax.broadcasted_iota(jnp.int32, (members, cells), 1) == cells - 1
    no_before = slab == 0
    no_after = slab == slabs - 1
    well_row = slice(2 * members, 2 * members + 1)

    def wells_of(i):
        if i < STEPS:
            return jnp.where(even, far_ref[i, well_row, :], near_ref[i, well_row, :])
        if i >= STEPS + rows:
            j = i - STEPS - rows
            return jnp.where(even, near_ref[j, well_row, :], far_ref[j, well_row, :])
        return wells_ref[i - STEPS : i - STEPS + 1, :]

    def head_of(step, i):
        if step == 0 and STEPS <= i < STEPS + rows:
            return start_ref[i - STEPS]
        return p_ref[i]

    def mobility_of(i, head):
        if i < STEPS:
            perm = rim_ref[i]
        elif i >= STEPS + rows:
            perm = rim_ref[i - rows]
        else:
            perm = perm_ref[i - STEPS]
        return perm * (1.0 + 0.5 * jnp.tanh(head))

    def row_flux(mobility, head, mobility_next, head_next, i):
        flux = 0.5 * (mobility_next + mobility) * (head_next - head)
        if i == STEPS - 1:
            flux = jnp.where(no_before, 0.0, flux)
        if i == STEPS + rows - 1:
            flux = jnp.where(no_after, 0.0, flux)
        return flux

    for step in range(STEPS):
        first = step + 1
        head_before = head_of(step, first - 1)
        head = head_of(step, first)
        mobility_before = mobility_of(first - 1, head_before)
        mobility = mobility_of(first, head)
        flux_before = row_flux(mobility_before, head_before, mobility, head, first - 1)
        for i in range(first, reach - first):
            head_next = head_of(step, i + 1)
            mobility_next = mobility_of(i + 1, head_next)
            flux_after = row_flux(mobility, head, mobility_next, head_next, i)
            along = 0.5 * (pltpu.roll(mobility, cells - 1, 1) + mobility) * (pltpu.roll(head, cells - 1, 1) - head)
            along = jnp.where(last_lane, 0.0, along)
            inflow = (flux_after - flux_before) + (along - pltpu.roll(along, 1, 1))
            p_ref[i] = head + time_step * (inflow + wells_of(i))
            head, mobility, flux_before = head_next, mobility_next, flux_after


def spread_product(left_ref, padded, kernel_ref, own_ref, other_ref):
    half = own_ref.shape[1]
    total = kernel_ref.shape[0]
    wide = 256 if half % 256 == 0 else 128
    deep = min(total, 512)
    for first in range(0, 2 * half, wide):
        value = None
        for cell in range(0, total, deep):
            high, low = split(kernel_ref[cell : cell + deep, first : first + wide])
            both = dot(left_ref[:, cell : cell + deep], high)
            thin = dot(left_ref[:padded, cell : cell + deep], low)
            part = both[:padded] + both[padded:] + thin
            value = part if value is None else value + part
        if first < half:
            own_ref[:, first : first + wide] = value
        else:
            other_ref[:, first - half : first - half + wide] = value


def forecast_kernel(slabs, slab_ref, start_ref, perm_ref, wells_ref, near_ref, far_ref, kernel_ref, cast_ref, own_ref, other_ref, p_ref, rim_ref, left_ref):
    rows, members, cells = start_ref.shape
    padded = cast_ref.shape[0]
    forecast_steps(slab_ref[0], slabs, start_ref, perm_ref, wells_ref, near_ref, far_ref, p_ref, rim_ref)
    if padded != members:
        cast_ref[...] = jnp.zeros_like(cast_ref)
        left_ref[...] = jnp.zeros_like(left_ref)
    for i in range(rows):
        value = p_ref[STEPS + i]
        high, low = split(value)
        lane = slice(i * cells, (i + 1) * cells)
        cast_ref[0:members, lane] = value
        left_ref[0:members, lane] = high
        left_ref[padded : padded + members, lane] = low
    spread_product(left_ref, padded, kernel_ref, own_ref, other_ref)


def forecast(slabs, padded, slab, start, perm, wells, near, far, kernel):
    rows, members, cells = start.shape
    total, observed = kernel.shape
    half = jax.ShapeDtypeStruct((padded, observed // 2), F32)
    return pl.pallas_call(
        functools.partial(forecast_kernel, slabs),
        out_shape=(jax.ShapeDtypeStruct((padded, total), F32), half, half),
        in_specs=[SMEM] + [VMEM] * 6,
        out_specs=(VMEM,) * 3,
        scratch_shapes=[
            pltpu.VMEM((rows + 2 * STEPS, members, cells), F32),
            pltpu.VMEM((2 * STEPS, members, cells), F32),
            pltpu.VMEM((2 * padded, total), BF16),
        ],
        compiler_params=params(20),
        cost_estimate=cost(6 * padded * total * observed, 4 * total * observed),
        name="forecast",
    )(slab, start, perm, wells, near, far, kernel)


def subsidence_kernel(groups, member_ref, *refs):
    pieces = refs[:groups]
    kernel_ref, own_ref, other_ref, left_ref = refs[groups:]
    padded, _ = pieces[0].shape
    every = groups * padded
    for offset in range(groups):
        at = member_ref[0] ^ offset
        high, low = split(pieces[offset][...])
        left_ref[pl.ds(pl.multiple_of(at * padded, padded), padded), :] = high
        left_ref[pl.ds(pl.multiple_of(every + at * padded, padded), padded), :] = low
    spread_product(left_ref, every, kernel_ref, own_ref, other_ref)


def subsidence_partial(member, pieces, kernel):
    groups = len(pieces)
    padded, total = pieces[0].shape
    pixels = kernel.shape[1]
    every = groups * padded
    out = jax.ShapeDtypeStruct((every, pixels // 2), F32)
    return pl.pallas_call(
        functools.partial(subsidence_kernel, groups),
        out_shape=(out, out),
        in_specs=[SMEM] + [VMEM] * (groups + 1),
        out_specs=(VMEM,) * 2,
        scratch_shapes=[pltpu.VMEM((2 * every, total), BF16)],
        compiler_params=params(24),
        cost_estimate=cost(6 * every * total * pixels, 4 * total * pixels + 4 * every * total),
        name="subsidence",
    )(member, *pieces, kernel)


def gram_kernel(groups, members, slab_ref, member_ref, *refs):
    pieces = refs[:groups]
    value_ref, sigma_ref, out_ref, seen_ref = refs[groups:]
    padded, half = pieces[0].shape
    every = groups * padded
    for offset in range(groups):
        seen_ref[member_ref[0] ^ offset] = pieces[offset][...]
    seen = seen_ref[...].reshape(every, half)
    centre = jnp.sum(seen, 0, keepdims=True) * (1.0 / (groups * members))
    anomaly = seen - centre
    if padded != members:
        here = lax.rem(lax.broadcasted_iota(jnp.int32, (every, half), 0), padded) < members
        anomaly = jnp.where(here, anomaly, 0.0)
    blocks = half // 128
    first = lax.rem(slab_ref[0], 2) * blocks
    rows_of = lambda ref: jnp.concatenate([ref[pl.ds(first + k, 1), :] for k in range(blocks)], 1)
    sigma = rows_of(sigma_ref)
    weighted = anomaly * (1.0 / (sigma * sigma))
    innovation = jnp.broadcast_to(rows_of(value_ref) - centre, (8, half))
    extra = jnp.where(lax.broadcasted_iota(jnp.int32, (8, half), 0) == 0, innovation, 0.0)
    contract = (((1,), (1,)), ((), ()))
    out_ref[...] = jnp.zeros_like(out_ref)
    out_ref[:, 0:every] = lax.dot_general(
        weighted, anomaly, contract, precision=lax.Precision.HIGHEST, preferred_element_type=F32
    )
    out_ref[:, every : every + 8] = lax.dot_general(
        weighted, extra, contract, precision=lax.Precision.HIGHEST, preferred_element_type=F32
    )


def gram_partial(members, slab, member, pieces, value, sigma):
    groups = len(pieces)
    padded, half = pieces[0].shape
    every = groups * padded
    width = -(-(every + 8) // 128) * 128
    return pl.pallas_call(
        functools.partial(gram_kernel, groups, members),
        out_shape=jax.ShapeDtypeStruct((every, width), F32),
        in_specs=[SMEM, SMEM] + [VMEM] * (groups + 2),
        out_specs=VMEM,
        scratch_shapes=[pltpu.VMEM((groups, padded, half), F32)],
        compiler_params=params(),
        cost_estimate=cost(12 * every * every * half, 4 * every * half),
        name="gram",
    )(slab, member, *pieces, value, sigma)


def eliminate_panel(rows, scaled, first, count):
    groups = count // 8
    tiles = rows.shape[1] // 128
    sub_row = lax.broadcasted_iota(jnp.int32, (8, 128), 0)
    lane = lax.broadcasted_iota(jnp.int32, (8, 128), 1)
    x = [[rows[8 * g : 8 * g + 8, 128 * t : 128 * t + 128] for t in range(tiles)] for g in range(groups)]
    full = lambda v: jnp.broadcast_to(v, (8, 128))
    scale = [None] * groups
    for s in range(groups):
        column = first + 8 * s
        tile, at = column // 128, column % 128
        c = [[full(x[g][tile][:, at + j : at + j + 1]) for g in range(s, groups)] for j in range(8)]
        scale[s] = jnp.zeros((8, 128), F32)
        for j in range(8):
            pivot = full(c[j][0][j : j + 1, :])
            inverse = pltpu.reciprocal(pivot, approx=False)
            below = sub_row > j
            m = [v * inverse for v in c[j]]
            m[0] = jnp.where(below, m[0], 0.0)
            root = lax.rsqrt(pivot)
            root = root * (1.5 - 0.5 * pivot * root * root)
            scale[s] = jnp.where(sub_row == j, root, scale[s])
            for l in range(j + 1, 8):
                entry = full(c[l][0][j : j + 1, :])
                c[l] = [v - k * entry for v, k in zip(c[l], m)]
            here = lane == at + j
            for t in range(tiles):
                row = full(x[s][t][j : j + 1, :])
                if t == tile:
                    row = jnp.where(here, 1.0, row)
                for g in range(s, groups):
                    old = x[g][t]
                    if t == tile:
                        old = jnp.where(here & below if g == s else here, 0.0, old)
                    x[g][t] = old - m[g - s] * row
    for g in range(groups):
        for t in range(tiles):
            value = x[g][t]
            column = lane + 128 * t
            row = first + 8 * g + sub_row
            inside = column < first + count
            value = jnp.where(inside & (column == row), 1.0, jnp.where(inside & (column > row), 0.0, value))
            scaled[first + 8 * g : first + 8 * g + 8, 128 * t : 128 * t + 128] = value * scale[g]


def invert(work_ref):
    every, width = work_ref.shape
    panel = 32
    for first in range(0, every, panel):
        eliminate_panel(work_ref[first : first + panel, :], work_ref, first, panel)
        below = first + panel
        if below < every:
            done = work_ref[first:below, :]
            product = lax.dot_general(
                done[:, below:every] if below % 128 == 0 else done[:, below // 128 * 128 : every],
                done,
                (((0,), (0,)), ((), ())),
                precision=lax.Precision.HIGHEST,
                preferred_element_type=F32,
            )
            column = lax.broadcasted_iota(jnp.int32, (every - below, width), 1)
            own = (column >= first) & (column < below)
            old = jnp.where(own, 0.0, work_ref[below:every, :])
            work_ref[below:every, :] = old - product[below - below // 128 * 128 :]


def finish_kernel(groups, members, member_ref, gram_ref, more_ref, *refs):
    pieces = refs[:groups]
    out_ref, cast_ref, work_ref = refs[groups:]
    padded, total = pieces[0].shape
    rows, cells = out_ref.shape[1:]
    every, width = work_ref.shape
    count = groups * members
    member = member_ref[0]
    for offset in range(groups):
        at = member ^ offset
        high, low = split(pieces[offset][...])
        cast_ref[at] = high
        cast_ref[groups + at] = low
    row = lax.broadcasted_iota(jnp.int32, (every, width), 0)
    column = lax.broadcasted_iota(jnp.int32, (every, width), 1)
    work_ref[...] = gram_ref[...] + more_ref[...] + jnp.where(row == column, count - 1.0, 0.0)
    invert(work_ref)

    solved = jnp.broadcast_to(work_ref[:, every : every + 1], (every, width))
    inverse = jnp.where(column <= row, work_ref[...], 0.0)
    weights = jnp.sum(inverse * solved, 0, keepdims=True)
    first = pl.multiple_of(member * padded, padded)
    column = lax.broadcasted_iota(jnp.int32, (padded, width), 1)
    row = lax.broadcasted_iota(jnp.int32, (padded, width), 0) + first
    own = jnp.where(column <= row, work_ref[pl.ds(first, padded), :], 0.0)
    here = column < every
    if padded != members:
        here = here & (lax.rem(column, padded) < members)
    mix = jnp.where(here, weights + math.sqrt(count - 1.0) * own, 0.0)
    mix = mix + (1.0 - jnp.sum(mix, 1, keepdims=True)) * (1.0 / count)
    mix = jnp.where(here, mix, 0.0)[:, :every]

    mix_high, mix_low = split(mix)
    mix_both = jnp.concatenate([mix_high, mix_low], 0)
    depth = 4 * cells if rows % 4 == 0 else cells
    for lane in range(0, total, depth):
        high = cast_ref[0:groups, :, lane : lane + depth].reshape(every, depth)
        low = cast_ref[groups:, :, lane : lane + depth].reshape(every, depth)
        both = dot(mix_both, high)
        value = both[:padded] + both[padded:] + dot(mix_high, low)
        for part in range(depth // cells):
            out_ref[:, lane // cells + part, :] = value[:members, part * cells : (part + 1) * cells]


def finish(members, rows, cells, member, gram, more, pieces):
    groups = len(pieces)
    padded, total = pieces[0].shape
    return pl.pallas_call(
        functools.partial(finish_kernel, groups, members),
        out_shape=jax.ShapeDtypeStruct((members, rows, cells), F32),
        in_specs=[SMEM] + [VMEM] * (groups + 2),
        out_specs=VMEM,
        scratch_shapes=[pltpu.VMEM((2 * groups, padded, total), BF16), pltpu.VMEM(gram.shape, F32)],
        compiler_params=params(),
        cost_estimate=cost(6 * padded * groups * padded * total, 4 * groups * padded * total),
        name="finish",
    )(member, gram, more, *pieces)


def cycle(head, perm, wells, layer, coords, obs_index, obs_value, obs_sigma):
    members, rows, cells = head.shape
    groups = lax.axis_size("member")
    slabs = lax.axis_size("slab")
    slab = lax.axis_index("slab")
    member = lax.axis_index("member")
    total_rows = rows * slabs
    padded = -(-members // 16) * 16
    slab_s = slab.astype(jnp.int32).reshape(1)
    member_s = member.astype(jnp.int32).reshape(1)
    pair = [(i, i ^ 1) for i in range(slabs)]
    across = [(i, i + 1) for i in range(1, slabs - 1, 2)] + [(i + 1, i) for i in range(1, slabs - 1, 2)]

    def swap(value, axis, offset):
        size = lax.axis_size(axis)
        return lax.ppermute(value, axis, [(i, i ^ offset) for i in range(size)])

    smalls = (wells, layer, coords, *(a.reshape(-1, 128) for a in (obs_index, obs_value, obs_sigma)))
    head, perm, wells, *smalls = (
        pltpu.with_memory_space_constraint(a, pltpu.HBM) for a in (head, perm, wells, *smalls)
    )
    near, far, wells, layer, coords, index, value, sigma = pack(slab_s, head, perm, wells, smalls)
    far = lax.ppermute(far, "slab", across)
    near = lax.ppermute(near, "slab", pair)

    kernel, start, perm_rows = kernel_of_observed(total_rows, slab_s, coords, index, layer, head, perm)
    cast, own, other = forecast(slabs, padded, slab_s, start, perm_rows, wells, near, far, kernel)
    seen = own + swap(other, "slab", 1)
    pieces = [cast] + [swap(cast, "member", offset) for offset in range(1, groups)]
    offset = 2
    while offset < slabs:
        seen = seen + swap(seen, "slab", offset)
        offset *= 2
    views = [seen] + [swap(seen, "member", offset) for offset in range(1, groups)]
    gram = gram_partial(members, slab_s, member_s, views, value, sigma)
    gram_more = swap(gram, "slab", 1)

    chips = slabs // 2
    own_rows = coords.shape[1] // (groups * slabs)
    kernel_all = kernel_of_pixels(total_rows, groups, slab_s, member_s, coords, layer)
    sunk, sunk_other = subsidence_partial(member_s, pieces, kernel_all)
    sunk_recv = swap(sunk_other, "slab", 1)
    chip = slab // 2

    def block(which):
        first = which * own_rows
        return lax.dynamic_slice_in_dim(sunk, first, own_rows, 1) + lax.dynamic_slice_in_dim(
            sunk_recv, first, own_rows, 1
        )

    sunk_own = block(chip)
    for offset in range(1, chips):
        sunk_own = sunk_own + swap(block(chip ^ offset), "slab", 2 * offset)
    if padded != members:
        sunk_own = sunk_own.reshape(groups, padded, own_rows)[:, :members].reshape(groups * members, own_rows)
    subsidence = sunk_own.T

    analysed = finish(members, rows, cells, member_s, gram, gram_more, pieces)
    return (analysed, subsidence)


def solution(mesh):
    return jax.shard_map(
        cycle,
        mesh=mesh,
        in_specs=(
            P("member", "slab", None),
            P("member", "slab", None),
            P("slab", None),
            P("slab", None),
            P(),
            P(),
            P(),
            P(),
        ),
        out_specs=(P("member", "slab", None), P(("member", "slab"), None)),
        check_vma=False,
    )
```

```python
import functools
import math

import jax
import jax.numpy as jnp
from jax import lax
from jax.experimental import pallas as pl
from jax.experimental.pallas import tpu as pltpu
from jax.sharding import PartitionSpec as P


STEPS = 4

time_step = 0.15
pixel_span = 64.0
top_depth = 2.0

F32 = jnp.float32
BF16 = jnp.bfloat16

MIB = 1024 * 1024


def params(mib=16, **more):
    return pltpu.CompilerParams(vmem_limit_bytes=mib * MIB, **more)


def cost(flops, bytes_accessed):
    return pl.CostEstimate(flops=int(flops), bytes_accessed=int(bytes_accessed), transcendentals=0)


def split(value):
    high = value.astype(BF16)
    return high, (value - high.astype(F32)).astype(BF16)


def dot(a, b):
    return lax.dot_general(a, b, (((1,), (0,)), ((), ())), preferred_element_type=F32)


VMEM = pl.BlockSpec(memory_space=pltpu.VMEM)
SMEM = pl.BlockSpec(memory_space=pltpu.SMEM)
HBM = pl.BlockSpec(memory_space=pltpu.HBM)


def pack_kernel(slab_ref, head_ref, perm_ref, wells_ref, *refs):
    small = (len(refs) - 3) // 2
    smalls = refs[:small]
    near_ref, far_ref = refs[small : small + 2]
    copies = refs[small + 2 : -1]
    sems = refs[-1]
    members, rows, _ = head_ref.shape
    even = lax.rem(slab_ref[0], 2) == 0
    moves = []

    def move(source, target):
        moves.append(pltpu.make_async_copy(source, target, sems.at[len(moves)]))
        moves[-1].start()

    for k in range(STEPS):
        near = jnp.where(even, rows - STEPS + k, k)
        far = jnp.where(even, k, rows - STEPS + k)
        for target, at in ((near_ref, near), (far_ref, far)):
            move(head_ref.at[:, at, :], target.at[k, 0:members, :])
            move(perm_ref.at[:, at, :], target.at[k, members : 2 * members, :])
            move(wells_ref.at[pl.ds(at, 1), :], target.at[k, 2 * members : 2 * members + 1, :])
    for source, target in zip(smalls, copies):
        move(source, target)
    for one in moves:
        one.wait()


def pack(slab, head, perm, wells, smalls):
    members, _, cells = head.shape
    out = jax.ShapeDtypeStruct((STEPS, 2 * members + 8, cells), F32)
    return pl.pallas_call(
        pack_kernel,
        out_shape=(out, out) + tuple(jax.ShapeDtypeStruct(a.shape, a.dtype) for a in smalls),
        in_specs=[SMEM] + [HBM] * (3 + len(smalls)),
        out_specs=(VMEM,) * (2 + len(smalls)),
        scratch_shapes=[pltpu.SemaphoreType.DMA((6 * STEPS + len(smalls),))],
        compiler_params=params(4),
        name="pack_rims",
    )(slab, head, perm, wells, *smalls)


def kernel_rows(total_rows, slab, at_ref, layer_ref, out_ref, dy2_ref):
    cells, pixels = dy2_ref.shape
    rows = layer_ref.shape[0]
    position = lax.broadcasted_iota(jnp.int32, (cells, 128), 0).astype(F32)
    cell_y = (position + 0.5) * (pixel_span / cells)
    for lane in range(0, pixels, 128):
        delta = cell_y - at_ref[1:2, lane : lane + 128]
        dy2_ref[:, lane : lane + 128] = delta * delta

    def one_row(row, carry):
        cell_x = ((slab * rows + row).astype(F32) + 0.5) * (pixel_span / total_rows)
        layer = layer_ref[pl.ds(row, 1), :].astype(F32) + top_depth
        depth = jnp.swapaxes(jnp.broadcast_to(layer, (cells, cells)), 0, 1)
        depth2 = depth * depth
        scaled = depth * (pixel_span * pixel_span / (total_rows * cells))
        for lane in range(0, pixels, 128):
            delta = cell_x - at_ref[0:1, lane : lane + 128]
            dx2 = jnp.broadcast_to(delta * delta, (32, 128))
            for sub in range(0, cells, 32):
                r2 = dy2_ref[sub : sub + 32, lane : lane + 128] + dx2 + depth2[sub : sub + 32, :128]
                inverse = lax.rsqrt(r2)
                at = pl.ds(pl.multiple_of(row * cells + sub, 32), 32)
                out_ref[at, lane : lane + 128] = scaled[sub : sub + 32, :128] * inverse * (inverse * inverse)
        return carry

    lax.fori_loop(0, rows, one_row, 0, unroll=4)


def observed_kernel(total_rows, slab_ref, coords_ref, index_ref, layer_ref, head_ref, perm_ref, out_ref, p_ref, k_ref, dy2_ref, at_ref, table_ref, sems):
    rows = layer_ref.shape[0]
    pixels = dy2_ref.shape[1]
    tall = table_ref.shape[0] // 2
    moves = []
    for row in range(rows):
        for source, target in ((head_ref, p_ref), (perm_ref, k_ref)):
            moves.append(pltpu.make_async_copy(source.at[:, row, :], target.at[row], sems.at[len(moves)]))
            moves[-1].start()
    for row in range(tall):
        for which in range(2):
            table_ref[which * tall + row : which * tall + row + 1, :] = coords_ref[
                which : which + 1, row * 128 : row * 128 + 128
            ].astype(F32)
    table = table_ref[...].astype(BF16)
    blocks = pixels // 128
    core = lax.rem(slab_ref[0], 2)
    for block in range(blocks):
        lane = block * 128
        index = index_ref[pl.ds(lax.rem(core * (blocks // 2) + block, blocks), 1), :]
        pick = (lax.broadcasted_iota(jnp.int32, (128, 128), 0) == (index & 127)).astype(BF16)
        found = dot(table, pick)
        own = lax.broadcasted_iota(jnp.int32, (tall, 128), 0) == (index >> 7)
        at_ref[0:1, lane : lane + 128] = jnp.sum(jnp.where(own, found[:tall], 0.0), 0, keepdims=True)
        at_ref[1:2, lane : lane + 128] = jnp.sum(jnp.where(own, found[tall:], 0.0), 0, keepdims=True)
    kernel_rows(total_rows, slab_ref[0], at_ref, layer_ref, out_ref, dy2_ref)
    for one in moves:
        one.wait()


def kernel_of_observed(total_rows, slab, coords, index, layer, head, perm):
    members = head.shape[0]
    rows, cells = layer.shape
    pixels = index.size
    out = jax.ShapeDtypeStruct((rows * cells, pixels), F32)
    state = jax.ShapeDtypeStruct((rows, members, cells), F32)
    return pl.pallas_call(
        functools.partial(observed_kernel, total_rows),
        out_shape=(out, state, state),
        in_specs=[SMEM, VMEM, VMEM, VMEM, HBM, HBM],
        out_specs=(VMEM,) * 3,
        scratch_shapes=[
            pltpu.VMEM((cells, pixels), F32),
            pltpu.VMEM((8, pixels), F32),
            pltpu.VMEM((coords.size // 128, 128), F32),
            pltpu.SemaphoreType.DMA((2 * rows,)),
        ],
        compiler_params=params(20),
        cost_estimate=cost(rows * cells * pixels * 16, rows * cells * pixels * 4),
        name="kernel_of_observed",
    )(slab, coords, index, layer, head, perm)


def pixel_kernel(total_rows, chips, own_rows, slab_ref, member_ref, coords_ref, layer_ref, out_ref, dy2_ref, at_ref):
    if own_rows % 128:
        at_ref[0:2, :] = coords_ref[...]
    else:
        core = lax.rem(slab_ref[0], 2)
        lane = 0
        for own in (core, 1 - core):
            for chip in range(chips):
                first = ((member_ref[0] * chips + chip) * 2 + own) * own_rows
                for part in range(0, own_rows, 128):
                    at = pl.ds(pl.multiple_of(first + part, 128), 128)
                    at_ref[0:2, lane : lane + 128] = coords_ref[:, at].astype(F32)
                    lane += 128
    kernel_rows(total_rows, slab_ref[0], at_ref, layer_ref, out_ref, dy2_ref)


def kernel_of_pixels(total_rows, groups, slab, member, coords, layer):
    rows, cells = layer.shape
    slabs = total_rows // rows
    chips = slabs // 2
    own_rows = coords.shape[1] // (groups * slabs)
    pixels = slabs * own_rows
    if own_rows % 128:
        coords = coords.astype(F32).reshape(2, groups, chips, 2, own_rows)
        coords = lax.dynamic_index_in_dim(coords, member[0], 1, keepdims=False)
        coords = jnp.swapaxes(coords, 1, 2)
        coords = jnp.where(slab[0] % 2 == 0, coords, coords[:, ::-1]).reshape(2, pixels)
    out = jax.ShapeDtypeStruct((rows * cells, pixels), F32)
    return pl.pallas_call(
        functools.partial(pixel_kernel, total_rows, chips, own_rows),
        out_shape=out,
        in_specs=[SMEM, SMEM, VMEM, VMEM],
        out_specs=VMEM,
        scratch_shapes=[pltpu.VMEM((cells, pixels), F32), pltpu.VMEM((8, pixels), F32)],
        compiler_params=params(20),
        cost_estimate=cost(rows * cells * pixels * 16, rows * cells * pixels * 4),
        name="kernel_of_pixels",
    )(slab, member, coords, layer)


def forecast_steps(slab, slabs, start_ref, perm_ref, wells_ref, near_ref, far_ref, p_ref, rim_ref):
    rows, members, cells = start_ref.shape
    even = lax.rem(slab, 2) == 0
    reach = rows + 2 * STEPS
    for k in range(STEPS):
        near = near_ref[k, 0 : 2 * members, :]
        far = far_ref[k, 0 : 2 * members, :]
        before = jnp.where(even, far, near)
        after = jnp.where(even, near, far)
        p_ref[k] = before[:members]
        rim_ref[k] = before[members:]
        p_ref[STEPS + rows + k] = after[:members]
        rim_ref[STEPS + k] = after[members:]
    last_lane = lax.broadcasted_iota(jnp.int32, (members, cells), 1) == cells - 1
    no_before = slab == 0
    no_after = slab == slabs - 1
    well_row = slice(2 * members, 2 * members + 1)

    def wells_of(i):
        if i < STEPS:
            return jnp.where(even, far_ref[i, well_row, :], near_ref[i, well_row, :])
        if i >= STEPS + rows:
            j = i - STEPS - rows
            return jnp.where(even, near_ref[j, well_row, :], far_ref[j, well_row, :])
        return wells_ref[i - STEPS : i - STEPS + 1, :]

    def head_of(step, i):
        if step == 0 and STEPS <= i < STEPS + rows:
            return start_ref[i - STEPS]
        return p_ref[i]

    def mobility_of(i, head):
        if i < STEPS:
            perm = rim_ref[i]
        elif i >= STEPS + rows:
            perm = rim_ref[i - rows]
        else:
            perm = perm_ref[i - STEPS]
        return perm * (1.0 + 0.5 * jnp.tanh(head))

    def row_flux(mobility, head, mobility_next, head_next, i):
        flux = 0.5 * (mobility_next + mobility) * (head_next - head)
        if i == STEPS - 1:
            flux = jnp.where(no_before, 0.0, flux)
        if i == STEPS + rows - 1:
            flux = jnp.where(no_after, 0.0, flux)
        return flux

    for step in range(STEPS):
        first = step + 1
        head_before = head_of(step, first - 1)
        head = head_of(step, first)
        mobility_before = mobility_of(first - 1, head_before)
        mobility = mobility_of(first, head)
        flux_before = row_flux(mobility_before, head_before, mobility, head, first - 1)
        for i in range(first, reach - first):
            head_next = head_of(step, i + 1)
            mobility_next = mobility_of(i + 1, head_next)
            flux_after = row_flux(mobility, head, mobility_next, head_next, i)
            along = 0.5 * (pltpu.roll(mobility, cells - 1, 1) + mobility) * (pltpu.roll(head, cells - 1, 1) - head)
            along = jnp.where(last_lane, 0.0, along)
            inflow = (flux_after - flux_before) + (along - pltpu.roll(along, 1, 1))
            p_ref[i] = head + time_step * (inflow + wells_of(i))
            head, mobility, flux_before = head_next, mobility_next, flux_after


def spread_product(left_ref, padded, kernel_ref, own_ref, other_ref):
    half = own_ref.shape[1]
    total = kernel_ref.shape[0]
    wide = 256 if half % 256 == 0 else 128
    deep = min(total, 512)
    for first in range(0, 2 * half, wide):
        value = None
        for cell in range(0, total, deep):
            high, low = split(kernel_ref[cell : cell + deep, first : first + wide])
            both = dot(left_ref[:, cell : cell + deep], high)
            thin = dot(left_ref[:padded, cell : cell + deep], low)
            part = both[:padded] + both[padded:] + thin
            value = part if value is None else value + part
        if first < half:
            own_ref[:, first : first + wide] = value
        else:
            other_ref[:, first - half : first - half + wide] = value


def forecast_kernel(slabs, slab_ref, start_ref, perm_ref, wells_ref, near_ref, far_ref, kernel_ref, cast_ref, own_ref, other_ref, p_ref, rim_ref, left_ref):
    rows, members, cells = start_ref.shape
    padded = cast_ref.shape[0]
    forecast_steps(slab_ref[0], slabs, start_ref, perm_ref, wells_ref, near_ref, far_ref, p_ref, rim_ref)
    if padded != members:
        cast_ref[...] = jnp.zeros_like(cast_ref)
        left_ref[...] = jnp.zeros_like(left_ref)
    for i in range(rows):
        value = p_ref[STEPS + i]
        high, low = split(value)
        lane = slice(i * cells, (i + 1) * cells)
        cast_ref[0:members, lane] = value
        left_ref[0:members, lane] = high
        left_ref[padded : padded + members, lane] = low
    spread_product(left_ref, padded, kernel_ref, own_ref, other_ref)


def forecast(slabs, padded, slab, start, perm, wells, near, far, kernel):
    rows, members, cells = start.shape
    total, observed = kernel.shape
    half = jax.ShapeDtypeStruct((padded, observed // 2), F32)
    return pl.pallas_call(
        functools.partial(forecast_kernel, slabs),
        out_shape=(jax.ShapeDtypeStruct((padded, total), F32), half, half),
        in_specs=[SMEM] + [VMEM] * 6,
        out_specs=(VMEM,) * 3,
        scratch_shapes=[
            pltpu.VMEM((rows + 2 * STEPS, members, cells), F32),
            pltpu.VMEM((2 * STEPS, members, cells), F32),
            pltpu.VMEM((2 * padded, total), BF16),
        ],
        compiler_params=params(20),
        cost_estimate=cost(6 * padded * total * observed, 4 * total * observed),
        name="forecast",
    )(slab, start, perm, wells, near, far, kernel)


def subsidence_kernel(groups, member_ref, *refs):
    pieces = refs[:groups]
    kernel_ref, own_ref, other_ref, left_ref = refs[groups:]
    padded, _ = pieces[0].shape
    every = groups * padded
    for offset in range(groups):
        at = member_ref[0] ^ offset
        high, low = split(pieces[offset][...])
        left_ref[pl.ds(pl.multiple_of(at * padded, padded), padded), :] = high
        left_ref[pl.ds(pl.multiple_of(every + at * padded, padded), padded), :] = low
    spread_product(left_ref, every, kernel_ref, own_ref, other_ref)


def subsidence_partial(member, pieces, kernel):
    groups = len(pieces)
    padded, total = pieces[0].shape
    pixels = kernel.shape[1]
    every = groups * padded
    out = jax.ShapeDtypeStruct((every, pixels // 2), F32)
    return pl.pallas_call(
        functools.partial(subsidence_kernel, groups),
        out_shape=(out, out),
        in_specs=[SMEM] + [VMEM] * (groups + 1),
        out_specs=(VMEM,) * 2,
        scratch_shapes=[pltpu.VMEM((2 * every, total), BF16)],
        compiler_params=params(24),
        cost_estimate=cost(6 * every * total * pixels, 4 * total * pixels + 4 * every * total),
        name="subsidence",
    )(member, *pieces, kernel)


def gram_kernel(groups, members, slab_ref, member_ref, *refs):
    pieces = refs[:groups]
    value_ref, sigma_ref, out_ref, seen_ref = refs[groups:]
    padded, half = pieces[0].shape
    every = groups * padded
    for offset in range(groups):
        seen_ref[member_ref[0] ^ offset] = pieces[offset][...]
    seen = seen_ref[...].reshape(every, half)
    centre = jnp.sum(seen, 0, keepdims=True) * (1.0 / (groups * members))
    anomaly = seen - centre
    if padded != members:
        here = lax.rem(lax.broadcasted_iota(jnp.int32, (every, half), 0), padded) < members
        anomaly = jnp.where(here, anomaly, 0.0)
    blocks = half // 128
    first = lax.rem(slab_ref[0], 2) * blocks
    rows_of = lambda ref: jnp.concatenate([ref[pl.ds(first + k, 1), :] for k in range(blocks)], 1)
    sigma = rows_of(sigma_ref)
    weighted = anomaly * (1.0 / (sigma * sigma))
    innovation = jnp.broadcast_to(rows_of(value_ref) - centre, (8, half))
    extra = jnp.where(lax.broadcasted_iota(jnp.int32, (8, half), 0) == 0, innovation, 0.0)
    contract = (((1,), (1,)), ((), ()))
    out_ref[...] = jnp.zeros_like(out_ref)
    out_ref[:, 0:every] = lax.dot_general(
        weighted, anomaly, contract, precision=lax.Precision.HIGHEST, preferred_element_type=F32
    )
    out_ref[:, every : every + 8] = lax.dot_general(
        weighted, extra, contract, precision=lax.Precision.HIGHEST, preferred_element_type=F32
    )


def gram_partial(members, slab, member, pieces, value, sigma):
    groups = len(pieces)
    padded, half = pieces[0].shape
    every = groups * padded
    width = -(-(every + 8) // 128) * 128
    return pl.pallas_call(
        functools.partial(gram_kernel, groups, members),
        out_shape=jax.ShapeDtypeStruct((every, width), F32),
        in_specs=[SMEM, SMEM] + [VMEM] * (groups + 2),
        out_specs=VMEM,
        scratch_shapes=[pltpu.VMEM((groups, padded, half), F32)],
        compiler_params=params(),
        cost_estimate=cost(12 * every * every * half, 4 * every * half),
        name="gram",
    )(slab, member, *pieces, value, sigma)


COLUMNS = 8


def eliminate_panel(rows, scaled, first, count):
    groups = count // 8
    tiles = rows.shape[1] // 128
    sub_row = lax.broadcasted_iota(jnp.int32, (8, 128), 0)
    lane = lax.broadcasted_iota(jnp.int32, (8, 128), 1)
    x = [[rows[8 * g : 8 * g + 8, 128 * t : 128 * t + 128] for t in range(tiles)] for g in range(groups)]
    pick = lambda v, j: jnp.take_along_axis(v, jnp.full((8, 128), j, jnp.int32), 0, mode="promise_in_bounds")
    scale = [jnp.zeros((8, 128), F32) for _ in range(groups)]
    batch = min(COLUMNS, count)
    for start in range(0, count, batch):
        low = start // 8
        c = []
        for j in range(batch):
            tile, at = (first + start + j) // 128, (first + start + j) % 128
            c.append({g: jnp.broadcast_to(x[g][tile][:, at : at + 1], (8, 128)) for g in range(low, groups)})
        pivot = pick(c[0][low], 0)
        for j in range(batch):
            own, sub = low + j // 8, j % 8
            tile, at = (first + start + j) // 128, (first + start + j) % 128
            inverse = pltpu.reciprocal(pivot, approx=False)
            root = lax.rsqrt(pivot)
            root = root * (1.5 - 0.5 * pivot * root * root)
            scale[own] = jnp.where(sub_row == sub, root, scale[own])
            if j + 1 < batch:
                after, after_sub = low + (j + 1) // 8, (j + 1) % 8
                cross = pick(c[j][after], after_sub) * pick(c[j + 1][own], sub)
                pivot = pick(c[j + 1][after], after_sub) - cross * inverse
            for l in range(j + 1, batch):
                entry = pick(c[l][own], sub)
                for g in range(own, groups):
                    c[l][g] = c[l][g] - (c[j][g] * entry) * inverse
            below = sub_row > sub
            m = {g: c[j][g] * inverse for g in range(own, groups)}
            m[own] = jnp.where(below, m[own], 0.0)
            here = lane == at
            for t in range(tiles):
                row = pick(x[own][t], sub)
                if t == tile:
                    row = jnp.where(here, 1.0, row)
                for g in range(own, groups):
                    old = x[g][t]
                    if t == tile:
                        old = jnp.where(here & below if g == own else here, 0.0, old)
                    x[g][t] = old - m[g] * row
    for g in range(groups):
        for t in range(tiles):
            value = x[g][t]
            column = lane + 128 * t
            row = first + 8 * g + sub_row
            inside = column < first + count
            value = jnp.where(inside & (column == row), 1.0, jnp.where(inside & (column > row), 0.0, value))
            scaled[first + 8 * g : first + 8 * g + 8, 128 * t : 128 * t + 128] = value * scale[g]


def invert(work_ref):
    every, width = work_ref.shape
    panel = math.gcd(every, 64)
    for first in range(0, every, panel):
        eliminate_panel(work_ref[first : first + panel, :], work_ref, first, panel)
        below = first + panel
        if below < every:
            done = work_ref[first:below, :]
            base = below // 128 * 128
            one = done.astype(BF16)
            rest = done - one.astype(F32)
            two = rest.astype(BF16)
            three = (rest - two.astype(F32)).astype(BF16)
            left = jnp.concatenate([one, one, two, two, one, three], 0)[:, base:every]
            right = jnp.concatenate([one, two, one, two, three, one], 0)
            product = lax.dot_general(
                left, right, (((0,), (0,)), ((), ())), preferred_element_type=F32
            )
            column = lax.broadcasted_iota(jnp.int32, (every - below, width), 1)
            own = (column >= first) & (column < below)
            old = jnp.where(own, 0.0, work_ref[below:every, :])
            work_ref[below:every, :] = old - product[below - base :]


def finish_kernel(groups, members, member_ref, gram_ref, more_ref, *refs):
    pieces = refs[:groups]
    out_ref, cast_ref, work_ref = refs[groups:]
    padded, total = pieces[0].shape
    rows, cells = out_ref.shape[1:]
    every, width = work_ref.shape
    count = groups * members
    member = member_ref[0]
    for offset in range(groups):
        at = member ^ offset
        high, low = split(pieces[offset][...])
        cast_ref[at] = high
        cast_ref[groups + at] = low
    row = lax.broadcasted_iota(jnp.int32, (every, width), 0)
    column = lax.broadcasted_iota(jnp.int32, (every, width), 1)
    work_ref[...] = gram_ref[...] + more_ref[...] + jnp.where(row == column, count - 1.0, 0.0)
    invert(work_ref)

    solved = jnp.broadcast_to(work_ref[:, every : every + 1], (every, width))
    inverse = jnp.where(column <= row, work_ref[...], 0.0)
    weights = jnp.sum(inverse * solved, 0, keepdims=True)
    first = pl.multiple_of(member * padded, padded)
    column = lax.broadcasted_iota(jnp.int32, (padded, width), 1)
    row = lax.broadcasted_iota(jnp.int32, (padded, width), 0) + first
    own = jnp.where(column <= row, work_ref[pl.ds(first, padded), :], 0.0)
    here = column < every
    if padded != members:
        here = here & (lax.rem(column, padded) < members)
    mix = jnp.where(here, weights + math.sqrt(count - 1.0) * own, 0.0)
    mix = mix + (1.0 - jnp.sum(mix, 1, keepdims=True)) * (1.0 / count)
    mix = jnp.where(here, mix, 0.0)[:, :every]

    mix_high, mix_low = split(mix)
    mix_both = jnp.concatenate([mix_high, mix_low], 0)
    depth = 4 * cells if rows % 4 == 0 else cells
    for lane in range(0, total, depth):
        high = cast_ref[0:groups, :, lane : lane + depth].reshape(every, depth)
        low = cast_ref[groups:, :, lane : lane + depth].reshape(every, depth)
        both = dot(mix_both, high)
        value = both[:padded] + both[padded:] + dot(mix_high, low)
        for part in range(depth // cells):
            out_ref[:, lane // cells + part, :] = value[:members, part * cells : (part + 1) * cells]


def finish(members, rows, cells, member, gram, more, pieces):
    groups = len(pieces)
    padded, total = pieces[0].shape
    return pl.pallas_call(
        functools.partial(finish_kernel, groups, members),
        out_shape=jax.ShapeDtypeStruct((members, rows, cells), F32),
        in_specs=[SMEM] + [VMEM] * (groups + 2),
        out_specs=VMEM,
        scratch_shapes=[pltpu.VMEM((2 * groups, padded, total), BF16), pltpu.VMEM(gram.shape, F32)],
        compiler_params=params(),
        cost_estimate=cost(6 * padded * groups * padded * total, 4 * groups * padded * total),
        name="finish",
    )(member, gram, more, *pieces)


def cycle(head, perm, wells, layer, coords, obs_index, obs_value, obs_sigma):
    members, rows, cells = head.shape
    groups = lax.axis_size("member")
    slabs = lax.axis_size("slab")
    slab = lax.axis_index("slab")
    member = lax.axis_index("member")
    total_rows = rows * slabs
    padded = -(-members // 16) * 16
    slab_s = slab.astype(jnp.int32).reshape(1)
    member_s = member.astype(jnp.int32).reshape(1)
    pair = [(i, i ^ 1) for i in range(slabs)]
    across = [(i, i + 1) for i in range(1, slabs - 1, 2)] + [(i + 1, i) for i in range(1, slabs - 1, 2)]

    def swap(value, axis, offset):
        size = lax.axis_size(axis)
        return lax.ppermute(value, axis, [(i, i ^ offset) for i in range(size)])

    smalls = (wells, layer, coords, *(a.reshape(-1, 128) for a in (obs_index, obs_value, obs_sigma)))
    head, perm, wells, *smalls = (
        pltpu.with_memory_space_constraint(a, pltpu.HBM) for a in (head, perm, wells, *smalls)
    )
    near, far, wells, layer, coords, index, value, sigma = pack(slab_s, head, perm, wells, smalls)
    far = lax.ppermute(far, "slab", across)
    near = lax.ppermute(near, "slab", pair)

    kernel, start, perm_rows = kernel_of_observed(total_rows, slab_s, coords, index, layer, head, perm)
    cast, own, other = forecast(slabs, padded, slab_s, start, perm_rows, wells, near, far, kernel)
    seen = own + swap(other, "slab", 1)
    pieces = [cast] + [swap(cast, "member", offset) for offset in range(1, groups)]
    offset = 2
    while offset < slabs:
        seen = seen + swap(seen, "slab", offset)
        offset *= 2
    views = [seen] + [swap(seen, "member", offset) for offset in range(1, groups)]
    gram = gram_partial(members, slab_s, member_s, views, value, sigma)
    gram_more = swap(gram, "slab", 1)

    chips = slabs // 2
    own_rows = coords.shape[1] // (groups * slabs)
    kernel_all = kernel_of_pixels(total_rows, groups, slab_s, member_s, coords, layer)
    sunk, sunk_other = subsidence_partial(member_s, pieces, kernel_all)
    sunk_recv = swap(sunk_other, "slab", 1)
    chip = slab // 2

    def block(which):
        first = which * own_rows
        return lax.dynamic_slice_in_dim(sunk, first, own_rows, 1) + lax.dynamic_slice_in_dim(
            sunk_recv, first, own_rows, 1
        )

    sunk_own = block(chip)
    for offset in range(1, chips):
        sunk_own = sunk_own + swap(block(chip ^ offset), "slab", 2 * offset)
    if padded != members:
        sunk_own = sunk_own.reshape(groups, padded, own_rows)[:, :members].reshape(groups * members, own_rows)
    subsidence = sunk_own.T

    analysed = finish(members, rows, cells, member_s, gram, gram_more, pieces)
    return (analysed, subsidence)


def solution(mesh):
    return jax.shard_map(
        cycle,
        mesh=mesh,
        in_specs=(
            P("member", "slab", None),
            P("member", "slab", None),
            P("slab", None),
            P("slab", None),
            P(),
            P(),
            P(),
            P(),
        ),
        out_specs=(P("member", "slab", None), P(("member", "slab"), None)),
        check_vma=False,
    )
```

```python
import functools
import math

import jax
import jax.numpy as jnp
from jax import lax
from jax.experimental import pallas as pl
from jax.experimental.pallas import tpu as pltpu
from jax.sharding import PartitionSpec as P


STEPS = 4

time_step = 0.15
pixel_span = 64.0
top_depth = 2.0

F32 = jnp.float32
BF16 = jnp.bfloat16

MIB = 1024 * 1024


def params(mib=16, **more):
    return pltpu.CompilerParams(vmem_limit_bytes=mib * MIB, **more)


def cost(flops, bytes_accessed):
    return pl.CostEstimate(flops=int(flops), bytes_accessed=int(bytes_accessed), transcendentals=0)


def split(value):
    high = value.astype(BF16)
    return high, (value - high.astype(F32)).astype(BF16)


def dot(a, b):
    return lax.dot_general(a, b, (((1,), (0,)), ((), ())), preferred_element_type=F32)


VMEM = pl.BlockSpec(memory_space=pltpu.VMEM)
SMEM = pl.BlockSpec(memory_space=pltpu.SMEM)
HBM = pl.BlockSpec(memory_space=pltpu.HBM)


def pack_kernel(slab_ref, head_ref, perm_ref, wells_ref, *refs):
    small = (len(refs) - 3) // 2
    smalls = refs[:small]
    near_ref, far_ref = refs[small : small + 2]
    copies = refs[small + 2 : -1]
    sems = refs[-1]
    members, rows, _ = head_ref.shape
    even = lax.rem(slab_ref[0], 2) == 0
    moves = []

    def move(source, target):
        moves.append(pltpu.make_async_copy(source, target, sems.at[len(moves)]))
        moves[-1].start()

    for k in range(STEPS):
        near = jnp.where(even, rows - STEPS + k, k)
        far = jnp.where(even, k, rows - STEPS + k)
        for target, at in ((near_ref, near), (far_ref, far)):
            move(head_ref.at[:, at, :], target.at[k, 0:members, :])
            move(perm_ref.at[:, at, :], target.at[k, members : 2 * members, :])
            move(wells_ref.at[pl.ds(at, 1), :], target.at[k, 2 * members : 2 * members + 1, :])
    for source, target in zip(smalls, copies):
        move(source, target)
    for one in moves:
        one.wait()


def pack(slab, head, perm, wells, smalls):
    members, _, cells = head.shape
    out = jax.ShapeDtypeStruct((STEPS, 2 * members + 8, cells), F32)
    return pl.pallas_call(
        pack_kernel,
        out_shape=(out, out) + tuple(jax.ShapeDtypeStruct(a.shape, a.dtype) for a in smalls),
        in_specs=[SMEM] + [HBM] * (3 + len(smalls)),
        out_specs=(VMEM,) * (2 + len(smalls)),
        scratch_shapes=[pltpu.SemaphoreType.DMA((6 * STEPS + len(smalls),))],
        compiler_params=params(4),
        name="pack_rims",
    )(slab, head, perm, wells, *smalls)


def kernel_rows(total_rows, slab, at_ref, layer_ref, out_ref, dy2_ref):
    cells, pixels = dy2_ref.shape
    rows = layer_ref.shape[0]
    position = lax.broadcasted_iota(jnp.int32, (cells, 128), 0).astype(F32)
    cell_y = (position + 0.5) * (pixel_span / cells)
    for lane in range(0, pixels, 128):
        delta = cell_y - at_ref[1:2, lane : lane + 128]
        dy2_ref[:, lane : lane + 128] = delta * delta

    def one_row(row, carry):
        cell_x = ((slab * rows + row).astype(F32) + 0.5) * (pixel_span / total_rows)
        layer = layer_ref[pl.ds(row, 1), :].astype(F32) + top_depth
        depth = jnp.swapaxes(jnp.broadcast_to(layer, (cells, cells)), 0, 1)
        depth2 = depth * depth
        scaled = depth * (pixel_span * pixel_span / (total_rows * cells))
        for lane in range(0, pixels, 128):
            delta = cell_x - at_ref[0:1, lane : lane + 128]
            dx2 = jnp.broadcast_to(delta * delta, (32, 128))
            for sub in range(0, cells, 32):
                r2 = dy2_ref[sub : sub + 32, lane : lane + 128] + dx2 + depth2[sub : sub + 32, :128]
                inverse = lax.rsqrt(r2)
                at = pl.ds(pl.multiple_of(row * cells + sub, 32), 32)
                out_ref[at, lane : lane + 128] = scaled[sub : sub + 32, :128] * inverse * (inverse * inverse)
        return carry

    lax.fori_loop(0, rows, one_row, 0, unroll=4)


def observed_kernel(total_rows, slab_ref, coords_ref, index_ref, layer_ref, head_ref, perm_ref, out_ref, p_ref, k_ref, dy2_ref, at_ref, table_ref, sems):
    rows = layer_ref.shape[0]
    pixels = dy2_ref.shape[1]
    tall = table_ref.shape[0] // 2
    moves = []
    for row in range(rows):
        for source, target in ((head_ref, p_ref), (perm_ref, k_ref)):
            moves.append(pltpu.make_async_copy(source.at[:, row, :], target.at[row], sems.at[len(moves)]))
            moves[-1].start()
    for row in range(tall):
        for which in range(2):
            table_ref[which * tall + row : which * tall + row + 1, :] = coords_ref[
                which : which + 1, row * 128 : row * 128 + 128
            ].astype(F32)
    table = table_ref[...].astype(BF16)
    blocks = pixels // 128
    core = lax.rem(slab_ref[0], 2)
    for block in range(blocks):
        lane = block * 128
        index = index_ref[pl.ds(lax.rem(core * (blocks // 2) + block, blocks), 1), :]
        pick = (lax.broadcasted_iota(jnp.int32, (128, 128), 0) == (index & 127)).astype(BF16)
        found = dot(table, pick)
        own = lax.broadcasted_iota(jnp.int32, (tall, 128), 0) == (index >> 7)
        at_ref[0:1, lane : lane + 128] = jnp.sum(jnp.where(own, found[:tall], 0.0), 0, keepdims=True)
        at_ref[1:2, lane : lane + 128] = jnp.sum(jnp.where(own, found[tall:], 0.0), 0, keepdims=True)
    kernel_rows(total_rows, slab_ref[0], at_ref, layer_ref, out_ref, dy2_ref)
    for one in moves:
        one.wait()


def kernel_of_observed(total_rows, slab, coords, index, layer, head, perm):
    members = head.shape[0]
    rows, cells = layer.shape
    pixels = index.size
    out = jax.ShapeDtypeStruct((rows * cells, pixels), F32)
    state = jax.ShapeDtypeStruct((rows, members, cells), F32)
    return pl.pallas_call(
        functools.partial(observed_kernel, total_rows),
        out_shape=(out, state, state),
        in_specs=[SMEM, VMEM, VMEM, VMEM, HBM, HBM],
        out_specs=(VMEM,) * 3,
        scratch_shapes=[
            pltpu.VMEM((cells, pixels), F32),
            pltpu.VMEM((8, pixels), F32),
            pltpu.VMEM((coords.size // 128, 128), F32),
            pltpu.SemaphoreType.DMA((2 * rows,)),
        ],
        compiler_params=params(20),
        cost_estimate=cost(rows * cells * pixels * 16, rows * cells * pixels * 4),
        name="kernel_of_observed",
    )(slab, coords, index, layer, head, perm)


def pixel_kernel(total_rows, chips, own_rows, slab_ref, member_ref, coords_ref, layer_ref, out_ref, dy2_ref, at_ref):
    if own_rows % 128:
        at_ref[0:2, :] = coords_ref[...]
    else:
        core = lax.rem(slab_ref[0], 2)
        lane = 0
        for own in (core, 1 - core):
            for chip in range(chips):
                first = ((member_ref[0] * chips + chip) * 2 + own) * own_rows
                for part in range(0, own_rows, 128):
                    at = pl.ds(pl.multiple_of(first + part, 128), 128)
                    at_ref[0:2, lane : lane + 128] = coords_ref[:, at].astype(F32)
                    lane += 128
    kernel_rows(total_rows, slab_ref[0], at_ref, layer_ref, out_ref, dy2_ref)


def kernel_of_pixels(total_rows, groups, slab, member, coords, layer):
    rows, cells = layer.shape
    slabs = total_rows // rows
    chips = slabs // 2
    own_rows = coords.shape[1] // (groups * slabs)
    pixels = slabs * own_rows
    if own_rows % 128:
        coords = coords.astype(F32).reshape(2, groups, chips, 2, own_rows)
        coords = lax.dynamic_index_in_dim(coords, member[0], 1, keepdims=False)
        coords = jnp.swapaxes(coords, 1, 2)
        coords = jnp.where(slab[0] % 2 == 0, coords, coords[:, ::-1]).reshape(2, pixels)
    out = jax.ShapeDtypeStruct((rows * cells, pixels), F32)
    return pl.pallas_call(
        functools.partial(pixel_kernel, total_rows, chips, own_rows),
        out_shape=out,
        in_specs=[SMEM, SMEM, VMEM, VMEM],
        out_specs=VMEM,
        scratch_shapes=[pltpu.VMEM((cells, pixels), F32), pltpu.VMEM((8, pixels), F32)],
        compiler_params=params(20),
        cost_estimate=cost(rows * cells * pixels * 16, rows * cells * pixels * 4),
        name="kernel_of_pixels",
    )(slab, member, coords, layer)


def forecast_steps(slab, slabs, start_ref, perm_ref, wells_ref, near_ref, far_ref, p_ref, rim_ref):
    rows, members, cells = start_ref.shape
    even = lax.rem(slab, 2) == 0
    reach = rows + 2 * STEPS
    for k in range(STEPS):
        near = near_ref[k, 0 : 2 * members, :]
        far = far_ref[k, 0 : 2 * members, :]
        before = jnp.where(even, far, near)
        after = jnp.where(even, near, far)
        p_ref[k] = before[:members]
        rim_ref[k] = before[members:]
        p_ref[STEPS + rows + k] = after[:members]
        rim_ref[STEPS + k] = after[members:]
    last_lane = lax.broadcasted_iota(jnp.int32, (members, cells), 1) == cells - 1
    no_before = slab == 0
    no_after = slab == slabs - 1
    well_row = slice(2 * members, 2 * members + 1)

    def wells_of(i):
        if i < STEPS:
            return jnp.where(even, far_ref[i, well_row, :], near_ref[i, well_row, :])
        if i >= STEPS + rows:
            j = i - STEPS - rows
            return jnp.where(even, near_ref[j, well_row, :], far_ref[j, well_row, :])
        return wells_ref[i - STEPS : i - STEPS + 1, :]

    def head_of(step, i):
        if step == 0 and STEPS <= i < STEPS + rows:
            return start_ref[i - STEPS]
        return p_ref[i]

    def mobility_of(i, head):
        if i < STEPS:
            perm = rim_ref[i]
        elif i >= STEPS + rows:
            perm = rim_ref[i - rows]
        else:
            perm = perm_ref[i - STEPS]
        return perm * (1.0 + 0.5 * jnp.tanh(head))

    def row_flux(mobility, head, mobility_next, head_next, i):
        flux = 0.5 * (mobility_next + mobility) * (head_next - head)
        if i == STEPS - 1:
            flux = jnp.where(no_before, 0.0, flux)
        if i == STEPS + rows - 1:
            flux = jnp.where(no_after, 0.0, flux)
        return flux

    for step in range(STEPS):
        first = step + 1
        head_before = head_of(step, first - 1)
        head = head_of(step, first)
        mobility_before = mobility_of(first - 1, head_before)
        mobility = mobility_of(first, head)
        flux_before = row_flux(mobility_before, head_before, mobility, head, first - 1)
        for i in range(first, reach - first):
            head_next = head_of(step, i + 1)
            mobility_next = mobility_of(i + 1, head_next)
            flux_after = row_flux(mobility, head, mobility_next, head_next, i)
            along = 0.5 * (pltpu.roll(mobility, cells - 1, 1) + mobility) * (pltpu.roll(head, cells - 1, 1) - head)
            along = jnp.where(last_lane, 0.0, along)
            inflow = (flux_after - flux_before) + (along - pltpu.roll(along, 1, 1))
            p_ref[i] = head + time_step * (inflow + wells_of(i))
            head, mobility, flux_before = head_next, mobility_next, flux_after


def spread_product(left_ref, padded, kernel_ref, own_ref, other_ref):
    half = own_ref.shape[1]
    total = kernel_ref.shape[0]
    wide = 256 if half % 256 == 0 else 128
    deep = min(total, 512)
    for first in range(0, 2 * half, wide):
        value = None
        for cell in range(0, total, deep):
            high, low = split(kernel_ref[cell : cell + deep, first : first + wide])
            both = dot(left_ref[:, cell : cell + deep], high)
            thin = dot(left_ref[:padded, cell : cell + deep], low)
            part = both[:padded] + both[padded:] + thin
            value = part if value is None else value + part
        if first < half:
            own_ref[:, first : first + wide] = value
        else:
            other_ref[:, first - half : first - half + wide] = value


def forecast_kernel(slabs, slab_ref, start_ref, perm_ref, wells_ref, near_ref, far_ref, kernel_ref, first_ref, second_ref, own_ref, other_ref, p_ref, rim_ref, left_ref):
    rows, members, cells = start_ref.shape
    padded = first_ref.shape[0]
    forecast_steps(slab_ref[0], slabs, start_ref, perm_ref, wells_ref, near_ref, far_ref, p_ref, rim_ref)
    if padded != members:
        first_ref[...] = jnp.zeros_like(first_ref)
        second_ref[...] = jnp.zeros_like(second_ref)
        left_ref[...] = jnp.zeros_like(left_ref)
    for i in range(rows):
        value = p_ref[STEPS + i]
        high, low = split(value)
        lane = slice(i * cells, (i + 1) * cells)
        part_ref, row = (first_ref, i) if i < rows // 2 else (second_ref, i - rows // 2)
        part_ref[0:members, row * cells : (row + 1) * cells] = value
        left_ref[0:members, lane] = high
        left_ref[padded : padded + members, lane] = low
    spread_product(left_ref, padded, kernel_ref, own_ref, other_ref)


def forecast(slabs, padded, slab, start, perm, wells, near, far, kernel):
    rows, members, cells = start.shape
    total, observed = kernel.shape
    half = jax.ShapeDtypeStruct((padded, observed // 2), F32)
    return pl.pallas_call(
        functools.partial(forecast_kernel, slabs),
        out_shape=(jax.ShapeDtypeStruct((padded, total // 2), F32),) * 2 + (half, half),
        in_specs=[SMEM] + [VMEM] * 6,
        out_specs=(VMEM,) * 4,
        scratch_shapes=[
            pltpu.VMEM((rows + 2 * STEPS, members, cells), F32),
            pltpu.VMEM((2 * STEPS, members, cells), F32),
            pltpu.VMEM((2 * padded, total), BF16),
        ],
        compiler_params=params(20),
        cost_estimate=cost(6 * padded * total * observed, 4 * total * observed),
        name="forecast",
    )(slab, start, perm, wells, near, far, kernel)


def pieces_of(plan, arrays, padded):
    for offset, halves in enumerate(plan):
        for which, (index, first) in enumerate(halves):
            yield offset, which, arrays[index][first : first + padded, :]


def subsidence_kernel(plan, padded, member_ref, *refs):
    arrays = refs[:-4]
    kernel_ref, own_ref, other_ref, left_ref = refs[-4:]
    every = len(plan) * padded
    width = arrays[0].shape[1]
    for offset, which, piece in pieces_of(plan, arrays, padded):
        at = member_ref[0] ^ offset
        high, low = split(piece)
        lane = slice(which * width, (which + 1) * width)
        left_ref[pl.ds(pl.multiple_of(at * padded, padded), padded), lane] = high
        left_ref[pl.ds(pl.multiple_of(every + at * padded, padded), padded), lane] = low
    spread_product(left_ref, every, kernel_ref, own_ref, other_ref)


def subsidence_partial(plan, padded, member, arrays, kernel):
    total, pixels = kernel.shape
    every = len(plan) * padded
    out = jax.ShapeDtypeStruct((every, pixels // 2), F32)
    return pl.pallas_call(
        functools.partial(subsidence_kernel, plan, padded),
        out_shape=(out, out),
        in_specs=[SMEM] + [VMEM] * (len(arrays) + 1),
        out_specs=(VMEM,) * 2,
        scratch_shapes=[pltpu.VMEM((2 * every, total), BF16)],
        compiler_params=params(24),
        cost_estimate=cost(6 * every * total * pixels, 4 * total * pixels + 4 * every * total),
        name="subsidence",
    )(member, *arrays, kernel)


def gram_kernel(groups, members, slab_ref, member_ref, *refs):
    pieces = refs[:groups]
    value_ref, sigma_ref, out_ref, seen_ref = refs[groups:]
    padded, half = pieces[0].shape
    every = groups * padded
    for offset in range(groups):
        seen_ref[member_ref[0] ^ offset] = pieces[offset][...]
    seen = seen_ref[...].reshape(every, half)
    centre = jnp.sum(seen, 0, keepdims=True) * (1.0 / (groups * members))
    anomaly = seen - centre
    if padded != members:
        here = lax.rem(lax.broadcasted_iota(jnp.int32, (every, half), 0), padded) < members
        anomaly = jnp.where(here, anomaly, 0.0)
    blocks = half // 128
    first = lax.rem(slab_ref[0], 2) * blocks
    rows_of = lambda ref: jnp.concatenate([ref[pl.ds(first + k, 1), :] for k in range(blocks)], 1)
    sigma = rows_of(sigma_ref)
    weighted = anomaly * (1.0 / (sigma * sigma))
    innovation = jnp.broadcast_to(rows_of(value_ref) - centre, (8, half))
    extra = jnp.where(lax.broadcasted_iota(jnp.int32, (8, half), 0) == 0, innovation, 0.0)
    contract = (((1,), (1,)), ((), ()))
    out_ref[...] = jnp.zeros_like(out_ref)
    out_ref[:, 0:every] = lax.dot_general(
        weighted, anomaly, contract, precision=lax.Precision.HIGHEST, preferred_element_type=F32
    )
    out_ref[:, every : every + 8] = lax.dot_general(
        weighted, extra, contract, precision=lax.Precision.HIGHEST, preferred_element_type=F32
    )


def gram_partial(members, slab, member, pieces, value, sigma):
    groups = len(pieces)
    padded, half = pieces[0].shape
    every = groups * padded
    width = -(-(every + 8) // 128) * 128
    return pl.pallas_call(
        functools.partial(gram_kernel, groups, members),
        out_shape=jax.ShapeDtypeStruct((every, width), F32),
        in_specs=[SMEM, SMEM] + [VMEM] * (groups + 2),
        out_specs=VMEM,
        scratch_shapes=[pltpu.VMEM((groups, padded, half), F32)],
        compiler_params=params(),
        cost_estimate=cost(12 * every * every * half, 4 * every * half),
        name="gram",
    )(slab, member, *pieces, value, sigma)


COLUMNS = 8


def eliminate_panel(rows, scaled, first, count):
    groups = count // 8
    tiles = rows.shape[1] // 128
    sub_row = lax.broadcasted_iota(jnp.int32, (8, 128), 0)
    lane = lax.broadcasted_iota(jnp.int32, (8, 128), 1)
    x = [[rows[8 * g : 8 * g + 8, 128 * t : 128 * t + 128] for t in range(tiles)] for g in range(groups)]
    pick = lambda v, j: jnp.take_along_axis(v, jnp.full((8, 128), j, jnp.int32), 0, mode="promise_in_bounds")
    scale = [jnp.zeros((8, 128), F32) for _ in range(groups)]
    batch = min(COLUMNS, count)
    for start in range(0, count, batch):
        low = start // 8
        c = []
        for j in range(batch):
            tile, at = (first + start + j) // 128, (first + start + j) % 128
            c.append({g: jnp.broadcast_to(x[g][tile][:, at : at + 1], (8, 128)) for g in range(low, groups)})
        pivot = pick(c[0][low], 0)
        for j in range(batch):
            own, sub = low + j // 8, j % 8
            tile, at = (first + start + j) // 128, (first + start + j) % 128
            inverse = pltpu.reciprocal(pivot, approx=False)
            root = lax.rsqrt(pivot)
            root = root * (1.5 - 0.5 * pivot * root * root)
            scale[own] = jnp.where(sub_row == sub, root, scale[own])
            if j + 1 < batch:
                after, after_sub = low + (j + 1) // 8, (j + 1) % 8
                cross = pick(c[j][after], after_sub) * pick(c[j + 1][own], sub)
                pivot = pick(c[j + 1][after], after_sub) - cross * inverse
            for l in range(j + 1, batch):
                entry = pick(c[l][own], sub)
                for g in range(own, groups):
                    c[l][g] = c[l][g] - (c[j][g] * entry) * inverse
            below = sub_row > sub
            m = {g: c[j][g] * inverse for g in range(own, groups)}
            m[own] = jnp.where(below, m[own], 0.0)
            here = lane == at
            for t in range(tiles):
                row = pick(x[own][t], sub)
                if t == tile:
                    row = jnp.where(here, 1.0, row)
                for g in range(own, groups):
                    old = x[g][t]
                    if t == tile:
                        old = jnp.where(here & below if g == own else here, 0.0, old)
                    x[g][t] = old - m[g] * row
    for g in range(groups):
        for t in range(tiles):
            value = x[g][t]
            column = lane + 128 * t
            row = first + 8 * g + sub_row
            inside = column < first + count
            value = jnp.where(inside & (column == row), 1.0, jnp.where(inside & (column > row), 0.0, value))
            scaled[first + 8 * g : first + 8 * g + 8, 128 * t : 128 * t + 128] = value * scale[g]


def invert(work_ref):
    every, width = work_ref.shape
    panel = math.gcd(every, 64)
    for first in range(0, every, panel):
        eliminate_panel(work_ref[first : first + panel, :], work_ref, first, panel)
        below = first + panel
        if below < every:
            done = work_ref[first:below, :]
            base = below // 128 * 128
            one = done.astype(BF16)
            rest = done - one.astype(F32)
            two = rest.astype(BF16)
            three = (rest - two.astype(F32)).astype(BF16)
            left = jnp.concatenate([one, one, two, two, one, three], 0)[:, base:every]
            right = jnp.concatenate([one, two, one, two, three, one], 0)
            product = lax.dot_general(
                left, right, (((0,), (0,)), ((), ())), preferred_element_type=F32
            )
            column = lax.broadcasted_iota(jnp.int32, (every - below, width), 1)
            own = (column >= first) & (column < below)
            old = jnp.where(own, 0.0, work_ref[below:every, :])
            work_ref[below:every, :] = old - product[below - base :]


def finish_kernel(plan, padded, members, member_ref, gram_ref, more_ref, *refs):
    groups = len(plan)
    arrays = refs[:-3]
    out_ref, cast_ref, work_ref = refs[-3:]
    total = cast_ref.shape[2]
    rows, cells = out_ref.shape[1:]
    every, width = work_ref.shape
    count = groups * members
    member = member_ref[0]
    for offset, which, piece in pieces_of(plan, arrays, padded):
        at = member ^ offset
        high, low = split(piece)
        lane = slice(which * (total // 2), (which + 1) * (total // 2))
        cast_ref[at, :, lane] = high
        cast_ref[groups + at, :, lane] = low
    row = lax.broadcasted_iota(jnp.int32, (every, width), 0)
    column = lax.broadcasted_iota(jnp.int32, (every, width), 1)
    work_ref[...] = gram_ref[...] + more_ref[...] + jnp.where(row == column, count - 1.0, 0.0)
    invert(work_ref)

    solved = jnp.broadcast_to(work_ref[:, every : every + 1], (every, width))
    inverse = jnp.where(column <= row, work_ref[...], 0.0)
    weights = jnp.sum(inverse * solved, 0, keepdims=True)
    first = pl.multiple_of(member * padded, padded)
    column = lax.broadcasted_iota(jnp.int32, (padded, width), 1)
    row = lax.broadcasted_iota(jnp.int32, (padded, width), 0) + first
    own = jnp.where(column <= row, work_ref[pl.ds(first, padded), :], 0.0)
    here = column < every
    if padded != members:
        here = here & (lax.rem(column, padded) < members)
    mix = jnp.where(here, weights + math.sqrt(count - 1.0) * own, 0.0)
    mix = mix + (1.0 - jnp.sum(mix, 1, keepdims=True)) * (1.0 / count)
    mix = jnp.where(here, mix, 0.0)[:, :every]

    mix_high, mix_low = split(mix)
    mix_both = jnp.concatenate([mix_high, mix_low], 0)
    depth = 4 * cells if rows % 4 == 0 else cells
    for lane in range(0, total, depth):
        high = cast_ref[0:groups, :, lane : lane + depth].reshape(every, depth)
        low = cast_ref[groups:, :, lane : lane + depth].reshape(every, depth)
        both = dot(mix_both, high)
        value = both[:padded] + both[padded:] + dot(mix_high, low)
        for part in range(depth // cells):
            out_ref[:, lane // cells + part, :] = value[:members, part * cells : (part + 1) * cells]


def finish(plan, padded, members, rows, cells, member, gram, more, arrays):
    groups = len(plan)
    total = rows * cells
    return pl.pallas_call(
        functools.partial(finish_kernel, plan, padded, members),
        out_shape=jax.ShapeDtypeStruct((members, rows, cells), F32),
        in_specs=[SMEM] + [VMEM] * (len(arrays) + 2),
        out_specs=VMEM,
        scratch_shapes=[pltpu.VMEM((2 * groups, padded, total), BF16), pltpu.VMEM(gram.shape, F32)],
        compiler_params=params(),
        cost_estimate=cost(6 * padded * groups * padded * total, 4 * groups * padded * total),
        name="finish",
    )(member, gram, more, *arrays)


def cycle(head, perm, wells, layer, coords, obs_index, obs_value, obs_sigma):
    members, rows, cells = head.shape
    groups = lax.axis_size("member")
    slabs = lax.axis_size("slab")
    slab = lax.axis_index("slab")
    member = lax.axis_index("member")
    total_rows = rows * slabs
    padded = -(-members // 16) * 16
    slab_s = slab.astype(jnp.int32).reshape(1)
    member_s = member.astype(jnp.int32).reshape(1)
    pair = [(i, i ^ 1) for i in range(slabs)]
    across = [(i, i + 1) for i in range(1, slabs - 1, 2)] + [(i + 1, i) for i in range(1, slabs - 1, 2)]

    def swap(value, axis, offset):
        size = lax.axis_size(axis)
        return lax.ppermute(value, axis, [(i, i ^ offset) for i in range(size)])

    smalls = (wells, layer, coords, *(a.reshape(-1, 128) for a in (obs_index, obs_value, obs_sigma)))
    head, perm, wells, *smalls = (
        pltpu.with_memory_space_constraint(a, pltpu.HBM) for a in (head, perm, wells, *smalls)
    )
    near, far, wells, layer, coords, index, value, sigma = pack(slab_s, head, perm, wells, smalls)
    far = lax.ppermute(far, "slab", across)
    near = lax.ppermute(near, "slab", pair)

    kernel, start, perm_rows = kernel_of_observed(total_rows, slab_s, coords, index, layer, head, perm)
    first, second, own, other = forecast(slabs, padded, slab_s, start, perm_rows, wells, near, far, kernel)
    seen = own + swap(other, "slab", 1)
    if groups == 4:
        across_first = swap(first, "member", 1)
        along_second = swap(second, "member", 2)
        far_first = swap(jnp.concatenate([first, across_first], 0), "member", 2)
        far_second = swap(jnp.concatenate([second, along_second], 0), "member", 1)
        arrays = (first, second, across_first, along_second, far_first, far_second)
        plan = (((0, 0), (1, 0)), ((2, 0), (5, 0)), ((4, 0), (3, 0)), ((4, padded), (5, padded)))
    else:
        both = jnp.concatenate([first, second], 0)
        arrays = (both,) + tuple(swap(both, "member", k) for k in range(1, groups))
        plan = tuple(((k, 0), (k, padded)) for k in range(groups))
    offset = 2
    while offset < slabs:
        seen = seen + swap(seen, "slab", offset)
        offset *= 2
    views = [seen] + [swap(seen, "member", offset) for offset in range(1, groups)]
    gram = gram_partial(members, slab_s, member_s, views, value, sigma)
    gram_more = swap(gram, "slab", 1)

    chips = slabs // 2
    own_rows = coords.shape[1] // (groups * slabs)
    kernel_all = kernel_of_pixels(total_rows, groups, slab_s, member_s, coords, layer)
    sunk, sunk_other = subsidence_partial(plan, padded, member_s, arrays, kernel_all)
    sunk_recv = swap(sunk_other, "slab", 1)
    chip = slab // 2

    def block(which):
        first = which * own_rows
        return lax.dynamic_slice_in_dim(sunk, first, own_rows, 1) + lax.dynamic_slice_in_dim(
            sunk_recv, first, own_rows, 1
        )

    sunk_own = block(chip)
    for offset in range(1, chips):
        sunk_own = sunk_own + swap(block(chip ^ offset), "slab", 2 * offset)
    if padded != members:
        sunk_own = sunk_own.reshape(groups, padded, own_rows)[:, :members].reshape(groups * members, own_rows)
    subsidence = sunk_own.T

    analysed = finish(plan, padded, members, rows, cells, member_s, gram, gram_more, arrays)
    return (analysed, subsidence)


def solution(mesh):
    return jax.shard_map(
        cycle,
        mesh=mesh,
        in_specs=(
            P("member", "slab", None),
            P("member", "slab", None),
            P("slab", None),
            P("slab", None),
            P(),
            P(),
            P(),
            P(),
        ),
        out_specs=(P("member", "slab", None), P(("member", "slab"), None)),
        check_vma=False,
    )
```

```python
import functools
import math

import jax
import jax.numpy as jnp
from jax import lax
from jax.experimental import pallas as pl
from jax.experimental.pallas import tpu as pltpu
from jax.sharding import PartitionSpec as P


STEPS = 4

time_step = 0.15
pixel_span = 64.0
top_depth = 2.0

F32 = jnp.float32
BF16 = jnp.bfloat16

MIB = 1024 * 1024


def params(mib=16, **more):
    return pltpu.CompilerParams(vmem_limit_bytes=mib * MIB, **more)


def cost(flops, bytes_accessed):
    return pl.CostEstimate(flops=int(flops), bytes_accessed=int(bytes_accessed), transcendentals=0)


def split(value):
    high = value.astype(BF16)
    return high, (value - high.astype(F32)).astype(BF16)


def dot(a, b):
    return lax.dot_general(a, b, (((1,), (0,)), ((), ())), preferred_element_type=F32)


VMEM = pl.BlockSpec(memory_space=pltpu.VMEM)
SMEM = pl.BlockSpec(memory_space=pltpu.SMEM)
HBM = pl.BlockSpec(memory_space=pltpu.HBM)


def pack_kernel(slab_ref, head_ref, perm_ref, wells_ref, *refs):
    small = (len(refs) - 3) // 2
    smalls = refs[:small]
    near_ref, far_ref = refs[small : small + 2]
    copies = refs[small + 2 : -1]
    sems = refs[-1]
    members, rows, _ = head_ref.shape
    even = lax.rem(slab_ref[0], 2) == 0
    moves = []

    def move(source, target):
        moves.append(pltpu.make_async_copy(source, target, sems.at[len(moves)]))
        moves[-1].start()

    for k in range(STEPS):
        near = jnp.where(even, rows - STEPS + k, k)
        far = jnp.where(even, k, rows - STEPS + k)
        for target, at in ((near_ref, near), (far_ref, far)):
            move(head_ref.at[:, at, :], target.at[k, 0:members, :])
            move(perm_ref.at[:, at, :], target.at[k, members : 2 * members, :])
            move(wells_ref.at[pl.ds(at, 1), :], target.at[k, 2 * members : 2 * members + 1, :])
    for source, target in zip(smalls, copies):
        move(source, target)
    for one in moves:
        one.wait()


def pack(slab, head, perm, wells, smalls):
    members, _, cells = head.shape
    out = jax.ShapeDtypeStruct((STEPS, 2 * members + 8, cells), F32)
    return pl.pallas_call(
        pack_kernel,
        out_shape=(out, out) + tuple(jax.ShapeDtypeStruct(a.shape, a.dtype) for a in smalls),
        in_specs=[SMEM] + [HBM] * (3 + len(smalls)),
        out_specs=(VMEM,) * (2 + len(smalls)),
        scratch_shapes=[pltpu.SemaphoreType.DMA((6 * STEPS + len(smalls),))],
        compiler_params=params(4),
        name="pack_rims",
    )(slab, head, perm, wells, *smalls)


def kernel_rows(total_rows, slab, at_ref, layer_ref, out_ref, dy2_ref):
    cells, pixels = dy2_ref.shape
    rows = layer_ref.shape[0]
    position = lax.broadcasted_iota(jnp.int32, (cells, 128), 0).astype(F32)
    cell_y = (position + 0.5) * (pixel_span / cells)
    for lane in range(0, pixels, 128):
        delta = cell_y - at_ref[1:2, lane : lane + 128]
        dy2_ref[:, lane : lane + 128] = delta * delta

    def one_row(row, carry):
        cell_x = ((slab * rows + row).astype(F32) + 0.5) * (pixel_span / total_rows)
        layer = layer_ref[pl.ds(row, 1), :].astype(F32) + top_depth
        depth = jnp.swapaxes(jnp.broadcast_to(layer, (cells, cells)), 0, 1)
        depth2 = depth * depth
        scaled = depth * (pixel_span * pixel_span / (total_rows * cells))
        for lane in range(0, pixels, 128):
            delta = cell_x - at_ref[0:1, lane : lane + 128]
            dx2 = jnp.broadcast_to(delta * delta, (32, 128))
            for sub in range(0, cells, 32):
                r2 = dy2_ref[sub : sub + 32, lane : lane + 128] + dx2 + depth2[sub : sub + 32, :128]
                inverse = lax.rsqrt(r2)
                at = pl.ds(pl.multiple_of(row * cells + sub, 32), 32)
                out_ref[at, lane : lane + 128] = scaled[sub : sub + 32, :128] * inverse * (inverse * inverse)
        return carry

    lax.fori_loop(0, rows, one_row, 0, unroll=4)


def observed_kernel(total_rows, slab_ref, coords_ref, index_ref, layer_ref, head_ref, perm_ref, out_ref, p_ref, k_ref, dy2_ref, at_ref, table_ref, sems):
    rows = layer_ref.shape[0]
    pixels = dy2_ref.shape[1]
    tall = table_ref.shape[0] // 2
    moves = []
    for row in range(rows):
        for source, target in ((head_ref, p_ref), (perm_ref, k_ref)):
            moves.append(pltpu.make_async_copy(source.at[:, row, :], target.at[row], sems.at[len(moves)]))
            moves[-1].start()
    for row in range(tall):
        for which in range(2):
            table_ref[which * tall + row : which * tall + row + 1, :] = coords_ref[
                which : which + 1, row * 128 : row * 128 + 128
            ].astype(F32)
    table = table_ref[...].astype(BF16)
    blocks = pixels // 128
    core = lax.rem(slab_ref[0], 2)
    for block in range(blocks):
        lane = block * 128
        index = index_ref[pl.ds(lax.rem(core * (blocks // 2) + block, blocks), 1), :]
        pick = (lax.broadcasted_iota(jnp.int32, (128, 128), 0) == (index & 127)).astype(BF16)
        found = dot(table, pick)
        own = lax.broadcasted_iota(jnp.int32, (tall, 128), 0) == (index >> 7)
        at_ref[0:1, lane : lane + 128] = jnp.sum(jnp.where(own, found[:tall], 0.0), 0, keepdims=True)
        at_ref[1:2, lane : lane + 128] = jnp.sum(jnp.where(own, found[tall:], 0.0), 0, keepdims=True)
    kernel_rows(total_rows, slab_ref[0], at_ref, layer_ref, out_ref, dy2_ref)
    for one in moves:
        one.wait()


def kernel_of_observed(total_rows, slab, coords, index, layer, head, perm):
    members = head.shape[0]
    rows, cells = layer.shape
    pixels = index.size
    out = jax.ShapeDtypeStruct((rows * cells, pixels), F32)
    state = jax.ShapeDtypeStruct((rows, members, cells), F32)
    return pl.pallas_call(
        functools.partial(observed_kernel, total_rows),
        out_shape=(out, state, state),
        in_specs=[SMEM, VMEM, VMEM, VMEM, HBM, HBM],
        out_specs=(VMEM,) * 3,
        scratch_shapes=[
            pltpu.VMEM((cells, pixels), F32),
            pltpu.VMEM((8, pixels), F32),
            pltpu.VMEM((coords.size // 128, 128), F32),
            pltpu.SemaphoreType.DMA((2 * rows,)),
        ],
        compiler_params=params(20),
        cost_estimate=cost(rows * cells * pixels * 16, rows * cells * pixels * 4),
        name="kernel_of_observed",
    )(slab, coords, index, layer, head, perm)


def pixel_kernel(total_rows, chips, own_rows, slab_ref, member_ref, coords_ref, layer_ref, out_ref, dy2_ref, at_ref):
    if own_rows % 128:
        at_ref[0:2, :] = coords_ref[...]
    else:
        core = lax.rem(slab_ref[0], 2)
        lane = 0
        for own in (core, 1 - core):
            for chip in range(chips):
                first = ((member_ref[0] * chips + chip) * 2 + own) * own_rows
                for part in range(0, own_rows, 128):
                    at = pl.ds(pl.multiple_of(first + part, 128), 128)
                    at_ref[0:2, lane : lane + 128] = coords_ref[:, at].astype(F32)
                    lane += 128
    kernel_rows(total_rows, slab_ref[0], at_ref, layer_ref, out_ref, dy2_ref)


def kernel_of_pixels(total_rows, groups, slab, member, coords, layer):
    rows, cells = layer.shape
    slabs = total_rows // rows
    chips = slabs // 2
    own_rows = coords.shape[1] // (groups * slabs)
    pixels = slabs * own_rows
    if own_rows % 128:
        coords = coords.astype(F32).reshape(2, groups, chips, 2, own_rows)
        coords = lax.dynamic_index_in_dim(coords, member[0], 1, keepdims=False)
        coords = jnp.swapaxes(coords, 1, 2)
        coords = jnp.where(slab[0] % 2 == 0, coords, coords[:, ::-1]).reshape(2, pixels)
    out = jax.ShapeDtypeStruct((rows * cells, pixels), F32)
    return pl.pallas_call(
        functools.partial(pixel_kernel, total_rows, chips, own_rows),
        out_shape=out,
        in_specs=[SMEM, SMEM, VMEM, VMEM],
        out_specs=VMEM,
        scratch_shapes=[pltpu.VMEM((cells, pixels), F32), pltpu.VMEM((8, pixels), F32)],
        compiler_params=params(20),
        cost_estimate=cost(rows * cells * pixels * 16, rows * cells * pixels * 4),
        name="kernel_of_pixels",
    )(slab, member, coords, layer)


def forecast_steps(slab, slabs, start_ref, perm_ref, wells_ref, near_ref, far_ref, p_ref, rim_ref):
    rows, members, cells = start_ref.shape
    even = lax.rem(slab, 2) == 0
    reach = rows + 2 * STEPS
    for k in range(STEPS):
        near = near_ref[k, 0 : 2 * members, :]
        far = far_ref[k, 0 : 2 * members, :]
        before = jnp.where(even, far, near)
        after = jnp.where(even, near, far)
        p_ref[k] = before[:members]
        rim_ref[k] = before[members:]
        p_ref[STEPS + rows + k] = after[:members]
        rim_ref[STEPS + k] = after[members:]
    last_lane = lax.broadcasted_iota(jnp.int32, (members, cells), 1) == cells - 1
    no_before = slab == 0
    no_after = slab == slabs - 1
    well_row = slice(2 * members, 2 * members + 1)

    def wells_of(i):
        if i < STEPS:
            return jnp.where(even, far_ref[i, well_row, :], near_ref[i, well_row, :])
        if i >= STEPS + rows:
            j = i - STEPS - rows
            return jnp.where(even, near_ref[j, well_row, :], far_ref[j, well_row, :])
        return wells_ref[i - STEPS : i - STEPS + 1, :]

    def head_of(step, i):
        if step == 0 and STEPS <= i < STEPS + rows:
            return start_ref[i - STEPS]
        return p_ref[i]

    def mobility_of(i, head):
        if i < STEPS:
            perm = rim_ref[i]
        elif i >= STEPS + rows:
            perm = rim_ref[i - rows]
        else:
            perm = perm_ref[i - STEPS]
        return perm * (0.5 + 0.25 * jnp.tanh(head))

    def row_flux(mobility, head, mobility_next, head_next, i):
        flux = (mobility_next + mobility) * (head_next - head)
        if i == STEPS - 1:
            flux = jnp.where(no_before, 0.0, flux)
        if i == STEPS + rows - 1:
            flux = jnp.where(no_after, 0.0, flux)
        return flux

    for step in range(STEPS):
        first = step + 1
        head_before = head_of(step, first - 1)
        head = head_of(step, first)
        mobility_before = mobility_of(first - 1, head_before)
        mobility = mobility_of(first, head)
        flux_before = row_flux(mobility_before, head_before, mobility, head, first - 1)
        for i in range(first, reach - first):
            head_next = head_of(step, i + 1)
            mobility_next = mobility_of(i + 1, head_next)
            flux_after = row_flux(mobility, head, mobility_next, head_next, i)
            along = (pltpu.roll(mobility, cells - 1, 1) + mobility) * (pltpu.roll(head, cells - 1, 1) - head)
            along = jnp.where(last_lane, 0.0, along)
            inflow = (flux_after - flux_before) + (along - pltpu.roll(along, 1, 1))
            p_ref[i] = head + time_step * (inflow + wells_of(i))
            head, mobility, flux_before = head_next, mobility_next, flux_after


def spread_product(left_ref, padded, kernel_ref, own_ref, other_ref):
    half = own_ref.shape[1]
    total = kernel_ref.shape[0]
    wide = 256 if half % 256 == 0 else 128
    deep = min(total, 512)
    for first in range(0, 2 * half, wide):
        value = None
        for cell in range(0, total, deep):
            high, low = split(kernel_ref[cell : cell + deep, first : first + wide])
            both = dot(left_ref[:, cell : cell + deep], high)
            thin = dot(left_ref[:padded, cell : cell + deep], low)
            part = both[:padded] + both[padded:] + thin
            value = part if value is None else value + part
        if first < half:
            own_ref[:, first : first + wide] = value
        else:
            other_ref[:, first - half : first - half + wide] = value


def forecast_kernel(slabs, slab_ref, start_ref, perm_ref, wells_ref, near_ref, far_ref, kernel_ref, first_ref, second_ref, own_ref, other_ref, p_ref, rim_ref, left_ref):
    rows, members, cells = start_ref.shape
    padded = first_ref.shape[0]
    forecast_steps(slab_ref[0], slabs, start_ref, perm_ref, wells_ref, near_ref, far_ref, p_ref, rim_ref)
    if padded != members:
        first_ref[...] = jnp.zeros_like(first_ref)
        second_ref[...] = jnp.zeros_like(second_ref)
        left_ref[...] = jnp.zeros_like(left_ref)
    for i in range(rows):
        value = p_ref[STEPS + i]
        high, low = split(value)
        lane = slice(i * cells, (i + 1) * cells)
        part_ref, row = (first_ref, i) if i < rows // 2 else (second_ref, i - rows // 2)
        part_ref[0:members, row * cells : (row + 1) * cells] = value
        left_ref[0:members, lane] = high
        left_ref[padded : padded + members, lane] = low
    spread_product(left_ref, padded, kernel_ref, own_ref, other_ref)


def forecast(slabs, padded, slab, start, perm, wells, near, far, kernel):
    rows, members, cells = start.shape
    total, observed = kernel.shape
    half = jax.ShapeDtypeStruct((padded, observed // 2), F32)
    return pl.pallas_call(
        functools.partial(forecast_kernel, slabs),
        out_shape=(jax.ShapeDtypeStruct((padded, total // 2), F32),) * 2 + (half, half),
        in_specs=[SMEM] + [VMEM] * 6,
        out_specs=(VMEM,) * 4,
        scratch_shapes=[
            pltpu.VMEM((rows + 2 * STEPS, members, cells), F32),
            pltpu.VMEM((2 * STEPS, members, cells), F32),
            pltpu.VMEM((2 * padded, total), BF16),
        ],
        compiler_params=params(20),
        cost_estimate=cost(6 * padded * total * observed, 4 * total * observed),
        name="forecast",
    )(slab, start, perm, wells, near, far, kernel)


def pieces_of(plan, arrays, padded):
    for offset, halves in enumerate(plan):
        for which, (index, first) in enumerate(halves):
            yield offset, which, arrays[index][first : first + padded, :]


def subsidence_kernel(plan, padded, member_ref, *refs):
    arrays = refs[:-4]
    kernel_ref, own_ref, other_ref, left_ref = refs[-4:]
    every = len(plan) * padded
    width = arrays[0].shape[1]
    for offset, which, piece in pieces_of(plan, arrays, padded):
        at = member_ref[0] ^ offset
        high, low = split(piece)
        lane = slice(which * width, (which + 1) * width)
        left_ref[pl.ds(pl.multiple_of(at * padded, padded), padded), lane] = high
        left_ref[pl.ds(pl.multiple_of(every + at * padded, padded), padded), lane] = low
    spread_product(left_ref, every, kernel_ref, own_ref, other_ref)


def subsidence_partial(plan, padded, member, arrays, kernel):
    total, pixels = kernel.shape
    every = len(plan) * padded
    out = jax.ShapeDtypeStruct((every, pixels // 2), F32)
    return pl.pallas_call(
        functools.partial(subsidence_kernel, plan, padded),
        out_shape=(out, out),
        in_specs=[SMEM] + [VMEM] * (len(arrays) + 1),
        out_specs=(VMEM,) * 2,
        scratch_shapes=[pltpu.VMEM((2 * every, total), BF16)],
        compiler_params=params(24),
        cost_estimate=cost(6 * every * total * pixels, 4 * total * pixels + 4 * every * total),
        name="subsidence",
    )(member, *arrays, kernel)


def gram_kernel(groups, members, slab_ref, member_ref, *refs):
    pieces = refs[:groups]
    value_ref, sigma_ref, out_ref, seen_ref = refs[groups:]
    padded, half = pieces[0].shape
    every = groups * padded
    for offset in range(groups):
        seen_ref[member_ref[0] ^ offset] = pieces[offset][...]
    seen = seen_ref[...].reshape(every, half)
    centre = jnp.sum(seen, 0, keepdims=True) * (1.0 / (groups * members))
    anomaly = seen - centre
    if padded != members:
        here = lax.rem(lax.broadcasted_iota(jnp.int32, (every, half), 0), padded) < members
        anomaly = jnp.where(here, anomaly, 0.0)
    blocks = half // 128
    first = lax.rem(slab_ref[0], 2) * blocks
    rows_of = lambda ref: jnp.concatenate([ref[pl.ds(first + k, 1), :] for k in range(blocks)], 1)
    sigma = rows_of(sigma_ref)
    weighted = anomaly * (1.0 / (sigma * sigma))
    innovation = jnp.broadcast_to(rows_of(value_ref) - centre, (8, half))
    extra = jnp.where(lax.broadcasted_iota(jnp.int32, (8, half), 0) == 0, innovation, 0.0)
    contract = (((1,), (1,)), ((), ()))
    out_ref[...] = jnp.zeros_like(out_ref)
    out_ref[:, 0:every] = lax.dot_general(
        weighted, anomaly, contract, precision=lax.Precision.HIGHEST, preferred_element_type=F32
    )
    out_ref[:, every : every + 8] = lax.dot_general(
        weighted, extra, contract, precision=lax.Precision.HIGHEST, preferred_element_type=F32
    )


def gram_partial(members, slab, member, pieces, value, sigma):
    groups = len(pieces)
    padded, half = pieces[0].shape
    every = groups * padded
    width = -(-(every + 8) // 128) * 128
    return pl.pallas_call(
        functools.partial(gram_kernel, groups, members),
        out_shape=jax.ShapeDtypeStruct((every, width), F32),
        in_specs=[SMEM, SMEM] + [VMEM] * (groups + 2),
        out_specs=VMEM,
        scratch_shapes=[pltpu.VMEM((groups, padded, half), F32)],
        compiler_params=params(),
        cost_estimate=cost(12 * every * every * half, 4 * every * half),
        name="gram",
    )(slab, member, *pieces, value, sigma)


COLUMNS = 8


def eliminate_panel(rows, scaled, first, count):
    groups = count // 8
    tiles = rows.shape[1] // 128
    sub_row = lax.broadcasted_iota(jnp.int32, (8, 128), 0)
    lane = lax.broadcasted_iota(jnp.int32, (8, 128), 1)
    x = [[rows[8 * g : 8 * g + 8, 128 * t : 128 * t + 128] for t in range(tiles)] for g in range(groups)]
    pick = lambda v, j: jnp.take_along_axis(v, jnp.full((8, 128), j, jnp.int32), 0, mode="promise_in_bounds")
    scale = [jnp.zeros((8, 128), F32) for _ in range(groups)]
    batch = min(COLUMNS, count)
    for start in range(0, count, batch):
        low = start // 8
        c = []
        for j in range(batch):
            tile, at = (first + start + j) // 128, (first + start + j) % 128
            c.append({g: jnp.broadcast_to(x[g][tile][:, at : at + 1], (8, 128)) for g in range(low, groups)})
        pivot = pick(c[0][low], 0)
        for j in range(batch):
            own, sub = low + j // 8, j % 8
            tile, at = (first + start + j) // 128, (first + start + j) % 128
            inverse = pltpu.reciprocal(pivot, approx=False)
            root = lax.rsqrt(pivot)
            root = root * (1.5 - 0.5 * pivot * root * root)
            scale[own] = jnp.where(sub_row == sub, root, scale[own])
            if j + 1 < batch:
                after, after_sub = low + (j + 1) // 8, (j + 1) % 8
                cross = pick(c[j][after], after_sub) * pick(c[j + 1][own], sub)
                pivot = pick(c[j + 1][after], after_sub) - cross * inverse
            for l in range(j + 1, batch):
                entry = pick(c[l][own], sub)
                for g in range(own, groups):
                    c[l][g] = c[l][g] - (c[j][g] * entry) * inverse
            below = sub_row > sub
            m = {g: c[j][g] * inverse for g in range(own, groups)}
            m[own] = jnp.where(below, m[own], 0.0)
            here = lane == at
            for t in range(tiles):
                row = pick(x[own][t], sub)
                if t == tile:
                    row = jnp.where(here, 1.0, row)
                for g in range(own, groups):
                    old = x[g][t]
                    if t == tile:
                        old = jnp.where(here & below if g == own else here, 0.0, old)
                    x[g][t] = old - m[g] * row
    for g in range(groups):
        for t in range(tiles):
            value = x[g][t]
            column = lane + 128 * t
            row = first + 8 * g + sub_row
            inside = column < first + count
            value = jnp.where(inside & (column == row), 1.0, jnp.where(inside & (column > row), 0.0, value))
            scaled[first + 8 * g : first + 8 * g + 8, 128 * t : 128 * t + 128] = value * scale[g]


def invert(work_ref):
    every, width = work_ref.shape
    panel = math.gcd(every, 64)
    for first in range(0, every, panel):
        eliminate_panel(work_ref[first : first + panel, :], work_ref, first, panel)
        below = first + panel
        if below < every:
            done = work_ref[first:below, :]
            base = below // 128 * 128
            one = done.astype(BF16)
            rest = done - one.astype(F32)
            two = rest.astype(BF16)
            three = (rest - two.astype(F32)).astype(BF16)
            left = jnp.concatenate([one, one, two, two, one, three], 0)[:, base:every]
            right = jnp.concatenate([one, two, one, two, three, one], 0)
            product = lax.dot_general(
                left, right, (((0,), (0,)), ((), ())), preferred_element_type=F32
            )
            column = lax.broadcasted_iota(jnp.int32, (every - below, width), 1)
            own = (column >= first) & (column < below)
            old = jnp.where(own, 0.0, work_ref[below:every, :])
            work_ref[below:every, :] = old - product[below - base :]


def finish_kernel(plan, padded, members, member_ref, gram_ref, more_ref, *refs):
    groups = len(plan)
    arrays = refs[:-3]
    out_ref, cast_ref, work_ref = refs[-3:]
    total = cast_ref.shape[2]
    rows, cells = out_ref.shape[1:]
    every, width = work_ref.shape
    count = groups * members
    member = member_ref[0]
    for offset, which, piece in pieces_of(plan, arrays, padded):
        at = member ^ offset
        high, low = split(piece)
        lane = slice(which * (total // 2), (which + 1) * (total // 2))
        cast_ref[at, :, lane] = high
        cast_ref[groups + at, :, lane] = low
    row = lax.broadcasted_iota(jnp.int32, (every, width), 0)
    column = lax.broadcasted_iota(jnp.int32, (every, width), 1)
    work_ref[...] = gram_ref[...] + more_ref[...] + jnp.where(row == column, count - 1.0, 0.0)
    invert(work_ref)

    solved = jnp.broadcast_to(work_ref[:, every : every + 1], (every, width))
    inverse = jnp.where(column <= row, work_ref[...], 0.0)
    weights = jnp.sum(inverse * solved, 0, keepdims=True)
    first = pl.multiple_of(member * padded, padded)
    column = lax.broadcasted_iota(jnp.int32, (padded, width), 1)
    row = lax.broadcasted_iota(jnp.int32, (padded, width), 0) + first
    own = jnp.where(column <= row, work_ref[pl.ds(first, padded), :], 0.0)
    here = column < every
    if padded != members:
        here = here & (lax.rem(column, padded) < members)
    mix = jnp.where(here, weights + math.sqrt(count - 1.0) * own, 0.0)
    mix = mix + (1.0 - jnp.sum(mix, 1, keepdims=True)) * (1.0 / count)
    mix = jnp.where(here, mix, 0.0)[:, :every]

    mix_high, mix_low = split(mix)
    mix_both = jnp.concatenate([mix_high, mix_low], 0)
    depth = 4 * cells if rows % 4 == 0 else cells
    for lane in range(0, total, depth):
        high = cast_ref[0:groups, :, lane : lane + depth].reshape(every, depth)
        low = cast_ref[groups:, :, lane : lane + depth].reshape(every, depth)
        both = dot(mix_both, high)
        value = both[:padded] + both[padded:] + dot(mix_high, low)
        for part in range(depth // cells):
            out_ref[:, lane // cells + part, :] = value[:members, part * cells : (part + 1) * cells]


def finish(plan, padded, members, rows, cells, member, gram, more, arrays):
    groups = len(plan)
    total = rows * cells
    return pl.pallas_call(
        functools.partial(finish_kernel, plan, padded, members),
        out_shape=jax.ShapeDtypeStruct((members, rows, cells), F32),
        in_specs=[SMEM] + [VMEM] * (len(arrays) + 2),
        out_specs=VMEM,
        scratch_shapes=[pltpu.VMEM((2 * groups, padded, total), BF16), pltpu.VMEM(gram.shape, F32)],
        compiler_params=params(),
        cost_estimate=cost(6 * padded * groups * padded * total, 4 * groups * padded * total),
        name="finish",
    )(member, gram, more, *arrays)


def cycle(head, perm, wells, layer, coords, obs_index, obs_value, obs_sigma):
    members, rows, cells = head.shape
    groups = lax.axis_size("member")
    slabs = lax.axis_size("slab")
    slab = lax.axis_index("slab")
    member = lax.axis_index("member")
    total_rows = rows * slabs
    padded = -(-members // 16) * 16
    slab_s = slab.astype(jnp.int32).reshape(1)
    member_s = member.astype(jnp.int32).reshape(1)
    pair = [(i, i ^ 1) for i in range(slabs)]
    across = [(i, i + 1) for i in range(1, slabs - 1, 2)] + [(i + 1, i) for i in range(1, slabs - 1, 2)]

    def swap(value, axis, offset):
        size = lax.axis_size(axis)
        return lax.ppermute(value, axis, [(i, i ^ offset) for i in range(size)])

    smalls = (wells, layer, coords, *(a.reshape(-1, 128) for a in (obs_index, obs_value, obs_sigma)))
    head, perm, wells, *smalls = (
        pltpu.with_memory_space_constraint(a, pltpu.HBM) for a in (head, perm, wells, *smalls)
    )
    near, far, wells, layer, coords, index, value, sigma = pack(slab_s, head, perm, wells, smalls)
    far = lax.ppermute(far, "slab", across)
    near = lax.ppermute(near, "slab", pair)

    kernel, start, perm_rows = kernel_of_observed(total_rows, slab_s, coords, index, layer, head, perm)
    first, second, own, other = forecast(slabs, padded, slab_s, start, perm_rows, wells, near, far, kernel)
    seen = own + swap(other, "slab", 1)
    if groups == 4:
        across_first = swap(first, "member", 1)
        along_second = swap(second, "member", 2)
        far_first = swap(jnp.concatenate([first, across_first], 0), "member", 2)
        far_second = swap(jnp.concatenate([second, along_second], 0), "member", 1)
        arrays = (first, second, across_first, along_second, far_first, far_second)
        plan = (((0, 0), (1, 0)), ((2, 0), (5, 0)), ((4, 0), (3, 0)), ((4, padded), (5, padded)))
    else:
        both = jnp.concatenate([first, second], 0)
        arrays = (both,) + tuple(swap(both, "member", k) for k in range(1, groups))
        plan = tuple(((k, 0), (k, padded)) for k in range(groups))
    offset = 2
    while offset < slabs:
        seen = seen + swap(seen, "slab", offset)
        offset *= 2
    views = [seen] + [swap(seen, "member", offset) for offset in range(1, groups)]
    gram = gram_partial(members, slab_s, member_s, views, value, sigma)
    gram_more = swap(gram, "slab", 1)

    chips = slabs // 2
    own_rows = coords.shape[1] // (groups * slabs)
    kernel_all = kernel_of_pixels(total_rows, groups, slab_s, member_s, coords, layer)
    sunk, sunk_other = subsidence_partial(plan, padded, member_s, arrays, kernel_all)
    sunk_recv = swap(sunk_other, "slab", 1)
    chip = slab // 2

    def block(which):
        first = which * own_rows
        return lax.dynamic_slice_in_dim(sunk, first, own_rows, 1) + lax.dynamic_slice_in_dim(
            sunk_recv, first, own_rows, 1
        )

    sunk_own = block(chip)
    for offset in range(1, chips):
        sunk_own = sunk_own + swap(block(chip ^ offset), "slab", 2 * offset)
    if padded != members:
        sunk_own = sunk_own.reshape(groups, padded, own_rows)[:, :members].reshape(groups * members, own_rows)
    subsidence = sunk_own.T

    analysed = finish(plan, padded, members, rows, cells, member_s, gram, gram_more, arrays)
    return (analysed, subsidence)


def solution(mesh):
    return jax.shard_map(
        cycle,
        mesh=mesh,
        in_specs=(
            P("member", "slab", None),
            P("member", "slab", None),
            P("slab", None),
            P("slab", None),
            P(),
            P(),
            P(),
            P(),
        ),
        out_specs=(P("member", "slab", None), P(("member", "slab"), None)),
        check_vma=False,
    )
```
